32 devices in a mesh: ctx: 16 (over z, x, core), fsdp: 2 (over y).
Axes of the slice: x: 2, y: 2, z: 4, core: 2. Of those that a mesh axis runs over, the one named last changes fastest.
Arguments:
- tokens: bfloat16 [2, 2048, 2048], P('fsdp', 'ctx'), may hold values from -6 to 6
- cotangent: bfloat16 [2, 2048, 2048], P('fsdp', 'ctx'), may hold values from -6 to 6
- attn_gain: bfloat16 [2048], P('fsdp'), may hold values from 0.25 to 1.75
- w_query: bfloat16 [2048, 2048], P('fsdp'), may hold values from -0.125 to 0.125
- w_key: bfloat16 [2048, 2048], P('fsdp'), may hold values from -0.125 to 0.125
- w_value: bfloat16 [2048, 2048], P('fsdp'), may hold values from -0.125 to 0.125
- w_out: bfloat16 [2048, 2048], P('fsdp'), may hold values from -6 to 6
- query_gain: bfloat16 [2048], P('fsdp'), may hold values from 0.25 to 1.75
- key_gain: bfloat16 [2048], P('fsdp'), may hold values from 0.25 to 1.75
- ffn_gain: bfloat16 [2048], P('fsdp'), may hold values from 0.25 to 1.75
- router: bfloat16 [2048, 16], P('fsdp'), may hold values from -0.5 to 0.5
- w_gate: bfloat16 [16, 2048, 1024], P('ctx', 'fsdp'), may hold values from -0.125 to 0.125
- w_up: bfloat16 [16, 2048, 1024], P('ctx', 'fsdp'), may hold values from -0.125 to 0.125
- w_down: bfloat16 [16, 1024, 2048], P('ctx', None, 'fsdp'), may hold values from -3 to 3
- routes: int32 [2, 2048, 8], P('fsdp', 'ctx'), may hold values from 0 to 15, all different within a row; in each aligned block of 128 rows (0 to 127, 128 to 255, ..., all dimensions but the last counted through in order) at most 128 rows name the same one
- priority: int32 [2, 2048, 8], P('fsdp', 'ctx'), may hold values from 0 to 3
- positions: int32 [2, 2048], P('fsdp', 'ctx'), may hold values from 0 to 2047
Outputs:
- layer_out: bfloat16 [2, 2048, 2048], P('fsdp', 'ctx')
- input_grad: bfloat16 [2, 2048, 2048], P('fsdp', 'ctx')
- attn_gain_grad: float32 [2048], P(('ctx', 'fsdp'))
- w_query_grad: float32 [2048, 2048], P(('ctx', 'fsdp'))
- w_key_grad: float32 [2048, 2048], P(('ctx', 'fsdp'))
- w_value_grad: float32 [2048, 2048], P(('ctx', 'fsdp'))
- w_out_grad: float32 [2048, 2048], P(('ctx', 'fsdp'))
- query_gain_grad: float32 [2048], P(('ctx', 'fsdp'))
- key_gain_grad: float32 [2048], P(('ctx', 'fsdp'))
- ffn_gain_grad: float32 [2048], P(('ctx', 'fsdp'))
- router_grad: float32 [2048, 16], P(('ctx', 'fsdp'))
- w_gate_grad: float32 [16, 2048, 1024], P('ctx', 'fsdp')
- w_up_grad: float32 [16, 2048, 1024], P('ctx', 'fsdp')
- w_down_grad: float32 [16, 1024, 2048], P('ctx', None, 'fsdp')
The draws below stay inside these ranges and needn't reach their ends.
Inputs may be any that keep to these rules, and one draw needn't show every extreme that they name: `routes`: each row names 8 different experts. In every aligned block of 128 rows (the rows of one device) no expert is named by more than 128 rows, and in some block an expert is named by exactly 128 rows.
All inputs are finite; a program needn't handle non-finite values.
Results may differ from the reference program's by a relative error of at most 0.02.
Values may be sent and summed in bfloat16 or wider, within the bound.
No kernel may reach another device: no remote copies, remote signals or barrier semaphores. Data moves between devices by JAX's collectives and lax.ppermute only.
A program may use at most 704 MiB of HBM per device.

```python
import math
import jax
import jax.numpy as jnp
import numpy as np
from jax import lax

D = 2048
HEADS = 16
HEAD_DIM = 128
EXPERT_FF = 1024
TOP = 8
TOK_DEV = 128
LEVELS = 4
SEQS = 2
LENGTH = 2048
EXPERTS = 16
CAP = 1152
SEND = 128


def with_ends(values, rng, low, top_value):
    index_at = [jax.random.randint(jax.random.fold_in(rng, axis), (), 0, length) for axis, length in enumerate(values.shape)]
    longest = values.shape.index(max(values.shape))
    next_to = index_at[:longest] + [(index_at[longest] + 1) % values.shape[longest]] + index_at[longest + 1:]
    return values.at[tuple(index_at)].set(low).at[tuple(next_to)].set(top_value)


def level_of(own_key, extent, split, low, largest):
    factor_of, own = 1.0, jax.random.fold_in(own_key, 6)
    for position, parts in split:
        heights = jnp.exp(jax.random.uniform(jax.random.fold_in(own, position), (parts,), jnp.float32, low / len(split), largest / len(split)))
        factor_of = factor_of * jnp.repeat(heights, extent[position] // parts).reshape([-1 if axis == position else 1 for axis in range(len(extent))])
    return factor_of


def routed_block(own_key, own, number, rows, count, top, limit, skew):
    order = jax.random.permutation(own_key, count)
    crowded, usual = portions_of(count, rows * top, limit, skew, True), portions_of(count, rows * top, limit, skew, False)
    places = jnp.arange(count)

    def named(lengths, offset_by):
        used = int((lengths > 0).sum())
        fixed = max(1, used // 4)
        shifted = fixed + (places - fixed + offset_by * (used - fixed)) % max(1, count - fixed)
        return jnp.zeros((count,), jnp.int32).at[order[jnp.where(places < fixed, places, shifted)]].set(jnp.asarray(lengths, jnp.int32))

    lengths = jnp.where(number % 4 == 0, named(crowded, number // 4), named(usual, number - number // 4 - 1))
    mixed = jax.random.permutation(jax.random.fold_in(own, 3), count)
    source_of, receiver = mixed[0:count // 2 * 2:2], mixed[1:count // 2 * 2:2]
    slack = jnp.minimum(lengths[source_of] - 1, limit - lengths[receiver]) // 2
    slack = jnp.where((source_of == order[0]) | (receiver == order[0]) | (lengths[receiver] == 0), 0, jnp.maximum(slack, 0))
    shifted = jax.random.randint(jax.random.fold_in(own, 4), (count // 2,), 0, 1 << 20) % (slack + 1)
    lengths = lengths.at[source_of].add(-shifted).at[receiver].add(shifted)
    items = jnp.searchsorted(jnp.cumsum(lengths), jnp.arange(rows * top), side="right").astype(jnp.int32)
    table = items.reshape(top, rows).T
    table = table[jax.random.permutation(jax.random.fold_in(own, 1), rows)]
    offset_by = jax.random.randint(jax.random.fold_in(own, 2), (rows, 1), 0, top)
    return jnp.take_along_axis(table, (jnp.arange(top)[None, :] + offset_by) % top, axis=1)


def portions_of(amount, total, most, slope, full):
    portions = [(1 << 20) // math.isqrt(rank ** slope) + 1 for rank in range(1, amount + 1)]
    largest = most if full else min(most, max(-(-total // amount), total * portions[0] // sum(portions)))
    least = 1 if total - largest >= amount - 1 else 0
    given, spare = [largest] + [least] * (amount - 1), total - largest - least * (amount - 1)
    while spare > 0:
        free = [i for i in range(1, amount) if given[i] < largest] or [i for i in range(1, amount) if given[i] < most]
        whole, remaining = sum([portions[i] for i in free]), spare
        for i in free:
            addition = min(most - given[i], max(1, remaining * portions[i] // whole), spare)
            given[i] = given[i] + addition
            spare = spare - addition
    return np.array(given)


def centred(rng, shape, spread, bound, shards=(), kind=jnp.bfloat16):
    loudness = level_of(rng, shape, shards, -0.22, 0.18) if shards else 1.0
    values = jax.random.normal(rng, shape, jnp.float32) * spread * loudness
    return jnp.minimum(jnp.maximum(values, -bound), bound).astype(kind)


def setup_inputs(seed: int = 0) -> dict:
    key_of = jax.random.split(jax.random.key(seed), 18)
    tokens = centred(key_of[0], (SEQS, LENGTH, D), 1.0, 6.0, ((0, 2), (1, 16)))
    cotangent = centred(key_of[1], (SEQS, LENGTH, D), 1.0, 6.0, ((0, 2), (1, 16)))
    attn_gain = jnp.clip(1.0 + 0.15 * jax.random.normal(key_of[2], (D,), jnp.float32), 0.25, 1.75).astype(jnp.bfloat16)
    w_query = centred(key_of[3], (D, D), D ** -0.5, 0.125, ((0, 2),))
    w_key = centred(key_of[4], (D, D), D ** -0.5, 0.125, ((0, 2),))
    w_value = centred(key_of[5], (D, D), D ** -0.5, 0.125, ((0, 2),))
    w_out = centred(key_of[6], (D, D), (0.6 * LENGTH ** 0.5 * D ** -0.5), 6.0, ((0, 2),))
    query_gain = jnp.clip(1.0 + 0.15 * jax.random.normal(key_of[7], (D,), jnp.float32), 0.25, 1.75).astype(jnp.bfloat16)
    key_gain = jnp.clip(1.0 + 0.15 * jax.random.normal(key_of[8], (D,), jnp.float32), 0.25, 1.75).astype(jnp.bfloat16)
    ffn_gain = jnp.clip(1.0 + 0.15 * jax.random.normal(key_of[9], (D,), jnp.float32), 0.25, 1.75).astype(jnp.bfloat16)
    router = centred(key_of[10], (D, EXPERTS), (1.5 * D ** -0.5), 0.5, ((0, 2),))
    w_gate = centred(key_of[11], (EXPERTS, D, EXPERT_FF), D ** -0.5, 0.125, ((0, 16), (1, 2)))
    w_up = centred(key_of[12], (EXPERTS, D, EXPERT_FF), D ** -0.5, 0.125, ((0, 16), (1, 2)))
    w_down = centred(key_of[13], (EXPERTS, EXPERT_FF, D), (0.4 * EXPERTS * EXPERT_FF ** -0.5), 3.0, ((0, 16), (2, 2)))
    routes_keys = jax.random.split(jax.random.fold_in(key_of[14], 1), SEQS * LENGTH // TOK_DEV)
    routes_turns = jax.random.permutation(jax.random.fold_in(key_of[14], 3), SEQS * LENGTH // TOK_DEV)
    routes = jax.vmap(lambda own, number: routed_block(jax.random.fold_in(key_of[14], 2), own, number, TOK_DEV, EXPERTS, TOP, SEND, 1))(routes_keys, routes_turns).reshape((SEQS, LENGTH, TOP))
    priority = with_ends(jax.random.randint(key_of[15], (SEQS, LENGTH, TOP), 0, LEVELS), jax.random.fold_in(key_of[15], 1), 0, LEVELS - 1).astype(jnp.int32)
    positions = with_ends(jax.random.randint(key_of[16], (SEQS, LENGTH), 0, LENGTH), jax.random.fold_in(key_of[16], 1), 0, LENGTH - 1).astype(jnp.int32)
    return dict(tokens=tokens, cotangent=cotangent, attn_gain=attn_gain, w_query=w_query, w_key=w_key, w_value=w_value, w_out=w_out, query_gain=query_gain, key_gain=key_gain, ffn_gain=ffn_gain, router=router, w_gate=w_gate, w_up=w_up, w_down=w_down, routes=routes, priority=priority, positions=positions)


epsilon = 1e-05
rope_base = 50000.0

@jax.custom_vjp
def low(v):
    return lax.optimization_barrier(v.astype(jnp.bfloat16)).astype(jnp.float32)

@jax.custom_vjp
def low_back(v):
    return v

def low_keep(v):
    return (low(v), None)

def low_pass(kept, grad):
    return (grad,)

def back_keep(v):
    return (v, None)

def back_low(kept, grad):
    return (low(grad),)
low.defvjp(low_keep, low_pass)
low_back.defvjp(back_keep, back_low)

def product(left, right):
    return jnp.dot(left, right, precision=lax.Precision.HIGHEST, preferred_element_type=jnp.float32)

def rms_scale(matrix, gain_row):
    return matrix * lax.rsqrt(lax.optimization_barrier(jnp.mean(matrix * matrix, axis=-1, keepdims=True)) + epsilon) * gain_row

def rotate(matrix, position_ids):
    count_rows = matrix.shape[0]
    by_head = matrix.reshape(count_rows, HEADS, HEAD_DIM)
    half_dim = HEAD_DIM // 2
    inverse = rope_base ** (-(jnp.arange(half_dim, dtype=jnp.float32) * 2.0) / HEAD_DIM)
    angles = position_ids.astype(jnp.float32)[:, None] * inverse[None, :]
    cosine = jnp.cos(angles)[:, None, :]
    sine_part = jnp.sin(angles)[:, None, :]
    lower_half = by_head[..., :half_dim]
    upper_half = by_head[..., half_dim:]
    turned = jnp.concatenate([lower_half * cosine - upper_half * sine_part, upper_half * cosine + lower_half * sine_part], axis=-1)
    return turned.reshape(count_rows, D)

def attend(queries, key_rows, value_rows):
    length = key_rows.shape[0]
    block_rows = math.gcd(length, 512)
    score_scale = HEAD_DIM ** (-0.5)
    key_heads = key_rows.reshape(length, HEADS, HEAD_DIM)
    value_heads = value_rows.reshape(length, HEADS, HEAD_DIM)
    query_blocks = queries.reshape(length // block_rows, block_rows, HEADS, HEAD_DIM)

    def one_block(query_block):
        scores = low_back(jnp.einsum('qhd,khd->hqk', query_block, key_heads, precision=lax.Precision.HIGHEST) * score_scale)
        row_max = lax.optimization_barrier(jnp.max(scores, axis=-1, keepdims=True))
        exps_raw = jnp.exp(scores - row_max)
        probs_low = low(exps_raw / lax.optimization_barrier(jnp.sum(exps_raw, axis=-1, keepdims=True)))
        return jnp.einsum('hqk,khd->qhd', probs_low, value_heads, precision=lax.Precision.HIGHEST)
    attended = lax.map(jax.checkpoint(one_block), query_blocks)
    return attended.reshape(length, D)

def sequence(inputs, params, route_ids, level_ids, position_ids):
    attn_gain, w_query, w_key, w_value, w_out, query_gain, key_gain, ffn_gain, router, w_gate, w_up, w_down = params
    length = inputs.shape[0]
    normed = low(rms_scale(inputs, attn_gain))
    q_lin = low_back(product(normed, w_query))
    k_lin = low_back(product(normed, w_key))
    v_lin = low_back(product(normed, w_value))
    queries = low(rotate(rms_scale(q_lin, query_gain), position_ids))
    key_rows = low(rotate(rms_scale(k_lin, key_gain), position_ids))
    value_rows = low(v_lin)
    mixed = low_back(low(attend(queries, key_rows, value_rows)))
    middle = inputs + low_back(product(mixed, w_out))
    hidden = low(rms_scale(middle, ffn_gain))
    logits = product(hidden, router)
    row_max = lax.optimization_barrier(jnp.max(logits, axis=-1, keepdims=True))
    exps_raw = jnp.exp(logits - row_max)
    router_probs = exps_raw / lax.optimization_barrier(jnp.sum(exps_raw, axis=-1, keepdims=True))
    pair_code = level_ids * EXPERTS + route_ids
    pair_table = (pair_code[:, :, None] == jnp.arange(LEVELS * EXPERTS, dtype=jnp.int32)[None, None, :]).astype(jnp.int32)
    per_token = lax.optimization_barrier(jnp.sum(pair_table, axis=1)).astype(jnp.int32)
    before_rows = (jnp.cumsum(per_token, axis=0) - per_token).astype(jnp.int32)
    level_totals = lax.optimization_barrier(jnp.sum(per_token, axis=0)).reshape(LEVELS, EXPERTS).astype(jnp.int32)
    level_base = (jnp.cumsum(level_totals, axis=0) - level_totals).reshape(LEVELS * EXPERTS).astype(jnp.int32)
    pair_rank = lax.optimization_barrier(jnp.sum(pair_table * (before_rows + level_base[None, :])[:, None, :], axis=-1)).astype(jnp.int32)
    is_kept = pair_rank < CAP
    token_index = jnp.broadcast_to(jnp.arange(length, dtype=jnp.int32)[:, None], (length, TOP))
    target = jnp.where(is_kept, route_ids * CAP + pair_rank, EXPERTS * CAP).astype(jnp.int32)
    slot_token = jnp.full((EXPERTS * CAP + 1,), length, jnp.int32).at[target.reshape(-1)].set(token_index.reshape(-1))[:EXPERTS * CAP]
    padded = jnp.concatenate([hidden, jnp.zeros((1, D), hidden.dtype)], axis=0)
    expert_in = low_back(padded[slot_token]).reshape(EXPERTS, CAP, D)
    gate_lin = low_back(jnp.einsum('ecd,edf->ecf', expert_in, w_gate, precision=lax.Precision.HIGHEST))
    up_lin = low_back(jnp.einsum('ecd,edf->ecf', expert_in, w_up, precision=lax.Precision.HIGHEST))
    swiglu = low(gate_lin * jax.nn.sigmoid(gate_lin) * up_lin)
    expert_out = low_back(low(jnp.einsum('ecf,efd->ecd', swiglu, w_down, precision=lax.Precision.HIGHEST)))
    out_flat = jnp.concatenate([expert_out.reshape(EXPERTS * CAP, D), jnp.zeros((1, D), expert_out.dtype)], axis=0)
    pair_out = out_flat[target]
    expert_hot = route_ids[:, :, None] == jnp.arange(EXPERTS, dtype=jnp.int32)[None, None, :]
    chosen = lax.optimization_barrier(jnp.sum(jnp.where(expert_hot, router_probs[:, None, :], 0.0), axis=-1))
    share = jnp.where(is_kept, chosen, 0.0)
    return middle + lax.optimization_barrier(jnp.sum(share[:, :, None] * pair_out, axis=1))

def reference(tokens, cotangent, attn_gain, w_query, w_key, w_value, w_out, query_gain, key_gain, ffn_gain, router, w_gate, w_up, w_down, routes, priority, positions):
    params = (attn_gain.astype(jnp.float32), w_query.astype(jnp.float32), w_key.astype(jnp.float32), w_value.astype(jnp.float32), w_out.astype(jnp.float32), query_gain.astype(jnp.float32), key_gain.astype(jnp.float32), ffn_gain.astype(jnp.float32), router.astype(jnp.float32), w_gate.astype(jnp.float32), w_up.astype(jnp.float32), w_down.astype(jnp.float32))
    inputs = tokens.astype(jnp.float32)

    def forward(layer_in, weights):
        return jnp.stack([sequence(layer_in[seq_index], weights, routes[seq_index], priority[seq_index], positions[seq_index]) for seq_index in range(SEQS)])
    result, pullback = jax.vjp(forward, inputs, params)
    grad_in, grads = pullback(cotangent.astype(jnp.float32))
    return (result.astype(jnp.bfloat16), grad_in.astype(jnp.bfloat16), grads[0], grads[1], grads[2], grads[3], grads[4], grads[5], grads[6], grads[7], grads[8], grads[9], grads[10], grads[11])
```

```python
import math

import jax
import jax.numpy as jnp
from jax import lax
from jax.experimental import pallas as pl
from jax.experimental.pallas import tpu as pltpu
from jax.sharding import Mesh
from jax.sharding import PartitionSpec as P

HEAD_DIM = 128
LEVELS = 4


epsilon = 1e-05
rope_base = 50000.0


def prefix(part, axis, combine, identity):
    place = lax.axis_index(axis)
    gathered = lax.all_gather(part, axis)
    state = jnp.zeros_like(part) + jnp.asarray(identity, part.dtype)

    def one(turn, state):
        return combine(state, lax.dynamic_index_in_dim(gathered, turn, 0, False))

    return lax.fori_loop(0, place, one, state)


def product(left, right):
    return jnp.dot(left, right, preferred_element_type=jnp.float32)


def precise(left, right):
    return jnp.dot(left, right, precision=lax.Precision.HIGHEST, preferred_element_type=jnp.float32)


def contract_rows(left, right):
    return lax.dot_general(
        left, right, (((0,), (0,)), ((), ())), preferred_element_type=jnp.float32
    )


def contract_cols(left, right):
    return lax.dot_general(
        left, right, (((1,), (1,)), ((), ())), preferred_element_type=jnp.float32
    )


def rms_forward(matrix, gain_row):
    inverse = lax.rsqrt(jnp.mean(matrix * matrix, axis=-1, keepdims=True) + epsilon)
    return (matrix * inverse * gain_row, inverse)


def rms_backward(matrix, inverse, gain_row, upstream):
    scaled = upstream * gain_row
    along = jnp.mean(scaled * matrix, axis=-1, keepdims=True)
    grad_rows = inverse * scaled - matrix * inverse * inverse * inverse * along
    grad_gain = jnp.sum(upstream * matrix * inverse, axis=0)
    return (grad_rows, grad_gain)


def rope_tables(position_ids, head_dim):
    half_dim = head_dim // 2
    inverse = rope_base ** (-(jnp.arange(half_dim, dtype=jnp.float32) * 2.0) / head_dim)
    angles = position_ids.astype(jnp.float32)[:, None] * inverse[None, :]
    return (jnp.cos(angles)[:, None, :], jnp.sin(angles)[:, None, :])


def rotate(matrix, cosine, sine_part, head_dim, turn_sign):
    count_rows = matrix.shape[0]
    by_head = matrix.reshape(count_rows, -1, head_dim)
    half_dim = head_dim // 2
    lower_half = by_head[..., :half_dim]
    upper_half = by_head[..., half_dim:]
    turned = jnp.concatenate(
        [
            lower_half * cosine - turn_sign * upper_half * sine_part,
            upper_half * cosine + turn_sign * lower_half * sine_part,
        ],
        axis=-1,
    )
    return turned.reshape(count_rows, -1)


def add_counts(earlier_part, later_part):
    return earlier_part + later_part


def score_block(query_part, key_part, score_scale):
    return (
        jnp.einsum("qhd,khd->hqk", query_part, key_part, preferred_element_type=jnp.float32)
        * score_scale
    )


def grad_block(query_part, dout_part, lse_part, delta_part, key_part, value_part, score_scale):
    probs = jnp.exp(score_block(query_part, key_part, score_scale) - lse_part)
    prob_low = probs.astype(jnp.bfloat16)
    dprob = jnp.einsum("qhd,khd->hqk", dout_part, value_part, preferred_element_type=jnp.float32)
    dscore = (probs * (dprob - delta_part)).astype(jnp.bfloat16)
    return (prob_low, dscore)


def general_body(
    tokens,
    cotangent,
    attn_gain,
    w_query,
    w_key,
    w_value,
    w_out,
    query_gain,
    key_gain,
    ffn_gain,
    router,
    w_gate,
    w_up,
    w_down,
    routes,
    priority,
    positions,
):
    ctx_count = lax.axis_size("ctx")
    (
        g_attn,
        q_weight,
        k_weight,
        v_weight,
        o_weight,
        g_query,
        g_key,
        g_ffn,
        r_weight,
        gate_full,
        up_full,
        down_full,
    ) = (
        lax.all_gather(attn_gain, "fsdp", axis=0, tiled=True),
        lax.all_gather(w_query, "fsdp", axis=0, tiled=True),
        lax.all_gather(w_key, "fsdp", axis=0, tiled=True),
        lax.all_gather(w_value, "fsdp", axis=0, tiled=True),
        lax.all_gather(w_out, "fsdp", axis=0, tiled=True),
        lax.all_gather(query_gain, "fsdp", axis=0, tiled=True),
        lax.all_gather(key_gain, "fsdp", axis=0, tiled=True),
        lax.all_gather(ffn_gain, "fsdp", axis=0, tiled=True),
        lax.all_gather(router, "fsdp", axis=0, tiled=True),
        lax.all_gather(w_gate, "fsdp", axis=1, tiled=True),
        lax.all_gather(w_up, "fsdp", axis=1, tiled=True),
        lax.all_gather(w_down, "fsdp", axis=2, tiled=True),
    )
    gate_weight = gate_full[0]
    up_weight = up_full[0]
    down_weight = down_full[0]
    tok_rows = tokens.shape[1]
    model_width = tokens.shape[2]
    head_dim = HEAD_DIM
    head_count = model_width // head_dim
    length = tok_rows * ctx_count
    top_k = routes.shape[2]
    capacity = 9 * tok_rows
    send_rows = 2 * tok_rows * top_k // ctx_count
    key_block = math.gcd(length, 1024)
    block_count = length // key_block
    score_scale = head_dim ** (-0.5)
    inputs = tokens[0].astype(jnp.float32)
    normed, inv_one = rms_forward(inputs, g_attn)
    h_one = normed.astype(jnp.bfloat16)
    q_lin = product(h_one, q_weight)
    k_lin = product(h_one, k_weight)
    v_lin = product(h_one, v_weight)
    cosine, sine_part = rope_tables(positions[0], head_dim)
    q_normed, inv_query = rms_forward(q_lin, g_query)
    k_normed, inv_key = rms_forward(k_lin, g_key)
    q_rot = rotate(q_normed, cosine, sine_part, head_dim, 1.0).astype(jnp.bfloat16)
    k_rot = rotate(k_normed, cosine, sine_part, head_dim, 1.0).astype(jnp.bfloat16)
    v_low = v_lin.astype(jnp.bfloat16)
    all_keys, all_values = (
        lax.all_gather(k_rot, "ctx", axis=0, tiled=True),
        lax.all_gather(v_low, "ctx", axis=0, tiled=True),
    )
    q_heads = q_rot.reshape(tok_rows, head_count, head_dim)

    def key_slice(block_id):
        start = block_id * key_block
        key_part = lax.dynamic_slice_in_dim(all_keys, start, key_block, 0).reshape(
            key_block, head_count, head_dim
        )
        value_part = lax.dynamic_slice_in_dim(all_values, start, key_block, 0).reshape(
            key_block, head_count, head_dim
        )
        return (key_part, value_part)

    def lse_step(carry, block_id):
        run_max, run_total = carry
        key_part, value_part = key_slice(block_id)
        scores = score_block(q_heads, key_part, score_scale)
        new_max = jnp.maximum(run_max, jnp.max(scores, axis=-1, keepdims=True))
        run_total = run_total * jnp.exp(run_max - new_max) + jnp.sum(
            jnp.exp(scores - new_max), axis=-1, keepdims=True
        )
        return ((new_max, run_total), None)

    start_max = jnp.full((head_count, tok_rows, 1), -jnp.inf, jnp.float32)
    start_total = jnp.zeros((head_count, tok_rows, 1), jnp.float32)
    (run_max, run_total), _ = lax.scan(lse_step, (start_max, start_total), jnp.arange(block_count))
    lse = run_max + jnp.log(run_total)

    def out_step(acc, block_id):
        key_part, value_part = key_slice(block_id)
        probs = jnp.exp(score_block(q_heads, key_part, score_scale) - lse).astype(jnp.bfloat16)
        return (
            acc + jnp.einsum("hqk,khd->qhd", probs, value_part, preferred_element_type=jnp.float32),
            None,
        )

    attended_heads, _ = lax.scan(
        out_step, jnp.zeros((tok_rows, head_count, head_dim), jnp.float32), jnp.arange(block_count)
    )
    attended = attended_heads.reshape(tok_rows, model_width)
    mixed_low = attended.astype(jnp.bfloat16)
    middle = inputs + product(mixed_low, o_weight)
    h_two_f, inv_two = rms_forward(middle, g_ffn)
    h_two = h_two_f.astype(jnp.bfloat16)
    logits = product(h_two, r_weight)
    row_max = jnp.max(logits, axis=-1, keepdims=True)
    exps_raw = jnp.exp(logits - row_max)
    router_probs = exps_raw / jnp.sum(exps_raw, axis=-1, keepdims=True)
    route_ids = routes[0]
    level_ids = priority[0]
    pair_code = level_ids * ctx_count + route_ids
    code_table = (
        pair_code[:, :, None] == jnp.arange(LEVELS * ctx_count, dtype=jnp.int32)[None, None, :]
    ).astype(jnp.float32)
    per_token = jnp.sum(code_table, axis=1)
    before_local = jnp.cumsum(per_token, axis=0) - per_token
    local_total = jnp.sum(per_token, axis=0)
    earlier = prefix(local_total, "ctx", add_counts, jnp.zeros_like(local_total))
    totals = lax.psum(local_total, "ctx")
    level_totals = totals.reshape(LEVELS, ctx_count)
    level_base = (jnp.cumsum(level_totals, axis=0) - level_totals).reshape(-1)
    offsets = before_local + (earlier + level_base)[None, :]
    pair_rank = jnp.sum(code_table * offsets[:, None, :], axis=-1).astype(jnp.int32)
    is_kept = pair_rank < capacity
    expert_hot = (
        route_ids[:, :, None] == jnp.arange(ctx_count, dtype=jnp.int32)[None, None, :]
    ).astype(jnp.float32)
    per_expert = jnp.sum(expert_hot, axis=1)
    local_before = jnp.cumsum(per_expert, axis=0) - per_expert
    local_slot = jnp.sum(expert_hot * local_before[:, None, :], axis=-1).astype(jnp.int32)
    send_index = (route_ids * send_rows + local_slot).reshape(-1)
    pair_count = tok_rows * top_k
    pair_of_slot = (
        jnp.full((ctx_count * send_rows,), pair_count, jnp.int32)
        .at[send_index]
        .set(jnp.arange(pair_count, dtype=jnp.int32))
    )
    slot_target = jnp.where(is_kept, pair_rank, capacity).reshape(-1)
    target_pad = jnp.concatenate([slot_target, jnp.full((1,), capacity, jnp.int32)], axis=0)
    send_slots = target_pad[pair_of_slot].reshape(ctx_count, send_rows)
    h_pad = jnp.concatenate([h_two, jnp.zeros((1, model_width), jnp.bfloat16)], axis=0)
    send_tokens = h_pad[pair_of_slot // top_k].reshape(ctx_count, send_rows, model_width)
    got_tokens, got_slots = (
        lax.all_to_all(send_tokens, "ctx", split_axis=0, concat_axis=0, tiled=True),
        lax.all_to_all(send_slots, "ctx", split_axis=0, concat_axis=0, tiled=True),
    )
    received_count = ctx_count * send_rows
    slots_flat = got_slots.reshape(-1)
    row_of_slot = (
        jnp.full((capacity,), received_count, jnp.int32)
        .at[slots_flat]
        .set(jnp.arange(received_count, dtype=jnp.int32), mode="drop")
    )
    got_pad = jnp.concatenate(
        [
            got_tokens.reshape(received_count, model_width),
            jnp.zeros((1, model_width), jnp.bfloat16),
        ],
        axis=0,
    )
    expert_in = got_pad[row_of_slot]
    gate_lin = product(expert_in, gate_weight)
    up_lin = product(expert_in, up_weight)
    sig_gate = jax.nn.sigmoid(gate_lin)
    silu_val = gate_lin * sig_gate
    swiglu = (silu_val * up_lin).astype(jnp.bfloat16)
    expert_out = product(swiglu, down_weight).astype(jnp.bfloat16)
    out_pad = jnp.concatenate([expert_out, jnp.zeros((1, model_width), jnp.bfloat16)], axis=0)
    back_rows = out_pad[slots_flat].reshape(ctx_count, send_rows, model_width)
    returned = lax.all_to_all(back_rows, "ctx", split_axis=0, concat_axis=0, tiled=True)
    returned_pad = jnp.concatenate(
        [
            returned.reshape(ctx_count * send_rows, model_width),
            jnp.zeros((1, model_width), jnp.bfloat16),
        ],
        axis=0,
    )
    pair_out = returned_pad[send_index].reshape(tok_rows, top_k, model_width)
    chosen = jnp.sum(router_probs[:, None, :] * expert_hot, axis=-1)
    share = jnp.where(is_kept, chosen, 0.0)
    mixture = jnp.einsum("tk,tkd->td", share, pair_out, preferred_element_type=jnp.float32)
    final_rows = middle + mixture
    layer_out = final_rows.astype(jnp.bfloat16)
    grad_out = cotangent[0].astype(jnp.float32)
    routed_grad = (share[:, :, None] * grad_out[:, None, :]).astype(jnp.bfloat16)
    share_grad = jnp.where(
        is_kept,
        jnp.einsum("tkd,td->tk", pair_out, grad_out, preferred_element_type=jnp.float32),
        0.0,
    )
    prob_grad = jnp.sum(expert_hot * share_grad[:, :, None], axis=1)
    logit_grad = router_probs * (
        prob_grad - jnp.sum(router_probs * prob_grad, axis=-1, keepdims=True)
    )
    routed_pad = jnp.concatenate(
        [routed_grad.reshape(pair_count, model_width), jnp.zeros((1, model_width), jnp.bfloat16)],
        axis=0,
    )
    send_grads = routed_pad[pair_of_slot].reshape(ctx_count, send_rows, model_width)
    got_grads = lax.all_to_all(send_grads, "ctx", split_axis=0, concat_axis=0, tiled=True)
    grad_pad = jnp.concatenate(
        [got_grads.reshape(received_count, model_width), jnp.zeros((1, model_width), jnp.bfloat16)],
        axis=0,
    )
    out_grad = grad_pad[row_of_slot]
    act_grad = contract_cols(out_grad, down_weight)
    down_wgrad = contract_rows(swiglu, out_grad)
    gate_grad = (act_grad * up_lin * sig_gate * (1.0 + gate_lin * (1.0 - sig_gate))).astype(
        jnp.bfloat16
    )
    up_grad = (act_grad * silu_val).astype(jnp.bfloat16)
    in_grad = (contract_cols(gate_grad, gate_weight) + contract_cols(up_grad, up_weight)).astype(
        jnp.bfloat16
    )
    gate_wgrad = contract_rows(expert_in, gate_grad)
    up_wgrad = contract_rows(expert_in, up_grad)
    in_pad = jnp.concatenate([in_grad, jnp.zeros((1, model_width), jnp.bfloat16)], axis=0)
    back_grads = in_pad[slots_flat].reshape(ctx_count, send_rows, model_width)
    pair_grads = lax.all_to_all(back_grads, "ctx", split_axis=0, concat_axis=0, tiled=True)
    pair_pad = jnp.concatenate(
        [
            pair_grads.reshape(ctx_count * send_rows, model_width),
            jnp.zeros((1, model_width), jnp.bfloat16),
        ],
        axis=0,
    )
    token_pair = pair_pad[send_index].reshape(tok_rows, top_k, model_width)
    hidden_grad = jnp.sum(token_pair.astype(jnp.float32), axis=1) + precise(
        logit_grad, r_weight.astype(jnp.float32).T
    )
    router_wgrad = precise(h_two.astype(jnp.float32).T, logit_grad)
    norm_grad, ffn_gain_grad = rms_backward(middle, inv_two, g_ffn, hidden_grad)
    middle_grad = grad_out + norm_grad
    branch_grad = middle_grad.astype(jnp.bfloat16)
    out_wgrad = contract_rows(mixed_low, branch_grad)
    mixed_grad = contract_cols(branch_grad, o_weight).astype(jnp.bfloat16)
    dout_heads = mixed_grad.reshape(tok_rows, head_count, head_dim)
    delta = jnp.sum(dout_heads.astype(jnp.float32) * attended_heads, axis=-1).T[:, :, None]

    def back_step(dq_acc, block_id):
        key_part, value_part = key_slice(block_id)
        prob_low, dscore = grad_block(
            q_heads, dout_heads, lse, delta, key_part, value_part, score_scale
        )
        dq_acc = dq_acc + jnp.einsum(
            "hqk,khd->qhd", dscore, key_part, preferred_element_type=jnp.float32
        )
        dk_part = jnp.einsum(
            "hqk,qhd->khd", dscore, q_heads, preferred_element_type=jnp.float32
        ).reshape(key_block, model_width)
        dv_part = jnp.einsum(
            "hqk,qhd->khd", prob_low, dout_heads, preferred_element_type=jnp.float32
        ).reshape(key_block, model_width)
        return (dq_acc, jnp.concatenate([dk_part, dv_part], axis=1))

    dq_heads, kv_terms = lax.scan(
        back_step, jnp.zeros((tok_rows, head_count, head_dim), jnp.float32), jnp.arange(block_count)
    )
    kv_mine = lax.psum_scatter(
        kv_terms.reshape(length, 2 * model_width), "ctx", scatter_dimension=0, tiled=True
    )
    key_grad = kv_mine[:, :model_width] * score_scale
    value_grad = kv_mine[:, model_width:]
    v_lin_low = value_grad.astype(jnp.bfloat16)
    q_grad = dq_heads.reshape(tok_rows, model_width) * score_scale
    q_back = rotate(q_grad, cosine, sine_part, head_dim, -1.0)
    k_back = rotate(key_grad, cosine, sine_part, head_dim, -1.0)
    q_lin_grad, query_gain_grad = rms_backward(q_lin, inv_query, g_query, q_back)
    k_lin_grad, key_gain_grad = rms_backward(k_lin, inv_key, g_key, k_back)
    q_lin_low = q_lin_grad.astype(jnp.bfloat16)
    k_lin_low = k_lin_grad.astype(jnp.bfloat16)
    h_grad = (
        contract_cols(q_lin_low, q_weight)
        + contract_cols(k_lin_low, k_weight)
        + contract_cols(v_lin_low, v_weight)
    )
    query_wgrad = contract_rows(h_one, q_lin_low)
    key_wgrad = contract_rows(h_one, k_lin_low)
    value_wgrad = contract_rows(h_one, v_lin_low)
    in_norm_grad, attn_gain_grad = rms_backward(inputs, inv_one, g_attn, h_grad)
    input_grad = (middle_grad + in_norm_grad).astype(jnp.bfloat16)
    s_gate, s_up, s_down = (
        lax.psum_scatter(
            gate_wgrad[None].astype(jnp.bfloat16), "fsdp", scatter_dimension=1, tiled=True
        ).astype(jnp.float32),
        lax.psum_scatter(
            up_wgrad[None].astype(jnp.bfloat16), "fsdp", scatter_dimension=1, tiled=True
        ).astype(jnp.float32),
        lax.psum_scatter(
            down_wgrad[None].astype(jnp.bfloat16), "fsdp", scatter_dimension=2, tiled=True
        ).astype(jnp.float32),
    )
    d_attn, d_query, d_key, d_value, d_out, d_qgain, d_kgain, d_ffn, d_router = (
        lax.psum_scatter(attn_gain_grad, ("ctx", "fsdp"), scatter_dimension=0, tiled=True),
        lax.psum_scatter(query_wgrad, ("ctx", "fsdp"), scatter_dimension=0, tiled=True),
        lax.psum_scatter(key_wgrad, ("ctx", "fsdp"), scatter_dimension=0, tiled=True),
        lax.psum_scatter(value_wgrad, ("ctx", "fsdp"), scatter_dimension=0, tiled=True),
        lax.psum_scatter(out_wgrad, ("ctx", "fsdp"), scatter_dimension=0, tiled=True),
        lax.psum_scatter(query_gain_grad, ("ctx", "fsdp"), scatter_dimension=0, tiled=True),
        lax.psum_scatter(key_gain_grad, ("ctx", "fsdp"), scatter_dimension=0, tiled=True),
        lax.psum_scatter(ffn_gain_grad, ("ctx", "fsdp"), scatter_dimension=0, tiled=True),
        lax.psum_scatter(router_wgrad, ("ctx", "fsdp"), scatter_dimension=0, tiled=True),
    )
    return (
        layer_out[None],
        input_grad[None],
        d_attn,
        d_query,
        d_key,
        d_value,
        d_out,
        d_qgain,
        d_kgain,
        d_ffn,
        d_router,
        s_gate,
        s_up,
        s_down,
    )


def ring_order(count):
    return [0, 2, 4, 6, 7, 5, 3, 1] if count == 8 else list(range(count))


def swap(array, axis):
    return lax.ppermute(array, axis, [(0, 1), (1, 0)])


def shift(array, by):
    order = ring_order(lax.axis_size("chip"))
    count = len(order)
    pairs = [(order[i], order[(i + by) % count]) for i in range(count)]
    return lax.ppermute(array, "chip", pairs)


def ring_blocks(block, row_axis=0):
    count = lax.axis_size("chip")
    blocks = {0: block}
    ahead, behind = block, block
    half = block.shape[row_axis] // 2
    for step in range(1, count // 2):
        ahead, behind = lax.optimization_barrier((ahead, behind))
        ahead, behind = shift(ahead, 1), shift(behind, -1)
        blocks[count - step] = ahead
        blocks[step] = behind
    low = lax.slice_in_dim(ahead, 0, half, axis=row_axis)
    high = lax.slice_in_dim(behind, half, 2 * half, axis=row_axis)
    low, high = lax.optimization_barrier((low, high))
    blocks[count // 2] = jnp.concatenate([shift(low, 1), shift(high, -1)], axis=row_axis)
    return [blocks[place] for place in range(count)]


def gather_rows(block, row_axis=0):
    mine = jnp.concatenate(ring_blocks(block, row_axis), axis=row_axis)
    return jnp.concatenate([mine, swap(mine, "core")], axis=row_axis)


def scatter_rows(terms):
    count = lax.axis_size("chip")
    half_rows = terms.shape[0] // 2
    rows = half_rows // count
    half = rows // 2
    both = terms[:half_rows].astype(jnp.float32) + swap(terms[half_rows:], "core").astype(
        jnp.float32
    )
    both = both.astype(jnp.bfloat16)

    def part(place):
        place = place % count
        return both[place * rows : (place + 1) * rows]

    far = count // 2
    ahead, behind = part(far)[:half], part(far)[half:]
    ahead, behind = shift(ahead, 1), shift(behind, -1)

    def grow(mine, low, high):
        return (
            mine.astype(jnp.float32)
            + jnp.concatenate(
                [
                    jnp.zeros_like(mine[:half]) if low is None else low,
                    jnp.zeros_like(mine[half:]) if high is None else high,
                ],
                axis=0,
            ).astype(jnp.float32)
        ).astype(jnp.bfloat16)

    ahead = grow(part(far - 1), ahead, None)
    behind = grow(part(far + 1), None, behind)
    for step in range(far - 2, -1, -1):
        ahead, behind = lax.optimization_barrier((ahead, behind))
        ahead, behind = shift(ahead, 1), shift(behind, -1)
        if step:
            ahead = (part(step).astype(jnp.float32) + ahead.astype(jnp.float32)).astype(
                jnp.bfloat16
            )
            behind = (part(-step).astype(jnp.float32) + behind.astype(jnp.float32)).astype(
                jnp.bfloat16
            )
    return part(0).astype(jnp.float32) + ahead.astype(jnp.float32) + behind.astype(jnp.float32)


def exchange(parts):
    count = lax.axis_size("chip")
    got = {0: parts[0]}
    for place in range(1, count):
        got[count - place] = shift(parts[place], place)
    return jnp.stack([got[place] for place in range(count)], axis=0)


def exchange_all(parts):
    count = lax.axis_size("chip")
    pair = jnp.stack([parts[:count], swap(parts[count:], "core")], axis=1)
    got = exchange(pair)
    return jnp.concatenate([got[:, 0], got[:, 1]], axis=0)


def sum_all(values):
    count = lax.axis_size("chip")
    both = values + swap(values[:, ::-1], "core")
    total = both
    for place in range(1, count):
        total = total + jnp.roll(shift(both, place), -place, axis=2)
    return total


ATTN_ROWS = 256


def attend_kernel(q_ref, k_ref, v_ref, out_ref, lse_ref, *, score_scale):
    scores = contract_cols(q_ref[...], k_ref[...]) * score_scale
    row_max = jnp.max(scores, axis=-1, keepdims=True)
    raw = jnp.exp(scores - row_max)
    total = jnp.sum(raw, axis=-1, keepdims=True)
    probs = (raw / total).astype(jnp.bfloat16)
    out_ref[...] = product(probs, v_ref[...]).astype(jnp.bfloat16)
    lse_ref[...] = row_max + jnp.log(total)


def attend(queries, keys, values, score_scale):
    length, width = queries.shape
    rows = ATTN_ROWS
    whole = pl.BlockSpec((length, width), lambda i: (0, 0))
    block = pl.BlockSpec((rows, width), lambda i: (i, 0))
    column = pl.BlockSpec((rows, 1), lambda i: (i, 0))
    return pl.pallas_call(
        lambda *refs: attend_kernel(*refs, score_scale=score_scale),
        grid=(length // rows,),
        in_specs=[block, whole, whole],
        out_specs=[block, column],
        out_shape=[
            jax.ShapeDtypeStruct((length, width), jnp.bfloat16),
            jax.ShapeDtypeStruct((length, 1), jnp.float32),
        ],
        compiler_params=pltpu.CompilerParams(vmem_limit_bytes=48 << 20),
        cost_estimate=pl.CostEstimate(
            flops=4 * length * length * width,
            bytes_accessed=8 * length * width,
            transcendentals=length * length,
        ),
        name="attend",
    )(queries, keys, values)


def attend_back_kernel(
    q_ref, d_ref, lse_ref, k_ref, v_ref, dq_ref, dk_ref, dv_ref, *, score_scale
):
    @pl.when(pl.program_id(0) == 0)
    def _():
        dk_ref[...] = jnp.zeros_like(dk_ref)
        dv_ref[...] = jnp.zeros_like(dv_ref)

    queries, douts = q_ref[...], d_ref[...]
    probs = jnp.exp(contract_cols(queries, k_ref[...]) * score_scale - lse_ref[...])
    dprobs = contract_cols(douts, v_ref[...])
    delta = jnp.sum(probs * dprobs, axis=-1, keepdims=True)
    dscores = (probs * (dprobs - delta)).astype(jnp.bfloat16)
    dq_ref[...] = product(dscores, k_ref[...]) * score_scale
    dk_ref[...] += contract_rows(dscores, queries) * score_scale
    dv_ref[...] += contract_rows(probs.astype(jnp.bfloat16), douts)


def attend_back(queries, douts, lse, keys, values, score_scale):
    length, width = queries.shape
    rows = ATTN_ROWS
    whole = pl.BlockSpec((length, width), lambda i: (0, 0))
    block = pl.BlockSpec((rows, width), lambda i: (i, 0))
    column = pl.BlockSpec((rows, 1), lambda i: (i, 0))
    return pl.pallas_call(
        lambda *refs: attend_back_kernel(*refs, score_scale=score_scale),
        grid=(length // rows,),
        in_specs=[block, block, column, whole, whole],
        out_specs=[block, whole, whole],
        out_shape=[jax.ShapeDtypeStruct((length, width), jnp.float32)] * 3,
        compiler_params=pltpu.CompilerParams(vmem_limit_bytes=48 << 20),
        cost_estimate=pl.CostEstimate(
            flops=10 * length * length * width,
            bytes_accessed=20 * length * width,
            transcendentals=length * length,
        ),
        name="attend_back",
    )(queries, douts, lse, keys, values)


def body(
    tokens,
    cotangent,
    attn_gain,
    w_query,
    w_key,
    w_value,
    w_out,
    query_gain,
    key_gain,
    ffn_gain,
    router,
    w_gate,
    w_up,
    w_down,
    routes,
    priority,
    positions,
):
    low = jnp.bfloat16
    chips = lax.axis_size("chip")
    ctx_count = chips * 2
    place = lax.axis_index("chip") * 2 + lax.axis_index("core")
    part = lax.axis_index("fsdp")
    tok_rows, model_width = tokens.shape[1:]
    half_width = model_width // 2
    head_dim = HEAD_DIM
    length = tok_rows * ctx_count
    capacity = 9 * tok_rows
    score_scale = head_dim ** (-0.5)
    per_half = ctx_count // 2

    def turn(matrix, axis=-1):
        first, second = jnp.split(matrix, 2, axis=axis)
        return jnp.where(
            part == 0, matrix, jnp.concatenate([second, first], axis=axis)
        )

    def head_rows(matrix, width):
        return lax.dynamic_slice_in_dim(matrix, (place % per_half) * width, width, 0)

    small = jnp.concatenate(
        [
            router.T,
            attn_gain[None],
            ffn_gain[None],
            jnp.concatenate(
                [
                    head_rows(query_gain, head_dim),
                    head_rows(key_gain, head_dim),
                    jnp.zeros((half_width - 2 * head_dim,), low),
                ]
            )[None],
        ],
        axis=0,
    )
    small_other = swap(small, "fsdp")
    expert_count = router.shape[1]
    r_weight = jnp.concatenate([small[:expert_count], small_other[:expert_count]], axis=1)
    g_attn = jnp.concatenate([small[expert_count], small_other[expert_count]]).astype(jnp.float32)
    g_ffn = jnp.concatenate([small[expert_count + 1], small_other[expert_count + 1]]).astype(
        jnp.float32
    )
    here = part == place // per_half
    g_heads = jnp.where(here, small[expert_count + 2], small_other[expert_count + 2]).astype(
        jnp.float32
    )
    g_query, g_key = g_heads[:head_dim], g_heads[head_dim : 2 * head_dim]

    qkv_mine = jnp.concatenate(
        [
            lax.dynamic_slice_in_dim(w, place * head_dim, head_dim, 1)
            for w in (w_query, w_key, w_value)
        ],
        axis=1,
    )
    qkv_weight = jnp.concatenate([qkv_mine, swap(qkv_mine, "fsdp")], axis=0)
    out_mine = head_rows(w_out, head_dim)
    out_weight = turn(jnp.where(here, out_mine, swap(out_mine, "fsdp")))

    route_ids, level_ids = routes[0], priority[0]
    hot = route_ids[:, :, None] == jnp.arange(expert_count, dtype=jnp.int32)[None, None, :]
    levels = jnp.sum(jnp.where(hot, level_ids[:, :, None] - LEVELS, 0), axis=1) + LEVELS
    tags = jnp.concatenate(
        [
            levels.T,
            (place * tok_rows + jnp.arange(tok_rows, dtype=jnp.int32))[None],
            positions,
        ],
        axis=0,
    )
    all_tags = gather_rows(tags, 1)
    expert_levels = lax.dynamic_index_in_dim(all_tags, place, 0, False)
    order_ids = all_tags[expert_count]
    sort_code = expert_levels * length + order_ids
    ranks = jnp.sum((sort_code[None, :] < sort_code[:, None]).astype(jnp.float32), axis=1)
    is_kept = (expert_levels < LEVELS) & (ranks < capacity)
    source_ids = order_ids.reshape(ctx_count, tok_rows)[:, 0] // tok_rows
    to_source = (
        source_ids[None, :] == jnp.arange(ctx_count, dtype=jnp.int32)[:, None]
    ).astype(jnp.float32)
    cosine, sine_part = rope_tables(all_tags[expert_count + 1], head_dim)
    cosine, sine_part = cosine[:, 0], sine_part[:, 0]
    cos_full = jnp.concatenate([cosine, cosine], axis=-1)
    sin_full = jnp.concatenate([-sine_part, sine_part], axis=-1)

    def spin(matrix):
        return jnp.concatenate([matrix[:, head_dim // 2 :], matrix[:, : head_dim // 2]], axis=-1)

    inputs = turn(tokens[0]).astype(jnp.float32)
    grad_low = turn(cotangent[0])
    grad_out = grad_low.astype(jnp.float32)
    normed, inv_one = rms_forward(inputs, g_attn)
    all_h_one = gather_rows(normed.astype(low))
    lin = product(all_h_one, qkv_weight)
    q_lin, k_lin, v_lin = jnp.split(lin, 3, axis=1)

    def token_sums(*columns):
        stacked = jnp.stack(columns, axis=0).reshape(len(columns), 2, chips, tok_rows)
        return sum_all(stacked).reshape(len(columns), length, 1) / model_width

    square = token_sums(jnp.sum(q_lin * q_lin, axis=-1), jnp.sum(k_lin * k_lin, axis=-1))
    inv_query, inv_key = lax.rsqrt(square[0] + epsilon), lax.rsqrt(square[1] + epsilon)
    q_normed = q_lin * inv_query * g_query
    k_normed = k_lin * inv_key * g_key
    q_rot = (q_normed * cos_full + spin(q_normed) * sin_full).astype(low)
    k_rot = (k_normed * cos_full + spin(k_normed) * sin_full).astype(low)
    v_low = v_lin.astype(low)
    mixed_low, lse = attend(q_rot, k_rot, v_low, score_scale)
    middle = inputs + scatter_rows(product(mixed_low, out_weight).astype(low))

    h_two_f, inv_two = rms_forward(middle, g_ffn)
    h_two = h_two_f.astype(low)
    logits = contract_cols(h_two, r_weight)
    row_max = jnp.max(logits, axis=-1, keepdims=True)
    exps_raw = jnp.exp(logits - row_max)
    router_probs = exps_raw / jnp.sum(exps_raw, axis=-1, keepdims=True)
    all_probs = gather_rows(router_probs.T, 1)
    share = jnp.where(is_kept, lax.dynamic_index_in_dim(all_probs, place, 0, False), 0.0)[:, None]
    all_h_two = gather_rows(h_two)
    all_grads = gather_rows(grad_low)
    gate_weight = jnp.concatenate([w_gate[0], swap(w_gate[0], "fsdp")], axis=0)
    up_weight = jnp.concatenate([w_up[0], swap(w_up[0], "fsdp")], axis=0)
    down_weight = jnp.concatenate([w_down[0], swap(w_down[0], "fsdp")], axis=1)
    gate_lin = product(all_h_two, gate_weight)
    up_lin = product(all_h_two, up_weight)
    sig_gate = jax.nn.sigmoid(gate_lin)
    silu_val = gate_lin * sig_gate
    swiglu = (silu_val * up_lin).astype(low)
    expert_out = product(swiglu, down_weight).astype(low).astype(jnp.float32)
    layer_rows = middle + scatter_rows((share * expert_out).astype(low))
    layer_out = turn(layer_rows.astype(low))
    grads_f = all_grads.astype(jnp.float32)
    share_grad = jnp.where(is_kept, jnp.sum(expert_out * grads_f, axis=-1), 0.0)
    out_grad = (share * grads_f).astype(low)
    act_grad = contract_cols(out_grad, down_weight)
    gate_grad = (act_grad * up_lin * sig_gate * (1.0 + gate_lin * (1.0 - sig_gate))).astype(low)
    up_grad = (act_grad * silu_val).astype(low)
    in_grad = (contract_cols(gate_grad, gate_weight) + contract_cols(up_grad, up_weight)).astype(low)
    hidden_sum = scatter_rows(in_grad)
    down_wgrad = contract_rows(swiglu, out_grad)
    gate_wgrad = contract_rows(all_h_two, gate_grad)
    up_wgrad = contract_rows(all_h_two, up_grad)

    def over_sequences(matrix, axis):
        mine, other = jnp.split(matrix, 2, axis=axis)
        return mine + swap(other.astype(low), "fsdp").astype(jnp.float32)

    s_gate = over_sequences(gate_wgrad, 0)[None]
    s_up = over_sequences(up_wgrad, 0)[None]
    s_down = over_sequences(down_wgrad, 1)[None]

    prob_grad = exchange_all(share_grad.reshape(ctx_count, tok_rows))
    prob_grad = precise(to_source, prob_grad).T
    logit_grad = router_probs * (
        prob_grad - jnp.sum(router_probs * prob_grad, axis=-1, keepdims=True)
    )
    hidden_grad = hidden_sum + precise(logit_grad, r_weight.astype(jnp.float32))
    router_wgrad = precise(h_two.astype(jnp.float32).T, logit_grad)
    norm_grad, ffn_gain_grad = rms_backward(middle, inv_two, g_ffn, hidden_grad)
    middle_grad = grad_out + norm_grad

    all_branch = gather_rows(middle_grad.astype(low))
    out_wgrad = contract_rows(mixed_low, all_branch)
    douts = contract_cols(all_branch, out_weight).astype(low)
    dq, dk, dv = attend_back(q_rot, douts, lse, k_rot, v_low, score_scale)
    q_back = dq * cos_full - spin(dq) * sin_full
    k_back = dk * cos_full - spin(dk) * sin_full
    along = token_sums(
        jnp.sum(q_back * g_query * q_lin, axis=-1), jnp.sum(k_back * g_key * k_lin, axis=-1)
    )
    q_lin_grad = inv_query * (q_back * g_query) - q_lin * inv_query**3 * along[0]
    k_lin_grad = inv_key * (k_back * g_key) - k_lin * inv_key**3 * along[1]
    query_gain_grad = jnp.sum(q_back * q_lin * inv_query, axis=0)
    key_gain_grad = jnp.sum(k_back * k_lin * inv_key, axis=0)
    lin_grad = jnp.concatenate([q_lin_grad, k_lin_grad, dv], axis=1).astype(low)
    h_grad = scatter_rows(contract_cols(lin_grad, qkv_weight).astype(low))
    qkv_wgrad = contract_rows(all_h_one, lin_grad)
    in_norm_grad, attn_gain_grad = rms_backward(inputs, inv_one, g_attn, h_grad)
    input_grad = turn((middle_grad + in_norm_grad).astype(low))

    own_rows = model_width // (2 * ctx_count)

    def pick(blocks, index):
        return lax.dynamic_index_in_dim(blocks, index, 1, False)

    def keep_part(blocks):
        sent = swap(pick(blocks, 1 - part).astype(low), "fsdp").astype(jnp.float32)
        return pick(blocks, part) + sent

    out_rows = turn(out_wgrad).reshape(1, 2, own_rows, model_width)
    d_out = keep_part(out_rows)[0]
    gain_rows = jnp.stack([query_gain_grad, key_gain_grad], axis=0).reshape(2, 2, own_rows)
    gain_rows = pick(gain_rows, part) + swap(pick(gain_rows, 1 - part), "fsdp")
    d_qgain, d_kgain = gain_rows[0], gain_rows[1]

    def by_owner(matrix):
        rows = turn(matrix, 0).reshape(ctx_count, 2, own_rows, -1)
        return rows

    wide = keep_part(by_owner(qkv_wgrad)).astype(low)
    received = exchange_all(wide[source_ids])
    back_ids = jnp.sum(
        to_source.astype(jnp.int32) * jnp.arange(ctx_count, dtype=jnp.int32)[None, :], axis=1
    )
    dense = received[back_ids].reshape(ctx_count, own_rows, 3, head_dim).astype(jnp.float32)
    d_query, d_key, d_value = (
        dense[:, :, i].transpose(1, 0, 2).reshape(own_rows, model_width) for i in range(3)
    )
    thin = jnp.concatenate(
        [router_wgrad, ffn_gain_grad[:, None], attn_gain_grad[:, None]], axis=1
    )
    thin_rows = by_owner(thin)
    thin_rows = pick(thin_rows, part) + swap(pick(thin_rows, 1 - part), "fsdp")
    thin_sum = jnp.sum(exchange_all(thin_rows[source_ids]), axis=0)
    d_router = thin_sum[:, :expert_count]
    d_ffn, d_attn = thin_sum[:, expert_count], thin_sum[:, expert_count + 1]
    return (
        layer_out[None],
        input_grad[None],
        d_attn,
        d_query,
        d_key,
        d_value,
        d_out,
        d_qgain,
        d_kgain,
        d_ffn,
        d_router,
        s_gate,
        s_up,
        s_down,
    )


def specs_of(ctx):
    rows, both = P("fsdp", ctx, None), ctx + ("fsdp",)
    dense = P("fsdp", None)
    ins = (
        rows,
        rows,
        P("fsdp"),
        dense,
        dense,
        dense,
        dense,
        P("fsdp"),
        P("fsdp"),
        P("fsdp"),
        dense,
        P(ctx, "fsdp", None),
        P(ctx, "fsdp", None),
        P(ctx, None, "fsdp"),
        rows,
        rows,
        P("fsdp", ctx),
    )
    line, matrix = P(both), P(both, None)
    outs = (
        rows,
        rows,
        line,
        matrix,
        matrix,
        matrix,
        matrix,
        line,
        line,
        line,
        matrix,
        P(ctx, "fsdp", None),
        P(ctx, "fsdp", None),
        P(ctx, None, "fsdp"),
    )
    return ins, outs


def solution(mesh):
    ctx_count, fsdp_count = mesh.shape["ctx"], mesh.shape["fsdp"]

    def whole(*arrays):
        heads = arrays[0].shape[2] // HEAD_DIM
        experts = arrays[10].shape[1]
        if ctx_count == heads == experts and fsdp_count == 2 and ctx_count % 4 == 0:
            chips = Mesh(mesh.devices.reshape(-1, 2, 2), ("chip", "core", "fsdp"))
            run, grid, ctx = body, chips, ("chip", "core")
        else:
            run, grid, ctx = general_body, mesh, ("ctx",)
        ins, outs = specs_of(ctx)
        return jax.shard_map(run, mesh=grid, in_specs=ins, out_specs=outs, check_vma=False)(*arrays)

    return whole
```

```python
import math

import jax
import jax.numpy as jnp
from jax import lax
from jax.experimental import pallas as pl
from jax.experimental.pallas import tpu as pltpu
from jax.sharding import Mesh
from jax.sharding import PartitionSpec as P

HEAD_DIM = 128
LEVELS = 4


epsilon = 1e-05
rope_base = 50000.0


def prefix(part, axis, combine, identity):
    place = lax.axis_index(axis)
    gathered = lax.all_gather(part, axis)
    state = jnp.zeros_like(part) + jnp.asarray(identity, part.dtype)

    def one(turn, state):
        return combine(state, lax.dynamic_index_in_dim(gathered, turn, 0, False))

    return lax.fori_loop(0, place, one, state)


def product(left, right):
    return jnp.dot(left, right, preferred_element_type=jnp.float32)


def precise(left, right):
    return jnp.dot(left, right, precision=lax.Precision.HIGHEST, preferred_element_type=jnp.float32)


def contract_rows(left, right):
    return lax.dot_general(
        left, right, (((0,), (0,)), ((), ())), preferred_element_type=jnp.float32
    )


def contract_cols(left, right):
    return lax.dot_general(
        left, right, (((1,), (1,)), ((), ())), preferred_element_type=jnp.float32
    )


def rms_forward(matrix, gain_row):
    inverse = lax.rsqrt(jnp.mean(matrix * matrix, axis=-1, keepdims=True) + epsilon)
    return (matrix * inverse * gain_row, inverse)


def rms_backward(matrix, inverse, gain_row, upstream):
    scaled = upstream * gain_row
    along = jnp.mean(scaled * matrix, axis=-1, keepdims=True)
    grad_rows = inverse * scaled - matrix * inverse * inverse * inverse * along
    grad_gain = jnp.sum(upstream * matrix * inverse, axis=0)
    return (grad_rows, grad_gain)


def rope_tables(position_ids, head_dim):
    half_dim = head_dim // 2
    inverse = rope_base ** (-(jnp.arange(half_dim, dtype=jnp.float32) * 2.0) / head_dim)
    angles = position_ids.astype(jnp.float32)[:, None] * inverse[None, :]
    return (jnp.cos(angles)[:, None, :], jnp.sin(angles)[:, None, :])


def rotate(matrix, cosine, sine_part, head_dim, turn_sign):
    count_rows = matrix.shape[0]
    by_head = matrix.reshape(count_rows, -1, head_dim)
    half_dim = head_dim // 2
    lower_half = by_head[..., :half_dim]
    upper_half = by_head[..., half_dim:]
    turned = jnp.concatenate(
        [
            lower_half * cosine - turn_sign * upper_half * sine_part,
            upper_half * cosine + turn_sign * lower_half * sine_part,
        ],
        axis=-1,
    )
    return turned.reshape(count_rows, -1)


def add_counts(earlier_part, later_part):
    return earlier_part + later_part


def score_block(query_part, key_part, score_scale):
    return (
        jnp.einsum("qhd,khd->hqk", query_part, key_part, preferred_element_type=jnp.float32)
        * score_scale
    )


def grad_block(query_part, dout_part, lse_part, delta_part, key_part, value_part, score_scale):
    probs = jnp.exp(score_block(query_part, key_part, score_scale) - lse_part)
    prob_low = probs.astype(jnp.bfloat16)
    dprob = jnp.einsum("qhd,khd->hqk", dout_part, value_part, preferred_element_type=jnp.float32)
    dscore = (probs * (dprob - delta_part)).astype(jnp.bfloat16)
    return (prob_low, dscore)


def general_body(
    tokens,
    cotangent,
    attn_gain,
    w_query,
    w_key,
    w_value,
    w_out,
    query_gain,
    key_gain,
    ffn_gain,
    router,
    w_gate,
    w_up,
    w_down,
    routes,
    priority,
    positions,
):
    ctx_count = lax.axis_size("ctx")
    (
        g_attn,
        q_weight,
        k_weight,
        v_weight,
        o_weight,
        g_query,
        g_key,
        g_ffn,
        r_weight,
        gate_full,
        up_full,
        down_full,
    ) = (
        lax.all_gather(attn_gain, "fsdp", axis=0, tiled=True),
        lax.all_gather(w_query, "fsdp", axis=0, tiled=True),
        lax.all_gather(w_key, "fsdp", axis=0, tiled=True),
        lax.all_gather(w_value, "fsdp", axis=0, tiled=True),
        lax.all_gather(w_out, "fsdp", axis=0, tiled=True),
        lax.all_gather(query_gain, "fsdp", axis=0, tiled=True),
        lax.all_gather(key_gain, "fsdp", axis=0, tiled=True),
        lax.all_gather(ffn_gain, "fsdp", axis=0, tiled=True),
        lax.all_gather(router, "fsdp", axis=0, tiled=True),
        lax.all_gather(w_gate, "fsdp", axis=1, tiled=True),
        lax.all_gather(w_up, "fsdp", axis=1, tiled=True),
        lax.all_gather(w_down, "fsdp", axis=2, tiled=True),
    )
    gate_weight = gate_full[0]
    up_weight = up_full[0]
    down_weight = down_full[0]
    tok_rows = tokens.shape[1]
    model_width = tokens.shape[2]
    head_dim = HEAD_DIM
    head_count = model_width // head_dim
    length = tok_rows * ctx_count
    top_k = routes.shape[2]
    capacity = 9 * tok_rows
    send_rows = 2 * tok_rows * top_k // ctx_count
    key_block = math.gcd(length, 1024)
    block_count = length // key_block
    score_scale = head_dim ** (-0.5)
    inputs = tokens[0].astype(jnp.float32)
    normed, inv_one = rms_forward(inputs, g_attn)
    h_one = normed.astype(jnp.bfloat16)
    q_lin = product(h_one, q_weight)
    k_lin = product(h_one, k_weight)
    v_lin = product(h_one, v_weight)
    cosine, sine_part = rope_tables(positions[0], head_dim)
    q_normed, inv_query = rms_forward(q_lin, g_query)
    k_normed, inv_key = rms_forward(k_lin, g_key)
    q_rot = rotate(q_normed, cosine, sine_part, head_dim, 1.0).astype(jnp.bfloat16)
    k_rot = rotate(k_normed, cosine, sine_part, head_dim, 1.0).astype(jnp.bfloat16)
    v_low = v_lin.astype(jnp.bfloat16)
    all_keys, all_values = (
        lax.all_gather(k_rot, "ctx", axis=0, tiled=True),
        lax.all_gather(v_low, "ctx", axis=0, tiled=True),
    )
    q_heads = q_rot.reshape(tok_rows, head_count, head_dim)

    def key_slice(block_id):
        start = block_id * key_block
        key_part = lax.dynamic_slice_in_dim(all_keys, start, key_block, 0).reshape(
            key_block, head_count, head_dim
        )
        value_part = lax.dynamic_slice_in_dim(all_values, start, key_block, 0).reshape(
            key_block, head_count, head_dim
        )
        return (key_part, value_part)

    def lse_step(carry, block_id):
        run_max, run_total = carry
        key_part, value_part = key_slice(block_id)
        scores = score_block(q_heads, key_part, score_scale)
        new_max = jnp.maximum(run_max, jnp.max(scores, axis=-1, keepdims=True))
        run_total = run_total * jnp.exp(run_max - new_max) + jnp.sum(
            jnp.exp(scores - new_max), axis=-1, keepdims=True
        )
        return ((new_max, run_total), None)

    start_max = jnp.full((head_count, tok_rows, 1), -jnp.inf, jnp.float32)
    start_total = jnp.zeros((head_count, tok_rows, 1), jnp.float32)
    (run_max, run_total), _ = lax.scan(lse_step, (start_max, start_total), jnp.arange(block_count))
    lse = run_max + jnp.log(run_total)

    def out_step(acc, block_id):
        key_part, value_part = key_slice(block_id)
        probs = jnp.exp(score_block(q_heads, key_part, score_scale) - lse).astype(jnp.bfloat16)
        return (
            acc + jnp.einsum("hqk,khd->qhd", probs, value_part, preferred_element_type=jnp.float32),
            None,
        )

    attended_heads, _ = lax.scan(
        out_step, jnp.zeros((tok_rows, head_count, head_dim), jnp.float32), jnp.arange(block_count)
    )
    attended = attended_heads.reshape(tok_rows, model_width)
    mixed_low = attended.astype(jnp.bfloat16)
    middle = inputs + product(mixed_low, o_weight)
    h_two_f, inv_two = rms_forward(middle, g_ffn)
    h_two = h_two_f.astype(jnp.bfloat16)
    logits = product(h_two, r_weight)
    row_max = jnp.max(logits, axis=-1, keepdims=True)
    exps_raw = jnp.exp(logits - row_max)
    router_probs = exps_raw / jnp.sum(exps_raw, axis=-1, keepdims=True)
    route_ids = routes[0]
    level_ids = priority[0]
    pair_code = level_ids * ctx_count + route_ids
    code_table = (
        pair_code[:, :, None] == jnp.arange(LEVELS * ctx_count, dtype=jnp.int32)[None, None, :]
    ).astype(jnp.float32)
    per_token = jnp.sum(code_table, axis=1)
    before_local = jnp.cumsum(per_token, axis=0) - per_token
    local_total = jnp.sum(per_token, axis=0)
    earlier = prefix(local_total, "ctx", add_counts, jnp.zeros_like(local_total))
    totals = lax.psum(local_total, "ctx")
    level_totals = totals.reshape(LEVELS, ctx_count)
    level_base = (jnp.cumsum(level_totals, axis=0) - level_totals).reshape(-1)
    offsets = before_local + (earlier + level_base)[None, :]
    pair_rank = jnp.sum(code_table * offsets[:, None, :], axis=-1).astype(jnp.int32)
    is_kept = pair_rank < capacity
    expert_hot = (
        route_ids[:, :, None] == jnp.arange(ctx_count, dtype=jnp.int32)[None, None, :]
    ).astype(jnp.float32)
    per_expert = jnp.sum(expert_hot, axis=1)
    local_before = jnp.cumsum(per_expert, axis=0) - per_expert
    local_slot = jnp.sum(expert_hot * local_before[:, None, :], axis=-1).astype(jnp.int32)
    send_index = (route_ids * send_rows + local_slot).reshape(-1)
    pair_count = tok_rows * top_k
    pair_of_slot = (
        jnp.full((ctx_count * send_rows,), pair_count, jnp.int32)
        .at[send_index]
        .set(jnp.arange(pair_count, dtype=jnp.int32))
    )
    slot_target = jnp.where(is_kept, pair_rank, capacity).reshape(-1)
    target_pad = jnp.concatenate([slot_target, jnp.full((1,), capacity, jnp.int32)], axis=0)
    send_slots = target_pad[pair_of_slot].reshape(ctx_count, send_rows)
    h_pad = jnp.concatenate([h_two, jnp.zeros((1, model_width), jnp.bfloat16)], axis=0)
    send_tokens = h_pad[pair_of_slot // top_k].reshape(ctx_count, send_rows, model_width)
    got_tokens, got_slots = (
        lax.all_to_all(send_tokens, "ctx", split_axis=0, concat_axis=0, tiled=True),
        lax.all_to_all(send_slots, "ctx", split_axis=0, concat_axis=0, tiled=True),
    )
    received_count = ctx_count * send_rows
    slots_flat = got_slots.reshape(-1)
    row_of_slot = (
        jnp.full((capacity,), received_count, jnp.int32)
        .at[slots_flat]
        .set(jnp.arange(received_count, dtype=jnp.int32), mode="drop")
    )
    got_pad = jnp.concatenate(
        [
            got_tokens.reshape(received_count, model_width),
            jnp.zeros((1, model_width), jnp.bfloat16),
        ],
        axis=0,
    )
    expert_in = got_pad[row_of_slot]
    gate_lin = product(expert_in, gate_weight)
    up_lin = product(expert_in, up_weight)
    sig_gate = jax.nn.sigmoid(gate_lin)
    silu_val = gate_lin * sig_gate
    swiglu = (silu_val * up_lin).astype(jnp.bfloat16)
    expert_out = product(swiglu, down_weight).astype(jnp.bfloat16)
    out_pad = jnp.concatenate([expert_out, jnp.zeros((1, model_width), jnp.bfloat16)], axis=0)
    back_rows = out_pad[slots_flat].reshape(ctx_count, send_rows, model_width)
    returned = lax.all_to_all(back_rows, "ctx", split_axis=0, concat_axis=0, tiled=True)
    returned_pad = jnp.concatenate(
        [
            returned.reshape(ctx_count * send_rows, model_width),
            jnp.zeros((1, model_width), jnp.bfloat16),
        ],
        axis=0,
    )
    pair_out = returned_pad[send_index].reshape(tok_rows, top_k, model_width)
    chosen = jnp.sum(router_probs[:, None, :] * expert_hot, axis=-1)
    share = jnp.where(is_kept, chosen, 0.0)
    mixture = jnp.einsum("tk,tkd->td", share, pair_out, preferred_element_type=jnp.float32)
    final_rows = middle + mixture
    layer_out = final_rows.astype(jnp.bfloat16)
    grad_out = cotangent[0].astype(jnp.float32)
    routed_grad = (share[:, :, None] * grad_out[:, None, :]).astype(jnp.bfloat16)
    share_grad = jnp.where(
        is_kept,
        jnp.einsum("tkd,td->tk", pair_out, grad_out, preferred_element_type=jnp.float32),
        0.0,
    )
    prob_grad = jnp.sum(expert_hot * share_grad[:, :, None], axis=1)
    logit_grad = router_probs * (
        prob_grad - jnp.sum(router_probs * prob_grad, axis=-1, keepdims=True)
    )
    routed_pad = jnp.concatenate(
        [routed_grad.reshape(pair_count, model_width), jnp.zeros((1, model_width), jnp.bfloat16)],
        axis=0,
    )
    send_grads = routed_pad[pair_of_slot].reshape(ctx_count, send_rows, model_width)
    got_grads = lax.all_to_all(send_grads, "ctx", split_axis=0, concat_axis=0, tiled=True)
    grad_pad = jnp.concatenate(
        [got_grads.reshape(received_count, model_width), jnp.zeros((1, model_width), jnp.bfloat16)],
        axis=0,
    )
    out_grad = grad_pad[row_of_slot]
    act_grad = contract_cols(out_grad, down_weight)
    down_wgrad = contract_rows(swiglu, out_grad)
    gate_grad = (act_grad * up_lin * sig_gate * (1.0 + gate_lin * (1.0 - sig_gate))).astype(
        jnp.bfloat16
    )
    up_grad = (act_grad * silu_val).astype(jnp.bfloat16)
    in_grad = (contract_cols(gate_grad, gate_weight) + contract_cols(up_grad, up_weight)).astype(
        jnp.bfloat16
    )
    gate_wgrad = contract_rows(expert_in, gate_grad)
    up_wgrad = contract_rows(expert_in, up_grad)
    in_pad = jnp.concatenate([in_grad, jnp.zeros((1, model_width), jnp.bfloat16)], axis=0)
    back_grads = in_pad[slots_flat].reshape(ctx_count, send_rows, model_width)
    pair_grads = lax.all_to_all(back_grads, "ctx", split_axis=0, concat_axis=0, tiled=True)
    pair_pad = jnp.concatenate(
        [
            pair_grads.reshape(ctx_count * send_rows, model_width),
            jnp.zeros((1, model_width), jnp.bfloat16),
        ],
        axis=0,
    )
    token_pair = pair_pad[send_index].reshape(tok_rows, top_k, model_width)
    hidden_grad = jnp.sum(token_pair.astype(jnp.float32), axis=1) + precise(
        logit_grad, r_weight.astype(jnp.float32).T
    )
    router_wgrad = precise(h_two.astype(jnp.float32).T, logit_grad)
    norm_grad, ffn_gain_grad = rms_backward(middle, inv_two, g_ffn, hidden_grad)
    middle_grad = grad_out + norm_grad
    branch_grad = middle_grad.astype(jnp.bfloat16)
    out_wgrad = contract_rows(mixed_low, branch_grad)
    mixed_grad = contract_cols(branch_grad, o_weight).astype(jnp.bfloat16)
    dout_heads = mixed_grad.reshape(tok_rows, head_count, head_dim)
    delta = jnp.sum(dout_heads.astype(jnp.float32) * attended_heads, axis=-1).T[:, :, None]

    def back_step(dq_acc, block_id):
        key_part, value_part = key_slice(block_id)
        prob_low, dscore = grad_block(
            q_heads, dout_heads, lse, delta, key_part, value_part, score_scale
        )
        dq_acc = dq_acc + jnp.einsum(
            "hqk,khd->qhd", dscore, key_part, preferred_element_type=jnp.float32
        )
        dk_part = jnp.einsum(
            "hqk,qhd->khd", dscore, q_heads, preferred_element_type=jnp.float32
        ).reshape(key_block, model_width)
        dv_part = jnp.einsum(
            "hqk,qhd->khd", prob_low, dout_heads, preferred_element_type=jnp.float32
        ).reshape(key_block, model_width)
        return (dq_acc, jnp.concatenate([dk_part, dv_part], axis=1))

    dq_heads, kv_terms = lax.scan(
        back_step, jnp.zeros((tok_rows, head_count, head_dim), jnp.float32), jnp.arange(block_count)
    )
    kv_mine = lax.psum_scatter(
        kv_terms.reshape(length, 2 * model_width), "ctx", scatter_dimension=0, tiled=True
    )
    key_grad = kv_mine[:, :model_width] * score_scale
    value_grad = kv_mine[:, model_width:]
    v_lin_low = value_grad.astype(jnp.bfloat16)
    q_grad = dq_heads.reshape(tok_rows, model_width) * score_scale
    q_back = rotate(q_grad, cosine, sine_part, head_dim, -1.0)
    k_back = rotate(key_grad, cosine, sine_part, head_dim, -1.0)
    q_lin_grad, query_gain_grad = rms_backward(q_lin, inv_query, g_query, q_back)
    k_lin_grad, key_gain_grad = rms_backward(k_lin, inv_key, g_key, k_back)
    q_lin_low = q_lin_grad.astype(jnp.bfloat16)
    k_lin_low = k_lin_grad.astype(jnp.bfloat16)
    h_grad = (
        contract_cols(q_lin_low, q_weight)
        + contract_cols(k_lin_low, k_weight)
        + contract_cols(v_lin_low, v_weight)
    )
    query_wgrad = contract_rows(h_one, q_lin_low)
    key_wgrad = contract_rows(h_one, k_lin_low)
    value_wgrad = contract_rows(h_one, v_lin_low)
    in_norm_grad, attn_gain_grad = rms_backward(inputs, inv_one, g_attn, h_grad)
    input_grad = (middle_grad + in_norm_grad).astype(jnp.bfloat16)
    s_gate, s_up, s_down = (
        lax.psum_scatter(
            gate_wgrad[None].astype(jnp.bfloat16), "fsdp", scatter_dimension=1, tiled=True
        ).astype(jnp.float32),
        lax.psum_scatter(
            up_wgrad[None].astype(jnp.bfloat16), "fsdp", scatter_dimension=1, tiled=True
        ).astype(jnp.float32),
        lax.psum_scatter(
            down_wgrad[None].astype(jnp.bfloat16), "fsdp", scatter_dimension=2, tiled=True
        ).astype(jnp.float32),
    )
    d_attn, d_query, d_key, d_value, d_out, d_qgain, d_kgain, d_ffn, d_router = (
        lax.psum_scatter(attn_gain_grad, ("ctx", "fsdp"), scatter_dimension=0, tiled=True),
        lax.psum_scatter(query_wgrad, ("ctx", "fsdp"), scatter_dimension=0, tiled=True),
        lax.psum_scatter(key_wgrad, ("ctx", "fsdp"), scatter_dimension=0, tiled=True),
        lax.psum_scatter(value_wgrad, ("ctx", "fsdp"), scatter_dimension=0, tiled=True),
        lax.psum_scatter(out_wgrad, ("ctx", "fsdp"), scatter_dimension=0, tiled=True),
        lax.psum_scatter(query_gain_grad, ("ctx", "fsdp"), scatter_dimension=0, tiled=True),
        lax.psum_scatter(key_gain_grad, ("ctx", "fsdp"), scatter_dimension=0, tiled=True),
        lax.psum_scatter(ffn_gain_grad, ("ctx", "fsdp"), scatter_dimension=0, tiled=True),
        lax.psum_scatter(router_wgrad, ("ctx", "fsdp"), scatter_dimension=0, tiled=True),
    )
    return (
        layer_out[None],
        input_grad[None],
        d_attn,
        d_query,
        d_key,
        d_value,
        d_out,
        d_qgain,
        d_kgain,
        d_ffn,
        d_router,
        s_gate,
        s_up,
        s_down,
    )


RING = [0, 2, 4, 6, 7, 5, 3, 1]
CHIPS = len(RING)
FAR = CHIPS // 2
EXTRA = 8
PLACES = [1, 7, 2, 6, 3, 5, 0, 4]
CHUNKS = {1: (0, 2), 2: (2, 2), 3: (4, 2), 0: (6, 1), FAR: (7, 1)}


def swap(array, axis):
    return lax.ppermute(array, axis, [(0, 1), (1, 0)])


def shift(array, by):
    pairs = [(RING[i], RING[(i + by) % CHIPS]) for i in range(CHIPS)]
    return lax.ppermute(array, "chip", pairs)


def fence(*groups):
    flat = lax.optimization_barrier(tuple(array for group in groups for array in group))
    out, at = [], 0
    for group in groups:
        out.append(list(flat[at : at + len(group)]))
        at += len(group)
    return out


def open_jobs(carried, jobs):
    opened = fence(carried, *[list(inputs) for inputs, _ in jobs])
    return opened[0], [(ins, function) for ins, (_, function) in zip(opened[1:], jobs)]


def run_jobs(jobs):
    return [list(function(*inputs)) for inputs, function in jobs]


def ring_gather(arrays, job, jobs=None):
    cut = arrays[0].shape[0] // 2 // 8 * 8
    ahead, behind = list(arrays), list(arrays)
    fresh = [[array] for array in arrays]
    results = {}
    for step in range(1, FAR + 1):
        if step == FAR:
            ahead, behind = [a[:cut] for a in ahead], [b[cut:] for b in behind]
        ahead, behind, *fresh = fence(ahead, behind, *fresh)
        ahead, opened = open_jobs(ahead, (jobs or {}).get(step, []))
        ahead, behind = [shift(a, 1) for a in ahead], [shift(b, -1) for b in behind]
        blocks = [[x for block in group for x in (block, swap(block, "core"))] for group in fresh]
        made, keep = job(step - 1, blocks)
        done = run_jobs(opened)
        ahead, behind, made, *done = fence(ahead, behind, list(made), *done)
        keep(made)
        results[step] = done
        fresh = [[b, a] for a, b in zip(ahead, behind)]
    last = [jnp.concatenate([a, b], axis=0) for a, b in zip(ahead, behind)]
    made, keep = job(FAR, [[block, swap(block, "core")] for block in last])
    keep(list(made))
    return results


class Scatter:
    def __init__(self, make, inputs=()):
        self.make, self.inputs = make, list(inputs)
        self.step = 0
        self.extras = {}
        (mine, other), self.extras[FAR] = make(FAR, *self.inputs)
        first = (mine.astype(jnp.float32) + swap(other, "core").astype(jnp.float32)).astype(
            jnp.bfloat16
        )
        self.cut = first.shape[0] // 2 // 8 * 8
        self.carried = [first[: self.cut], first[self.cut :]]

    def job(self):
        near = FAR - self.step - 1

        def function(ahead, behind, *inputs):
            ahead, behind = shift(ahead, 1), shift(behind, -1)
            terms, extras = self.make(near, *inputs)
            terms = [t if i % 2 == 0 else swap(t, "core") for i, t in enumerate(terms)]
            return [ahead, behind, *terms, *extras]

        return self.carried + self.inputs, function

    def take(self, results):
        self.step += 1
        near = FAR - self.step
        ahead, behind, *terms = results
        count = 4 if near else 2
        terms, self.extras[near] = terms[:count], terms[count:]
        terms = [t.astype(jnp.float32) for t in terms]
        ahead, behind = ahead.astype(jnp.float32), behind.astype(jnp.float32)
        if near == 0:
            self.total = terms[0] + terms[1] + ahead + behind
            return
        if self.step == 1:
            ahead = jnp.concatenate([ahead, jnp.zeros_like(behind)], axis=0)
            behind = jnp.concatenate([jnp.zeros_like(ahead[: self.cut]), behind], axis=0)
        self.carried = [
            (terms[0] + terms[1] + ahead).astype(jnp.bfloat16),
            (terms[2] + terms[3] + behind).astype(jnp.bfloat16),
        ]


def window(scatters, jobs):
    every = [scatter.job() for scatter in scatters] + list(jobs)
    _, opened = open_jobs([], every)
    results = fence(*run_jobs(opened))
    for scatter, result in zip(scatters, results):
        scatter.take(result)
    return results[len(scatters) :]


def exchange_all(parts):
    pair = jnp.stack([parts[:, 0], swap(parts[:, 1], "core")], axis=1)
    got = {0: pair[0]}
    for at in range(1, CHIPS):
        got[CHIPS - at] = shift(pair[at], at)
    return jnp.stack([got[at] for at in range(CHIPS)], axis=0)


def sum_all(values, jobs):
    (values,), jobs = open_jobs([values], jobs)
    both = values + swap(values[:, :, ::-1], "core")
    moved = [shift(both, at) for at in range(1, CHIPS)]
    done = run_jobs(jobs)
    moved, *done = fence(moved, *done)
    total = both
    for at in range(1, CHIPS):
        total = total + jnp.roll(moved[at - 1], -at, axis=1)
    return total, done


def by_place(values, axis):
    return jnp.stack(
        [lax.index_in_dim(values, PLACES.index(at), axis, False) for at in range(CHIPS)], axis
    )


def by_chunk(values, axis):
    return jnp.stack([lax.index_in_dim(values, at, axis, False) for at in PLACES], axis)


def call(kernel, name, inputs, ins, outs, shapes, earlier=(), grid=(1,), scratch=(), cost=None, mib=56):
    return pl.pallas_call(
        kernel,
        grid=grid,
        in_specs=ins + [pl.BlockSpec(memory_space=pl.ANY)] * len(earlier),
        out_specs=outs,
        out_shape=shapes,
        scratch_shapes=list(scratch),
        input_output_aliases={len(ins) + i: i for i in range(len(earlier))},
        compiler_params=pltpu.CompilerParams(vmem_limit_bytes=mib << 20),
        cost_estimate=pl.CostEstimate(flops=cost[0], bytes_accessed=cost[1], transcendentals=cost[2]),
        name=name,
    )(*inputs, *earlier)


def whole(array):
    return pl.BlockSpec(array.shape, lambda i: (0,) * len(array.shape))


def once(array):
    return pl.BlockSpec(
        array.shape, lambda i: (0,) * len(array.shape), pipeline_mode=pl.Buffered(1)
    )


def rows_of(step, tok_rows, cols):
    first, count = CHUNKS[step]
    index = first // count
    return pl.BlockSpec((2 * count * tok_rows, cols), lambda i: (index, 0))


def lin_chunk(step, blocks, weight, place, tok_rows, earlier):
    count, width, cols = len(blocks), weight.shape[0], weight.shape[1]
    length = 2 * CHIPS * tok_rows
    rows, head = count * tok_rows, weight.shape[1] // 3

    def kernel(*refs):
        block_refs, weight_ref, place_ref = refs[:count], refs[count], refs[count + 1]
        lin_ref, all_ref, sum_ref, tag_ref = refs[-4:]
        lanes = pl.ds(pl.multiple_of(place_ref[0] * tok_rows, tok_rows), tok_rows)
        for i in range(count):
            all_ref[i * tok_rows : (i + 1) * tok_rows] = block_refs[i][:tok_rows]
            levels = block_refs[i][tok_rows:, lanes].astype(jnp.float32)
            others = block_refs[i][tok_rows:, : 3 * tok_rows].astype(jnp.float32)
            tag_ref[i * EXTRA : (i + 1) * EXTRA] = jnp.concatenate(
                [levels[:1]]
                + [others[1:2, k * tok_rows : (k + 1) * tok_rows] for k in range(3)]
                + [jnp.zeros((EXTRA - 4, tok_rows), jnp.float32)],
                axis=0,
            )
        lin = product(all_ref[...], weight_ref[...])
        lin_ref[...] = lin
        line = lax.broadcasted_iota(jnp.int32, (8, head), 0)
        total = jnp.zeros((8, rows), jnp.float32)
        for k in range(2):
            part = lin[:, k * head : (k + 1) * head]
            total = total + lax.dot_general(
                (line == k).astype(jnp.float32),
                part * part,
                (((1,), (1,)), ((), ())),
                precision=lax.Precision.HIGHEST,
                preferred_element_type=jnp.float32,
            )
        sum_ref[...] = total

    tags = jax.ShapeDtypeStruct((count * EXTRA, tok_rows), jnp.float32)
    sums = jax.ShapeDtypeStruct((8, rows), jnp.float32)
    return call(
        kernel,
        "lin",
        [*blocks, weight, place],
        [whole(b) for b in blocks] + [whole(weight), pl.BlockSpec(memory_space=pltpu.SMEM)],
        [rows_of(step, tok_rows, cols), rows_of(step, tok_rows, width), whole(sums), whole(tags)],
        [
            jax.ShapeDtypeStruct((length, cols), jnp.float32),
            jax.ShapeDtypeStruct((length, width), jnp.bfloat16),
            sums,
            tags,
        ],
        earlier,
        cost=(2 * rows * width * cols, 4 * rows * width + 2 * weight.size, 0),
    )


def attend_chunk(step, queries, keys, values, weight, tok_rows, score_scale):
    count = 2 * CHUNKS[step][1]
    head, width, length = keys.shape[1], weight.shape[1], keys.shape[0]

    def kernel(q_ref, k_ref, v_ref, w_ref, out_ref, lse_ref, *parts):
        for i in range(0, count, 2):
            span = pl.ds(i * tok_rows, 2 * tok_rows)
            scores = contract_cols(q_ref[span], k_ref[...]) * score_scale
            row_max = jnp.max(scores, axis=-1, keepdims=True)
            raw = jnp.exp(scores - row_max)
            total = jnp.sum(raw, axis=-1, keepdims=True)
            probs = (raw / total).astype(jnp.bfloat16)
            mixed = product(probs, v_ref[...]).astype(jnp.bfloat16)
            out_ref[span] = mixed
            lse_ref[span] = row_max + jnp.log(total)
            term = product(mixed, w_ref[...]).astype(jnp.bfloat16)
            parts[i][...] = term[:tok_rows]
            parts[i + 1][...] = term[tok_rows:]

    rows = count * tok_rows
    shapes = [
        jax.ShapeDtypeStruct((rows, head), jnp.bfloat16),
        jax.ShapeDtypeStruct((rows, 1), jnp.float32),
    ] + [jax.ShapeDtypeStruct((tok_rows, width), jnp.bfloat16)] * count
    return call(
        kernel,
        "attend",
        [queries, keys, values, weight],
        [rows_of(step, tok_rows, head), whole(keys), whole(values), whole(weight)],
        [whole(shape) for shape in shapes],
        shapes,
        cost=(
            4 * rows * length * head + 2 * rows * head * width,
            4 * length * head + 2 * rows * width,
            rows * length,
        ),
    )


def attend_back_chunk(
    step, blocks, queries, lse, keys, values, weight, tok_rows, score_scale, earlier
):
    count = len(blocks)
    length, head = keys.shape
    width = weight.shape[1]
    rows = count * tok_rows

    def kernel(*refs):
        block_refs = refs[:count]
        q_ref, lse_ref, k_ref, v_ref, w_ref = refs[count : count + 5]
        dq_ref, all_ref, dk_ref, dv_ref = refs[-4:]
        for i in range(count):
            all_ref[i * tok_rows : (i + 1) * tok_rows] = block_refs[i][...]
        if earlier:
            dk_in, dv_in = refs[count + 5 : count + 7]
            dk, dv = dk_in[...], dv_in[...]
        else:
            dk, dv = 0.0, 0.0
        for i in range(0, count, 2):
            span = pl.ds(i * tok_rows, 2 * tok_rows)
            queries = q_ref[span]
            douts = contract_cols(all_ref[span], w_ref[...]).astype(jnp.bfloat16)
            probs = jnp.exp(contract_cols(queries, k_ref[...]) * score_scale - lse_ref[span])
            dprobs = contract_cols(douts, v_ref[...])
            delta = jnp.sum(probs * dprobs, axis=-1, keepdims=True)
            dscores = (probs * (dprobs - delta)).astype(jnp.bfloat16)
            dq_ref[span] = product(dscores, k_ref[...]) * score_scale
            dk = dk + contract_rows(dscores, queries) * score_scale
            dv = dv + contract_rows(probs.astype(jnp.bfloat16), douts)
        dk_ref[...] = dk
        dv_ref[...] = dv

    total = jax.ShapeDtypeStruct((length, head), jnp.float32)
    inputs = [*blocks, queries, lse, keys, values, weight]
    ins = [whole(b) for b in blocks] + [
        rows_of(step, tok_rows, head),
        rows_of(step, tok_rows, 1),
        whole(keys),
        whole(values),
        whole(weight),
    ]
    sums = list(earlier[2:])
    return pl.pallas_call(
        kernel,
        grid=(1,),
        in_specs=ins
        + [whole(s) for s in sums]
        + [pl.BlockSpec(memory_space=pl.ANY)] * len(earlier[:2]),
        out_specs=[
            rows_of(step, tok_rows, head),
            rows_of(step, tok_rows, width),
            whole(total),
            whole(total),
        ],
        out_shape=[
            total,
            jax.ShapeDtypeStruct((length, width), jnp.bfloat16),
            total,
            total,
        ],
        input_output_aliases={
            len(ins): 2,
            len(ins) + 1: 3,
            len(ins) + 2: 0,
            len(ins) + 3: 1,
        }
        if earlier
        else {},
        compiler_params=pltpu.CompilerParams(vmem_limit_bytes=56 << 20),
        cost_estimate=pl.CostEstimate(
            flops=10 * rows * length * head + 2 * rows * head * width,
            bytes_accessed=16 * length * head + 4 * rows * width,
            transcendentals=rows * length,
        ),
        name="attend_back",
    )(*inputs, *sums, *earlier[:2])


EXPERT_COLS = 256


def expert_chunk(step, h_blocks, g_blocks, place, kept, router, gate, up, down, tok_rows, earlier):
    count = len(h_blocks)
    width, hidden = gate.shape
    cols = EXPERT_COLS
    rows = count * tok_rows
    length = 2 * CHIPS * tok_rows
    low = jnp.bfloat16
    first, places = CHUNKS[step]
    index = first // places

    def kernel(*refs):
        h_refs, g_refs = refs[:count], refs[count : 2 * count]
        place_ref, kept_ref, router_ref, gate_ref, up_ref, down_ref = refs[
            2 * count : 2 * count + 6
        ]
        outs = refs[-(2 * count + 9) : -4]
        act_ref, dgate_ref, dup_ref, h_all, g_all = outs[:5]
        mix_refs, dx_refs = outs[5 : 5 + count], outs[5 + count :]
        mix_sum, dx_sum, share_ref, dshare_ref = refs[-4:]
        turn = pl.program_id(0)
        last = pl.num_programs(0) - 1

        @pl.when(turn == 0)
        def _():
            for i in range(count):
                h_all[i * tok_rows : (i + 1) * tok_rows] = h_refs[i][...]
                g_all[i * tok_rows : (i + 1) * tok_rows] = g_refs[i][...]
            logits = contract_cols(h_all[...], router_ref[...])
            raw = jnp.exp(logits - jnp.max(logits, axis=-1, keepdims=True))
            probs = raw / jnp.sum(raw, axis=-1, keepdims=True)
            lanes = lax.broadcasted_iota(jnp.int32, probs.shape, 1)
            chosen = jnp.sum(
                jnp.where(lanes == place_ref[0], probs, 0.0), axis=-1, keepdims=True
            )
            share_ref[...] = chosen * kept_ref[...]

        hidden_rows, grads, share = h_all[...], g_all[...], share_ref[...]
        gate_lin = product(hidden_rows, gate_ref[...])
        up_lin = product(hidden_rows, up_ref[...])
        back = contract_cols(grads, down_ref[...])
        sig = jax.nn.sigmoid(gate_lin)
        silu = gate_lin * sig
        act = silu * up_lin
        dshare = jnp.sum(act * back, axis=-1, keepdims=True)
        act_low = (act * share).astype(low)
        back = back * share
        dgate = (back * up_lin * (sig * (1.0 + gate_lin * (1.0 - sig)))).astype(low)
        dup = (back * silu).astype(low)
        act_ref[...] = act_low
        dgate_ref[...] = dgate
        dup_ref[...] = dup
        mix = product(act_low, down_ref[...])
        dx = contract_cols(dgate, gate_ref[...]) + contract_cols(dup, up_ref[...])

        @pl.when(turn == 0)
        def _():
            dshare_ref[...] = dshare
            mix_sum[...] = mix
            dx_sum[...] = dx

        @pl.when((turn > 0) & (turn < last))
        def _():
            dshare_ref[...] += dshare
            mix_sum[...] += mix
            dx_sum[...] += dx

        @pl.when(turn == last)
        def _():
            mix_low = (mix_sum[...] + mix).astype(low)
            dx_low = (dx_sum[...] + dx).astype(low)
            total = (dshare_ref[...] + dshare) * kept_ref[...]
            same = lax.broadcasted_iota(jnp.int32, (tok_rows, tok_rows), 0) == (
                lax.broadcasted_iota(jnp.int32, (tok_rows, tok_rows), 1)
            )
            lanes = pl.ds(pl.multiple_of(place_ref[0] * tok_rows, tok_rows), tok_rows)
            for i in range(count):
                span = slice(i * tok_rows, (i + 1) * tok_rows)
                mix_refs[i][...] = mix_low[span]
                dx_refs[i][:tok_rows] = dx_low[span]
                line = jnp.sum(jnp.where(same, total[span], 0.0), axis=0, keepdims=True)
                pieces, rest = [], line
                for _ in range(3):
                    piece = rest.astype(low)
                    rest = rest - piece.astype(jnp.float32)
                    pieces.append(piece.astype(jnp.float32))
                pieces.append(jnp.zeros((EXTRA - 3, tok_rows), jnp.float32))
                dx_refs[i][tok_rows:] = jnp.zeros((EXTRA, width), low)
                dx_refs[i][tok_rows:, lanes] = jnp.concatenate(pieces, axis=0).astype(low)

    tile = pl.BlockSpec((rows, cols), lambda j: (index, j))
    all_rows = pl.BlockSpec((rows, width), lambda j: (index, 0))
    wide = jax.ShapeDtypeStruct((length, hidden), low)
    full = jax.ShapeDtypeStruct((length, width), low)
    block = jax.ShapeDtypeStruct((tok_rows, width), low)
    longer = jax.ShapeDtypeStruct((tok_rows + EXTRA, width), low)
    return call(
        kernel,
        "expert",
        [*h_blocks, *g_blocks, place, kept, router, gate, up, down],
        [once(b) for b in [*h_blocks, *g_blocks]]
        + [
            pl.BlockSpec(memory_space=pltpu.SMEM),
            pl.BlockSpec((rows, 1), lambda j: (index, 0)),
            whole(router),
            pl.BlockSpec((width, cols), lambda j: (0, j)),
            pl.BlockSpec((width, cols), lambda j: (0, j)),
            pl.BlockSpec((cols, width), lambda j: (j, 0)),
        ],
        [tile] * 3 + [all_rows] * 2 + [whole(block)] * count + [whole(longer)] * count,
        [wide] * 3 + [full] * 2 + [block] * count + [longer] * count,
        earlier,
        grid=(hidden // cols,),
        scratch=[pltpu.VMEM((rows, width), jnp.float32)] * 2
        + [pltpu.VMEM((rows, 1), jnp.float32)] * 2,
        cost=(
            12 * rows * width * hidden,
            6 * width * hidden + 12 * rows * width,
            2 * rows * hidden,
        ),
        mib=60,
    )


def body(
    tokens,
    cotangent,
    attn_gain,
    w_query,
    w_key,
    w_value,
    w_out,
    query_gain,
    key_gain,
    ffn_gain,
    router,
    w_gate,
    w_up,
    w_down,
    routes,
    priority,
    positions,
):
    low = jnp.bfloat16
    ctx_count = 2 * CHIPS
    place = lax.axis_index("chip") * 2 + lax.axis_index("core")
    part = lax.axis_index("fsdp")
    tok_rows, model_width = tokens.shape[1:]
    half_width = model_width // 2
    head_dim = HEAD_DIM
    length = tok_rows * ctx_count
    capacity = 9 * tok_rows
    score_scale = head_dim ** (-0.5)
    per_half = ctx_count // 2
    expert_count = router.shape[1]

    def joined(mine, other, axis):
        return jnp.where(
            part == 0,
            jnp.concatenate([mine, other], axis=axis),
            jnp.concatenate([other, mine], axis=axis),
        )

    def head_rows(matrix, width):
        return lax.dynamic_slice_in_dim(matrix, (place % per_half) * width, width, 0)

    small = jnp.concatenate(
        [
            router.T,
            attn_gain[None],
            ffn_gain[None],
            jnp.concatenate(
                [
                    head_rows(query_gain, head_dim),
                    head_rows(key_gain, head_dim),
                    jnp.zeros((half_width - 2 * head_dim,), low),
                ]
            )[None],
        ],
        axis=0,
    )
    small_other = swap(small, "fsdp")
    small_full = joined(small, small_other, 1)
    r_weight = small_full[:expert_count]
    g_attn = small_full[expert_count].astype(jnp.float32)
    g_ffn = small_full[expert_count + 1].astype(jnp.float32)
    here = part == place // per_half
    g_heads = jnp.where(here, small[expert_count + 2], small_other[expert_count + 2]).astype(
        jnp.float32
    )
    g_query, g_key = g_heads[:head_dim], g_heads[head_dim : 2 * head_dim]
    qkv_mine = jnp.concatenate(
        [
            lax.dynamic_slice_in_dim(w, place * head_dim, head_dim, 1)
            for w in (w_query, w_key, w_value)
        ],
        axis=1,
    )
    qkv_other = swap(qkv_mine, "fsdp")
    qkv_weight = joined(qkv_mine, qkv_other, 0)
    out_mine = head_rows(w_out, head_dim)
    out_weight = jnp.where(here, out_mine, swap(out_mine, "fsdp"))
    gate_weight = lax.all_gather(w_gate[0], "fsdp", axis=0, tiled=True)
    up_weight = lax.all_gather(w_up[0], "fsdp", axis=0, tiled=True)
    down_weight = lax.all_gather(w_down[0], "fsdp", axis=1, tiled=True)

    hot = routes[0][:, :, None] == jnp.arange(expert_count, dtype=jnp.int32)[None, None, :]
    levels = jnp.sum(jnp.where(hot, priority[0][:, :, None] - LEVELS, 0), axis=1) + LEVELS
    spot = positions[0]
    line = jnp.concatenate(
        [spot // 128, spot % 128, jnp.full((model_width - 2 * tok_rows,), place, jnp.int32)]
    )
    tags = jnp.concatenate(
        [
            levels.T.reshape(1, model_width),
            line[None],
            jnp.zeros((EXTRA - 2, model_width), jnp.int32),
        ],
        axis=0,
    ).astype(low)

    inputs = tokens[0].astype(jnp.float32)
    normed, inv_one = rms_forward(inputs, g_attn)
    place_one = place.astype(jnp.int32).reshape(1)
    ready = ()
    sum_parts, tag_parts, rope_parts = {}, {}, {}

    def lin_job(step, blocks):
        made = lin_chunk(step, blocks[0], qkv_weight, place_one, tok_rows, ready)
        lines = made[3].reshape(-1, EXTRA, tok_rows)
        spots = (lines[:, 1] * 128.0 + lines[:, 2]).reshape(-1)
        cosine, sine_part = rope_tables(spots, head_dim)
        cosine, sine_part = cosine[:, 0], sine_part[:, 0]
        tables = [
            jnp.concatenate([cosine, cosine], axis=-1),
            jnp.concatenate([-sine_part, sine_part], axis=-1),
        ]

        def keep(made):
            nonlocal ready
            ready = tuple(made[:2])
            sum_parts[step], tag_parts[step] = made[2][:2], made[3]
            rope_parts[step] = made[4:]

        return [*made, *tables], keep

    ring_gather([jnp.concatenate([normed.astype(low), tags], axis=0)], lin_job)
    lin, all_h_one = ready
    q_lin, k_lin, v_lin = jnp.split(lin, 3, axis=1)
    cos_full, sin_full = (
        jnp.concatenate([rope_parts[step][k] for step in CHUNKS], axis=0) for k in range(2)
    )
    all_tags = jnp.concatenate([tag_parts[step] for step in CHUNKS], axis=0).reshape(
        ctx_count, EXTRA, tok_rows
    )

    def token_sums(lines, jobs):
        total, done = sum_all(by_place(lines.reshape(-1, CHIPS, 2, tok_rows), 1), jobs)
        return by_chunk(total, 1).reshape(-1, length, 1) / model_width, done

    def rank_job(all_tags):
        mine, owner = all_tags[:, 0], all_tags[:, 3, :1]
        order = owner * tok_rows + jnp.arange(tok_rows, dtype=jnp.float32)[None]
        mine = mine.reshape(length)
        code = mine * length + order.reshape(length)
        ranks = jnp.sum((code[None, :] < code[:, None]).astype(jnp.float32), axis=1)
        kept = (mine < LEVELS) & (ranks < capacity)
        return kept.astype(jnp.float32)[:, None], owner[:, 0].astype(jnp.int32)

    square, _ = token_sums(
        jnp.concatenate([sum_parts[step] for step in CHUNKS], axis=1),
        [],
    )
    inv_query, inv_key = lax.rsqrt(square[0] + epsilon), lax.rsqrt(square[1] + epsilon)

    def spin(matrix):
        return jnp.concatenate([matrix[:, head_dim // 2 :], matrix[:, : head_dim // 2]], axis=-1)

    q_normed = q_lin * inv_query * g_query
    k_normed = k_lin * inv_key * g_key
    q_rot = (q_normed * cos_full + spin(q_normed) * sin_full).astype(low)
    k_rot = (k_normed * cos_full + spin(k_normed) * sin_full).astype(low)
    v_low = v_lin.astype(low)

    def attend_terms(step, queries, keys, values):
        mixed, lse, *terms = attend_chunk(
            step, queries, keys, values, out_weight, tok_rows, score_scale
        )
        return terms, [mixed, lse]

    out_sum = Scatter(attend_terms, [q_rot, k_rot, v_low])
    ((kept, owners),) = window([out_sum], [([all_tags], rank_job)])
    for _ in range(FAR - 1):
        window([out_sum], [])
    mixed_low, lse = (
        jnp.concatenate([out_sum.extras[step][k] for step in CHUNKS], axis=0) for k in range(2)
    )
    projected = out_sum.total
    middle = inputs + projected

    h_two_f, inv_two = rms_forward(middle, g_ffn)
    h_two = h_two_f.astype(low)
    grad_out = cotangent[0].astype(jnp.float32)
    filled = ()
    mix_terms, dx_terms = {}, {}

    def expert_job(step, blocks):
        made = expert_chunk(
            step,
            blocks[0],
            blocks[1],
            place_one,
            kept,
            r_weight,
            gate_weight,
            up_weight,
            down_weight,
            tok_rows,
            filled,
        )

        def keep(made):
            nonlocal filled
            filled, terms = tuple(made[:5]), made[5:]
            half = len(terms) // 2
            mix_terms[step], dx_terms[step] = terms[:half], terms[half:]

        return made, keep

    ring_gather([h_two, cotangent[0]], expert_job)
    act_low, gate_grad, up_grad, all_h_two, all_grads = filled

    def wgrad(left, right):
        return (contract_rows(left, right).astype(low),)

    logits = contract_cols(h_two, r_weight)
    row_max = jnp.max(logits, axis=-1, keepdims=True)
    exps_raw = jnp.exp(logits - row_max)
    router_probs = exps_raw / jnp.sum(exps_raw, axis=-1, keepdims=True)
    dx_sum = Scatter(lambda step: (dx_terms[step], []))
    mix_sum = Scatter(lambda step: (mix_terms[step], []))
    ((gate_wgrad,),) = window([dx_sum, mix_sum], [([all_h_two, gate_grad], wgrad)])
    ((up_wgrad,),) = window([dx_sum, mix_sum], [([all_h_two, up_grad], wgrad)])
    window([dx_sum], [])
    window([dx_sum], [])
    hidden_sum = dx_sum.total

    def over_sequences(matrix, axis):
        return lax.psum_scatter(matrix, "fsdp", scatter_dimension=axis, tiled=True)

    sums = [over_sequences(gate_wgrad, 0), over_sequences(up_wgrad, 0)]

    prob_grad = jnp.sum(hidden_sum[tok_rows : tok_rows + 3], axis=0)
    prob_grad = prob_grad.reshape(expert_count, tok_rows).T
    logit_grad = router_probs * (
        prob_grad - jnp.sum(router_probs * prob_grad, axis=-1, keepdims=True)
    )
    hidden_grad = hidden_sum[:tok_rows] + precise(logit_grad, r_weight.astype(jnp.float32))
    norm_grad, ffn_gain_grad = rms_backward(middle, inv_two, g_ffn, hidden_grad)
    middle_grad = grad_out + norm_grad

    sofar = ()

    def back_job(step, blocks):
        made = attend_back_chunk(
            step,
            blocks[0],
            q_rot,
            lse,
            k_rot,
            v_low,
            out_weight,
            tok_rows,
            score_scale,
            sofar,
        )

        def keep(made):
            nonlocal sofar
            sofar = tuple(made)

        return made, keep

    mix_step = mix_sum.job()
    done = ring_gather(
        [middle_grad.astype(low)],
        back_job,
        {2: [mix_step], 4: [([act_low, all_grads], wgrad)]},
    )
    mix_sum.take(done[2][0])
    down_wgrad = done[4][0][0]
    sums.append(over_sequences(down_wgrad, 1))
    dq, all_branch, dk, dv = sofar
    q_back = dq * cos_full - spin(dq) * sin_full
    k_back = dk * cos_full - spin(dk) * sin_full

    def out_job(mixed_low, all_branch):
        return (contract_rows(mixed_low, all_branch),)

    def router_job(h_two, logit_grad):
        return (precise(h_two.astype(jnp.float32).T, logit_grad),)

    along, ((out_wgrad,), (router_wgrad,), mixed) = token_sums(
        jnp.stack(
            [
                jnp.sum(q_back * g_query * q_lin, axis=-1),
                jnp.sum(k_back * g_key * k_lin, axis=-1),
            ],
            axis=0,
        ),
        [
            ([mixed_low, all_branch], out_job),
            ([h_two, logit_grad], router_job),
            mix_sum.job(),
        ],
    )
    mix_sum.take(mixed)
    layer_out = (middle + mix_sum.total).astype(low)
    q_lin_grad = inv_query * (q_back * g_query) - q_lin * inv_query**3 * along[0]
    k_lin_grad = inv_key * (k_back * g_key) - k_lin * inv_key**3 * along[1]
    query_gain_grad = jnp.sum(q_back * q_lin * inv_query, axis=0)
    key_gain_grad = jnp.sum(k_back * k_lin * inv_key, axis=0)
    lin_grad = jnp.concatenate([q_lin_grad, k_lin_grad, dv], axis=1).astype(low)

    own_rows = model_width // (2 * ctx_count)

    def pick(blocks, index):
        return lax.dynamic_index_in_dim(blocks, index, 1, False)

    def split_low(values):
        high = values.astype(low)
        return jnp.concatenate([high, (values - high.astype(jnp.float32)).astype(low)], axis=-1)

    wide_cols = 3 * head_dim
    thin_cols = expert_count + 2
    source_ids = by_place(owners.reshape(CHIPS, 2), 0)

    def dense_job(all_h_one, lin_grad, router_wgrad, ffn_gain_grad):
        wgrad = contract_rows(all_h_one, lin_grad)
        attn_term = jnp.sum(wgrad * qkv_weight.astype(jnp.float32), axis=1) / g_attn
        thin = jnp.concatenate(
            [router_wgrad, ffn_gain_grad[:, None], attn_term[:, None]], axis=1
        )

        def by_owner(matrix):
            return matrix.reshape(ctx_count, 2, own_rows, -1)

        wide, thin = by_owner(wgrad), by_owner(thin)
        sent = jnp.concatenate(
            [pick(wide, 1 - part).astype(low), split_low(pick(thin, 1 - part))], axis=-1
        )
        return sent, pick(wide, part), pick(thin, part)

    def pair_job(sent, wide, thin):
        got = swap(sent, "fsdp").astype(jnp.float32)
        wide = wide + got[..., :wide_cols]
        thin = thin + (
            got[..., wide_cols : wide_cols + thin_cols] + got[..., wide_cols + thin_cols :]
        )
        payload = jnp.concatenate([wide.astype(low), split_low(thin)], axis=-1)
        return (payload[source_ids],)

    out_rows = out_wgrad.reshape(1, 2, own_rows, model_width)
    d_out = pick(out_rows, part)[0] + swap(pick(out_rows, 1 - part)[0].astype(low), "fsdp").astype(
        jnp.float32
    )
    gain_rows = jnp.stack([query_gain_grad, key_gain_grad], axis=0).reshape(2, 2, own_rows)
    gain_rows = pick(gain_rows, part) + swap(pick(gain_rows, 1 - part), "fsdp")
    d_qgain, d_kgain = gain_rows[0], gain_rows[1]

    def h_terms(step, lin_grad):
        first, count = CHUNKS[step]
        rows = lin_grad[2 * first * tok_rows : 2 * (first + count) * tok_rows]
        term = contract_cols(rows, qkv_weight).astype(low)
        return [term[k * tok_rows : (k + 1) * tok_rows] for k in range(2 * count)], []

    h_sum = Scatter(h_terms, [lin_grad])
    (made,) = window(
        [h_sum], [([all_h_one, lin_grad, router_wgrad, ffn_gain_grad], dense_job)]
    )
    ((payload,),) = window([h_sum], [(made, pair_job)])
    (sums,) = window(
        [h_sum], [(sums, lambda *sums: [total.astype(jnp.float32) for total in sums])]
    )
    received = exchange_all(payload)
    window([h_sum], [])
    h_grad = h_sum.total
    s_gate, s_up, s_down = (total[None] for total in sums)
    in_norm_grad, _ = rms_backward(inputs, inv_one, g_attn, h_grad)
    input_grad = (middle_grad + in_norm_grad).astype(low)
    received = received.reshape(ctx_count, own_rows, -1)
    here_order = (
        source_ids.reshape(1, -1) == jnp.arange(ctx_count, dtype=jnp.int32)[:, None]
    ).astype(jnp.int32)
    back_ids = jnp.sum(here_order * jnp.arange(ctx_count, dtype=jnp.int32)[None, :], axis=1)
    dense = received[..., :wide_cols][back_ids].astype(jnp.float32)
    dense = dense.reshape(ctx_count, own_rows, 3, head_dim)
    d_query, d_key, d_value = (
        dense[:, :, i].transpose(1, 0, 2).reshape(own_rows, model_width) for i in range(3)
    )
    thin_sum = jnp.sum(received[..., wide_cols:].astype(jnp.float32), axis=0)
    thin_sum = thin_sum[:, :thin_cols] + thin_sum[:, thin_cols:]
    d_router = thin_sum[:, :expert_count]
    d_ffn, d_attn = thin_sum[:, expert_count], thin_sum[:, expert_count + 1]
    return (
        layer_out[None],
        input_grad[None],
        d_attn,
        d_query,
        d_key,
        d_value,
        d_out,
        d_qgain,
        d_kgain,
        d_ffn,
        d_router,
        s_gate,
        s_up,
        s_down,
    )


def specs_of(ctx):
    rows, both = P("fsdp", ctx, None), ctx + ("fsdp",)
    dense = P("fsdp", None)
    ins = (
        rows,
        rows,
        P("fsdp"),
        dense,
        dense,
        dense,
        dense,
        P("fsdp"),
        P("fsdp"),
        P("fsdp"),
        dense,
        P(ctx, "fsdp", None),
        P(ctx, "fsdp", None),
        P(ctx, None, "fsdp"),
        rows,
        rows,
        P("fsdp", ctx),
    )
    line, matrix = P(both), P(both, None)
    outs = (
        rows,
        rows,
        line,
        matrix,
        matrix,
        matrix,
        matrix,
        line,
        line,
        line,
        matrix,
        P(ctx, "fsdp", None),
        P(ctx, "fsdp", None),
        P(ctx, None, "fsdp"),
    )
    return ins, outs


def solution(mesh):
    ctx_count, fsdp_count = mesh.shape["ctx"], mesh.shape["fsdp"]

    def whole(*arrays):
        heads = arrays[0].shape[2] // HEAD_DIM
        experts = arrays[10].shape[1]
        if ctx_count == 2 * CHIPS == heads == experts and fsdp_count == 2:
            chips = Mesh(mesh.devices.reshape(-1, 2, 2), ("chip", "core", "fsdp"))
            run, grid, ctx = body, chips, ("chip", "core")
        else:
            run, grid, ctx = general_body, mesh, ("ctx",)
        ins, outs = specs_of(ctx)
        return jax.shard_map(run, mesh=grid, in_specs=ins, out_specs=outs, check_vma=False)(*arrays)

    return whole
```

```python
import math

import jax
import jax.numpy as jnp
from jax import lax
from jax.experimental import pallas as pl
from jax.experimental.pallas import tpu as pltpu
from jax.sharding import Mesh
from jax.sharding import PartitionSpec as P

HEAD_DIM = 128
LEVELS = 4


epsilon = 1e-05
rope_base = 50000.0


def prefix(part, axis, combine, identity):
    place = lax.axis_index(axis)
    gathered = lax.all_gather(part, axis)
    state = jnp.zeros_like(part) + jnp.asarray(identity, part.dtype)

    def one(turn, state):
        return combine(state, lax.dynamic_index_in_dim(gathered, turn, 0, False))

    return lax.fori_loop(0, place, one, state)


def product(left, right):
    return jnp.dot(left, right, preferred_element_type=jnp.float32)


def precise(left, right):
    return jnp.dot(left, right, precision=lax.Precision.HIGHEST, preferred_element_type=jnp.float32)


def contract_rows(left, right):
    return lax.dot_general(
        left, right, (((0,), (0,)), ((), ())), preferred_element_type=jnp.float32
    )


def contract_cols(left, right):
    return lax.dot_general(
        left, right, (((1,), (1,)), ((), ())), preferred_element_type=jnp.float32
    )


def rms_forward(matrix, gain_row):
    inverse = lax.rsqrt(jnp.mean(matrix * matrix, axis=-1, keepdims=True) + epsilon)
    return (matrix * inverse * gain_row, inverse)


def rms_backward(matrix, inverse, gain_row, upstream):
    scaled = upstream * gain_row
    along = jnp.mean(scaled * matrix, axis=-1, keepdims=True)
    grad_rows = inverse * scaled - matrix * inverse * inverse * inverse * along
    grad_gain = jnp.sum(upstream * matrix * inverse, axis=0)
    return (grad_rows, grad_gain)


def rope_tables(position_ids, head_dim):
    half_dim = head_dim // 2
    inverse = rope_base ** (-(jnp.arange(half_dim, dtype=jnp.float32) * 2.0) / head_dim)
    angles = position_ids.astype(jnp.float32)[:, None] * inverse[None, :]
    return (jnp.cos(angles)[:, None, :], jnp.sin(angles)[:, None, :])


def rotate(matrix, cosine, sine_part, head_dim, turn_sign):
    count_rows = matrix.shape[0]
    by_head = matrix.reshape(count_rows, -1, head_dim)
    half_dim = head_dim // 2
    lower_half = by_head[..., :half_dim]
    upper_half = by_head[..., half_dim:]
    turned = jnp.concatenate(
        [
            lower_half * cosine - turn_sign * upper_half * sine_part,
            upper_half * cosine + turn_sign * lower_half * sine_part,
        ],
        axis=-1,
    )
    return turned.reshape(count_rows, -1)


def add_counts(earlier_part, later_part):
    return earlier_part + later_part


def score_block(query_part, key_part, score_scale):
    return (
        jnp.einsum("qhd,khd->hqk", query_part, key_part, preferred_element_type=jnp.float32)
        * score_scale
    )


def grad_block(query_part, dout_part, lse_part, delta_part, key_part, value_part, score_scale):
    probs = jnp.exp(score_block(query_part, key_part, score_scale) - lse_part)
    prob_low = probs.astype(jnp.bfloat16)
    dprob = jnp.einsum("qhd,khd->hqk", dout_part, value_part, preferred_element_type=jnp.float32)
    dscore = (probs * (dprob - delta_part)).astype(jnp.bfloat16)
    return (prob_low, dscore)


def general_body(
    tokens,
    cotangent,
    attn_gain,
    w_query,
    w_key,
    w_value,
    w_out,
    query_gain,
    key_gain,
    ffn_gain,
    router,
    w_gate,
    w_up,
    w_down,
    routes,
    priority,
    positions,
):
    ctx_count = lax.axis_size("ctx")
    (
        g_attn,
        q_weight,
        k_weight,
        v_weight,
        o_weight,
        g_query,
        g_key,
        g_ffn,
        r_weight,
        gate_full,
        up_full,
        down_full,
    ) = (
        lax.all_gather(attn_gain, "fsdp", axis=0, tiled=True),
        lax.all_gather(w_query, "fsdp", axis=0, tiled=True),
        lax.all_gather(w_key, "fsdp", axis=0, tiled=True),
        lax.all_gather(w_value, "fsdp", axis=0, tiled=True),
        lax.all_gather(w_out, "fsdp", axis=0, tiled=True),
        lax.all_gather(query_gain, "fsdp", axis=0, tiled=True),
        lax.all_gather(key_gain, "fsdp", axis=0, tiled=True),
        lax.all_gather(ffn_gain, "fsdp", axis=0, tiled=True),
        lax.all_gather(router, "fsdp", axis=0, tiled=True),
        lax.all_gather(w_gate, "fsdp", axis=1, tiled=True),
        lax.all_gather(w_up, "fsdp", axis=1, tiled=True),
        lax.all_gather(w_down, "fsdp", axis=2, tiled=True),
    )
    gate_weight = gate_full[0]
    up_weight = up_full[0]
    down_weight = down_full[0]
    tok_rows = tokens.shape[1]
    model_width = tokens.shape[2]
    head_dim = HEAD_DIM
    head_count = model_width // head_dim
    length = tok_rows * ctx_count
    top_k = routes.shape[2]
    capacity = 9 * tok_rows
    send_rows = 2 * tok_rows * top_k // ctx_count
    key_block = math.gcd(length, 1024)
    block_count = length // key_block
    score_scale = head_dim ** (-0.5)
    inputs = tokens[0].astype(jnp.float32)
    normed, inv_one = rms_forward(inputs, g_attn)
    h_one = normed.astype(jnp.bfloat16)
    q_lin = product(h_one, q_weight)
    k_lin = product(h_one, k_weight)
    v_lin = product(h_one, v_weight)
    cosine, sine_part = rope_tables(positions[0], head_dim)
    q_normed, inv_query = rms_forward(q_lin, g_query)
    k_normed, inv_key = rms_forward(k_lin, g_key)
    q_rot = rotate(q_normed, cosine, sine_part, head_dim, 1.0).astype(jnp.bfloat16)
    k_rot = rotate(k_normed, cosine, sine_part, head_dim, 1.0).astype(jnp.bfloat16)
    v_low = v_lin.astype(jnp.bfloat16)
    all_keys, all_values = (
        lax.all_gather(k_rot, "ctx", axis=0, tiled=True),
        lax.all_gather(v_low, "ctx", axis=0, tiled=True),
    )
    q_heads = q_rot.reshape(tok_rows, head_count, head_dim)

    def key_slice(block_id):
        start = block_id * key_block
        key_part = lax.dynamic_slice_in_dim(all_keys, start, key_block, 0).reshape(
            key_block, head_count, head_dim
        )
        value_part = lax.dynamic_slice_in_dim(all_values, start, key_block, 0).reshape(
            key_block, head_count, head_dim
        )
        return (key_part, value_part)

    def lse_step(carry, block_id):
        run_max, run_total = carry
        key_part, value_part = key_slice(block_id)
        scores = score_block(q_heads, key_part, score_scale)
        new_max = jnp.maximum(run_max, jnp.max(scores, axis=-1, keepdims=True))
        run_total = run_total * jnp.exp(run_max - new_max) + jnp.sum(
            jnp.exp(scores - new_max), axis=-1, keepdims=True
        )
        return ((new_max, run_total), None)

    start_max = jnp.full((head_count, tok_rows, 1), -jnp.inf, jnp.float32)
    start_total = jnp.zeros((head_count, tok_rows, 1), jnp.float32)
    (run_max, run_total), _ = lax.scan(lse_step, (start_max, start_total), jnp.arange(block_count))
    lse = run_max + jnp.log(run_total)

    def out_step(acc, block_id):
        key_part, value_part = key_slice(block_id)
        probs = jnp.exp(score_block(q_heads, key_part, score_scale) - lse).astype(jnp.bfloat16)
        return (
            acc + jnp.einsum("hqk,khd->qhd", probs, value_part, preferred_element_type=jnp.float32),
            None,
        )

    attended_heads, _ = lax.scan(
        out_step, jnp.zeros((tok_rows, head_count, head_dim), jnp.float32), jnp.arange(block_count)
    )
    attended = attended_heads.reshape(tok_rows, model_width)
    mixed_low = attended.astype(jnp.bfloat16)
    middle = inputs + product(mixed_low, o_weight)
    h_two_f, inv_two = rms_forward(middle, g_ffn)
    h_two = h_two_f.astype(jnp.bfloat16)
    logits = product(h_two, r_weight)
    row_max = jnp.max(logits, axis=-1, keepdims=True)
    exps_raw = jnp.exp(logits - row_max)
    router_probs = exps_raw / jnp.sum(exps_raw, axis=-1, keepdims=True)
    route_ids = routes[0]
    level_ids = priority[0]
    pair_code = level_ids * ctx_count + route_ids
    code_table = (
        pair_code[:, :, None] == jnp.arange(LEVELS * ctx_count, dtype=jnp.int32)[None, None, :]
    ).astype(jnp.float32)
    per_token = jnp.sum(code_table, axis=1)
    before_local = jnp.cumsum(per_token, axis=0) - per_token
    local_total = jnp.sum(per_token, axis=0)
    earlier = prefix(local_total, "ctx", add_counts, jnp.zeros_like(local_total))
    totals = lax.psum(local_total, "ctx")
    level_totals = totals.reshape(LEVELS, ctx_count)
    level_base = (jnp.cumsum(level_totals, axis=0) - level_totals).reshape(-1)
    offsets = before_local + (earlier + level_base)[None, :]
    pair_rank = jnp.sum(code_table * offsets[:, None, :], axis=-1).astype(jnp.int32)
    is_kept = pair_rank < capacity
    expert_hot = (
        route_ids[:, :, None] == jnp.arange(ctx_count, dtype=jnp.int32)[None, None, :]
    ).astype(jnp.float32)
    per_expert = jnp.sum(expert_hot, axis=1)
    local_before = jnp.cumsum(per_expert, axis=0) - per_expert
    local_slot = jnp.sum(expert_hot * local_before[:, None, :], axis=-1).astype(jnp.int32)
    send_index = (route_ids * send_rows + local_slot).reshape(-1)
    pair_count = tok_rows * top_k
    pair_of_slot = (
        jnp.full((ctx_count * send_rows,), pair_count, jnp.int32)
        .at[send_index]
        .set(jnp.arange(pair_count, dtype=jnp.int32))
    )
    slot_target = jnp.where(is_kept, pair_rank, capacity).reshape(-1)
    target_pad = jnp.concatenate([slot_target, jnp.full((1,), capacity, jnp.int32)], axis=0)
    send_slots = target_pad[pair_of_slot].reshape(ctx_count, send_rows)
    h_pad = jnp.concatenate([h_two, jnp.zeros((1, model_width), jnp.bfloat16)], axis=0)
    send_tokens = h_pad[pair_of_slot // top_k].reshape(ctx_count, send_rows, model_width)
    got_tokens, got_slots = (
        lax.all_to_all(send_tokens, "ctx", split_axis=0, concat_axis=0, tiled=True),
        lax.all_to_all(send_slots, "ctx", split_axis=0, concat_axis=0, tiled=True),
    )
    received_count = ctx_count * send_rows
    slots_flat = got_slots.reshape(-1)
    row_of_slot = (
        jnp.full((capacity,), received_count, jnp.int32)
        .at[slots_flat]
        .set(jnp.arange(received_count, dtype=jnp.int32), mode="drop")
    )
    got_pad = jnp.concatenate(
        [
            got_tokens.reshape(received_count, model_width),
            jnp.zeros((1, model_width), jnp.bfloat16),
        ],
        axis=0,
    )
    expert_in = got_pad[row_of_slot]
    gate_lin = product(expert_in, gate_weight)
    up_lin = product(expert_in, up_weight)
    sig_gate = jax.nn.sigmoid(gate_lin)
    silu_val = gate_lin * sig_gate
    swiglu = (silu_val * up_lin).astype(jnp.bfloat16)
    expert_out = product(swiglu, down_weight).astype(jnp.bfloat16)
    out_pad = jnp.concatenate([expert_out, jnp.zeros((1, model_width), jnp.bfloat16)], axis=0)
    back_rows = out_pad[slots_flat].reshape(ctx_count, send_rows, model_width)
    returned = lax.all_to_all(back_rows, "ctx", split_axis=0, concat_axis=0, tiled=True)
    returned_pad = jnp.concatenate(
        [
            returned.reshape(ctx_count * send_rows, model_width),
            jnp.zeros((1, model_width), jnp.bfloat16),
        ],
        axis=0,
    )
    pair_out = returned_pad[send_index].reshape(tok_rows, top_k, model_width)
    chosen = jnp.sum(router_probs[:, None, :] * expert_hot, axis=-1)
    share = jnp.where(is_kept, chosen, 0.0)
    mixture = jnp.einsum("tk,tkd->td", share, pair_out, preferred_element_type=jnp.float32)
    final_rows = middle + mixture
    layer_out = final_rows.astype(jnp.bfloat16)
    grad_out = cotangent[0].astype(jnp.float32)
    routed_grad = (share[:, :, None] * grad_out[:, None, :]).astype(jnp.bfloat16)
    share_grad = jnp.where(
        is_kept,
        jnp.einsum("tkd,td->tk", pair_out, grad_out, preferred_element_type=jnp.float32),
        0.0,
    )
    prob_grad = jnp.sum(expert_hot * share_grad[:, :, None], axis=1)
    logit_grad = router_probs * (
        prob_grad - jnp.sum(router_probs * prob_grad, axis=-1, keepdims=True)
    )
    routed_pad = jnp.concatenate(
        [routed_grad.reshape(pair_count, model_width), jnp.zeros((1, model_width), jnp.bfloat16)],
        axis=0,
    )
    send_grads = routed_pad[pair_of_slot].reshape(ctx_count, send_rows, model_width)
    got_grads = lax.all_to_all(send_grads, "ctx", split_axis=0, concat_axis=0, tiled=True)
    grad_pad = jnp.concatenate(
        [got_grads.reshape(received_count, model_width), jnp.zeros((1, model_width), jnp.bfloat16)],
        axis=0,
    )
    out_grad = grad_pad[row_of_slot]
    act_grad = contract_cols(out_grad, down_weight)
    down_wgrad = contract_rows(swiglu, out_grad)
    gate_grad = (act_grad * up_lin * sig_gate * (1.0 + gate_lin * (1.0 - sig_gate))).astype(
        jnp.bfloat16
    )
    up_grad = (act_grad * silu_val).astype(jnp.bfloat16)
    in_grad = (contract_cols(gate_grad, gate_weight) + contract_cols(up_grad, up_weight)).astype(
        jnp.bfloat16
    )
    gate_wgrad = contract_rows(expert_in, gate_grad)
    up_wgrad = contract_rows(expert_in, up_grad)
    in_pad = jnp.concatenate([in_grad, jnp.zeros((1, model_width), jnp.bfloat16)], axis=0)
    back_grads = in_pad[slots_flat].reshape(ctx_count, send_rows, model_width)
    pair_grads = lax.all_to_all(back_grads, "ctx", split_axis=0, concat_axis=0, tiled=True)
    pair_pad = jnp.concatenate(
        [
            pair_grads.reshape(ctx_count * send_rows, model_width),
            jnp.zeros((1, model_width), jnp.bfloat16),
        ],
        axis=0,
    )
    token_pair = pair_pad[send_index].reshape(tok_rows, top_k, model_width)
    hidden_grad = jnp.sum(token_pair.astype(jnp.float32), axis=1) + precise(
        logit_grad, r_weight.astype(jnp.float32).T
    )
    router_wgrad = precise(h_two.astype(jnp.float32).T, logit_grad)
    norm_grad, ffn_gain_grad = rms_backward(middle, inv_two, g_ffn, hidden_grad)
    middle_grad = grad_out + norm_grad
    branch_grad = middle_grad.astype(jnp.bfloat16)
    out_wgrad = contract_rows(mixed_low, branch_grad)
    mixed_grad = contract_cols(branch_grad, o_weight).astype(jnp.bfloat16)
    dout_heads = mixed_grad.reshape(tok_rows, head_count, head_dim)
    delta = jnp.sum(dout_heads.astype(jnp.float32) * attended_heads, axis=-1).T[:, :, None]

    def back_step(dq_acc, block_id):
        key_part, value_part = key_slice(block_id)
        prob_low, dscore = grad_block(
            q_heads, dout_heads, lse, delta, key_part, value_part, score_scale
        )
        dq_acc = dq_acc + jnp.einsum(
            "hqk,khd->qhd", dscore, key_part, preferred_element_type=jnp.float32
        )
        dk_part = jnp.einsum(
            "hqk,qhd->khd", dscore, q_heads, preferred_element_type=jnp.float32
        ).reshape(key_block, model_width)
        dv_part = jnp.einsum(
            "hqk,qhd->khd", prob_low, dout_heads, preferred_element_type=jnp.float32
        ).reshape(key_block, model_width)
        return (dq_acc, jnp.concatenate([dk_part, dv_part], axis=1))

    dq_heads, kv_terms = lax.scan(
        back_step, jnp.zeros((tok_rows, head_count, head_dim), jnp.float32), jnp.arange(block_count)
    )
    kv_mine = lax.psum_scatter(
        kv_terms.reshape(length, 2 * model_width), "ctx", scatter_dimension=0, tiled=True
    )
    key_grad = kv_mine[:, :model_width] * score_scale
    value_grad = kv_mine[:, model_width:]
    v_lin_low = value_grad.astype(jnp.bfloat16)
    q_grad = dq_heads.reshape(tok_rows, model_width) * score_scale
    q_back = rotate(q_grad, cosine, sine_part, head_dim, -1.0)
    k_back = rotate(key_grad, cosine, sine_part, head_dim, -1.0)
    q_lin_grad, query_gain_grad = rms_backward(q_lin, inv_query, g_query, q_back)
    k_lin_grad, key_gain_grad = rms_backward(k_lin, inv_key, g_key, k_back)
    q_lin_low = q_lin_grad.astype(jnp.bfloat16)
    k_lin_low = k_lin_grad.astype(jnp.bfloat16)
    h_grad = (
        contract_cols(q_lin_low, q_weight)
        + contract_cols(k_lin_low, k_weight)
        + contract_cols(v_lin_low, v_weight)
    )
    query_wgrad = contract_rows(h_one, q_lin_low)
    key_wgrad = contract_rows(h_one, k_lin_low)
    value_wgrad = contract_rows(h_one, v_lin_low)
    in_norm_grad, attn_gain_grad = rms_backward(inputs, inv_one, g_attn, h_grad)
    input_grad = (middle_grad + in_norm_grad).astype(jnp.bfloat16)
    s_gate, s_up, s_down = (
        lax.psum_scatter(
            gate_wgrad[None].astype(jnp.bfloat16), "fsdp", scatter_dimension=1, tiled=True
        ).astype(jnp.float32),
        lax.psum_scatter(
            up_wgrad[None].astype(jnp.bfloat16), "fsdp", scatter_dimension=1, tiled=True
        ).astype(jnp.float32),
        lax.psum_scatter(
            down_wgrad[None].astype(jnp.bfloat16), "fsdp", scatter_dimension=2, tiled=True
        ).astype(jnp.float32),
    )
    d_attn, d_query, d_key, d_value, d_out, d_qgain, d_kgain, d_ffn, d_router = (
        lax.psum_scatter(attn_gain_grad, ("ctx", "fsdp"), scatter_dimension=0, tiled=True),
        lax.psum_scatter(query_wgrad, ("ctx", "fsdp"), scatter_dimension=0, tiled=True),
        lax.psum_scatter(key_wgrad, ("ctx", "fsdp"), scatter_dimension=0, tiled=True),
        lax.psum_scatter(value_wgrad, ("ctx", "fsdp"), scatter_dimension=0, tiled=True),
        lax.psum_scatter(out_wgrad, ("ctx", "fsdp"), scatter_dimension=0, tiled=True),
        lax.psum_scatter(query_gain_grad, ("ctx", "fsdp"), scatter_dimension=0, tiled=True),
        lax.psum_scatter(key_gain_grad, ("ctx", "fsdp"), scatter_dimension=0, tiled=True),
        lax.psum_scatter(ffn_gain_grad, ("ctx", "fsdp"), scatter_dimension=0, tiled=True),
        lax.psum_scatter(router_wgrad, ("ctx", "fsdp"), scatter_dimension=0, tiled=True),
    )
    return (
        layer_out[None],
        input_grad[None],
        d_attn,
        d_query,
        d_key,
        d_value,
        d_out,
        d_qgain,
        d_kgain,
        d_ffn,
        d_router,
        s_gate,
        s_up,
        s_down,
    )


RING = [0, 2, 4, 6, 7, 5, 3, 1]
CHIPS = len(RING)
FAR = CHIPS // 2
EXTRA = 8
PLACES = [1, 7, 2, 6, 3, 5, 0, 4]
CHUNKS = {1: (0, 2), 2: (2, 2), 3: (4, 2), 0: (6, 1), FAR: (7, 1)}
LAST = -1
WIDE_CHUNKS = {1: (0, 2), 2: (2, 2), 3: (4, 2), LAST: (6, 2)}


BRIEF = pl.CostEstimate(flops=0, bytes_accessed=0, transcendentals=0)


def swap(array, axis):
    return lax.ppermute(array, axis, [(0, 1), (1, 0)])


def shift(array, by):
    pairs = [(RING[i], RING[(i + by) % CHIPS]) for i in range(CHIPS)]
    return lax.ppermute(array, "chip", pairs)


def fence(*groups):
    flat = lax.optimization_barrier(tuple(array for group in groups for array in group))
    out, at = [], 0
    for group in groups:
        out.append(list(flat[at : at + len(group)]))
        at += len(group)
    return out


def open_jobs(carried, jobs):
    opened = fence(carried, *[list(inputs) for inputs, _ in jobs])
    return opened[0], [(ins, function) for ins, (_, function) in zip(opened[1:], jobs)]


def run_jobs(jobs):
    return [list(function(*inputs)) for inputs, function in jobs]


class Gather:
    def __init__(self, block):
        self.ahead = self.behind = block
        self.cut = block.shape[0] // 2 // 8 * 8
        self.fresh = [block]
        self.step = 0
        self.chunks = {}

    def job(self):
        ahead, behind = self.ahead, self.behind
        if self.step + 1 == FAR:
            ahead, behind = ahead[: self.cut], behind[self.cut :]

        def function(ahead, behind, *fresh):
            ahead, behind = shift(ahead, 1), shift(behind, -1)
            self.now = [x for block in fresh for x in (block, swap(block, "core"))]
            return [ahead, behind, *self.now]

        return [ahead, behind, *self.fresh], function

    def take(self, results):
        self.ahead, self.behind, *self.chunks[self.step] = results
        self.step += 1
        if self.step == FAR:
            last = jnp.concatenate([self.ahead, self.behind], axis=0)
            self.chunks[FAR] = [last, swap(last, "core")]
            self.chunks[LAST] = self.chunks[0] + self.chunks[FAR]
        self.fresh = [self.behind, self.ahead]


class Scatter:
    def __init__(self, make, inputs=()):
        self.make, self.inputs = make, list(inputs)
        self.step = 0
        mine, other = make(FAR, *self.inputs)
        first = mine
        if other is not None:
            first = mine.astype(jnp.float32) + swap(other, "core").astype(jnp.float32)
            first = first.astype(jnp.bfloat16)
        self.rows = first.shape[0]
        self.cut = self.rows // 2 // 8 * 8
        self.carried = [first[: self.cut], first[self.cut :]]

    def job(self):
        near = FAR - self.step - 1

        def function(ahead, behind, *inputs):
            ahead, behind = shift(ahead, 1), shift(behind, -1)
            mine, other = self.make(near, *inputs)
            return [ahead, behind, mine] + ([] if other is None else [swap(other, "core")])

        return self.carried + self.inputs, function

    def take(self, results):
        self.step += 1
        ahead, behind, *terms = results
        ahead, behind = ahead.astype(jnp.float32), behind.astype(jnp.float32)

        def term(i):
            span = slice(i * self.rows, (i + 1) * self.rows)
            return sum(part[span].astype(jnp.float32) for part in terms)

        if self.step == FAR:
            self.total = term(0) + ahead + behind
            return
        if self.step == 1:
            ahead = jnp.concatenate([ahead, jnp.zeros_like(behind)], axis=0)
            behind = jnp.concatenate([jnp.zeros_like(ahead[: self.cut]), behind], axis=0)
        self.carried = [
            (term(0) + ahead).astype(jnp.bfloat16),
            (term(1) + behind).astype(jnp.bfloat16),
        ]


def window(items, jobs=(), loose=()):
    every = [item.job() for item in items] + list(jobs) + list(loose)
    _, opened = open_jobs([], every)
    results = run_jobs(opened)
    count = len(items) + len(jobs)
    results = fence(*results[:count]) + results[count:]
    for item, result in zip(items, results):
        item.take(result)
    return results[len(items) :]


def sum_all(values, jobs):
    (values,), jobs = open_jobs([values], jobs)
    core = lax.axis_index("core")
    both = values + swap(values[:, :, ::-1], "core")

    def heard(by):
        pairs = [
            (2 * RING[i] + c, 2 * RING[(i + (by if c == 0 else -by)) % CHIPS] + c)
            for i in range(CHIPS)
            for c in range(2)
        ]
        return lax.ppermute(both, ("chip", "core"), pairs)

    moved = [heard(by) for by in range(1, FAR + 1)]
    done = run_jobs(jobs)
    moved, *done = fence(moved, *done)
    total = jnp.where(core == 0, both, jnp.roll(moved[-1], -FAR, axis=1))
    for by in range(1, FAR):
        total = total + jnp.where(
            core == 0, jnp.roll(moved[by - 1], -by, axis=1), jnp.roll(moved[by - 1], by, axis=1)
        )
    return total + swap(total[:, :, ::-1], "core"), done


def by_place(values, axis):
    return jnp.stack(
        [lax.index_in_dim(values, PLACES.index(at), axis, False) for at in range(CHIPS)], axis
    )


def by_chunk(values, axis):
    return jnp.stack([lax.index_in_dim(values, at, axis, False) for at in PLACES], axis)


def in_hbm(arrays, specs):
    return [
        array
        if spec.memory_space == pltpu.SMEM
        else pltpu.with_memory_space_constraint(array, pltpu.HBM)
        for array, spec in zip(arrays, specs)
    ]


def call(kernel, name, inputs, ins, outs, shapes, earlier=(), grid=(1,), scratch=(), mib=56):
    return pl.pallas_call(
        kernel,
        grid=grid,
        in_specs=ins + [pl.BlockSpec(memory_space=pl.ANY)] * len(earlier),
        out_specs=outs,
        out_shape=shapes,
        scratch_shapes=list(scratch),
        input_output_aliases={len(ins) + i: i for i in range(len(earlier))},
        compiler_params=pltpu.CompilerParams(vmem_limit_bytes=mib << 20),
        cost_estimate=BRIEF,
        name=name,
    )(*in_hbm(inputs, ins), *earlier)


def whole(array):
    return pl.BlockSpec(array.shape, lambda i: (0,) * len(array.shape))


def once(array):
    return pl.BlockSpec(
        array.shape, lambda i: (0,) * len(array.shape), pipeline_mode=pl.Buffered(1)
    )


def rows_of(step, tok_rows, cols):
    first, count = WIDE_CHUNKS[step] if step == LAST else CHUNKS[step]
    index = first // count
    return pl.BlockSpec((2 * count * tok_rows, cols), lambda i: (index, 0))


def lin_chunk(step, blocks, weight, gain, place, tok_rows, earlier):
    count, width, cols = len(blocks), weight.shape[0], weight.shape[1]
    length = 2 * CHIPS * tok_rows
    rows, head = count * tok_rows, weight.shape[1] // 3

    def kernel(*refs):
        block_refs, weight_ref, gain_ref, place_ref = refs[:count], *refs[count : count + 3]
        lin_ref, all_ref, sum_ref, tag_ref = refs[-4:]
        lanes = pl.ds(pl.multiple_of(place_ref[0] * tok_rows, tok_rows), tok_rows)
        for i in range(count):
            normed, _ = rms_forward(block_refs[i][:tok_rows].astype(jnp.float32), gain_ref[...])
            all_ref[i * tok_rows : (i + 1) * tok_rows] = normed.astype(jnp.bfloat16)
            levels = block_refs[i][tok_rows:, lanes].astype(jnp.float32)
            others = block_refs[i][tok_rows:, : 3 * tok_rows].astype(jnp.float32)
            tag_ref[i * EXTRA : (i + 1) * EXTRA] = jnp.concatenate(
                [levels[:1]]
                + [others[1:2, k * tok_rows : (k + 1) * tok_rows] for k in range(3)]
                + [jnp.zeros((EXTRA - 4, tok_rows), jnp.float32)],
                axis=0,
            )
        lin = product(all_ref[...], weight_ref[...])
        lin_ref[...] = lin
        line = lax.broadcasted_iota(jnp.int32, (8, head), 0)
        total = jnp.zeros((8, rows), jnp.float32)
        for k in range(2):
            part = lin[:, k * head : (k + 1) * head]
            total = total + lax.dot_general(
                (line == k).astype(jnp.float32),
                part * part,
                (((1,), (1,)), ((), ())),
                precision=lax.Precision.HIGHEST,
                preferred_element_type=jnp.float32,
            )
        sum_ref[...] = total

    tags = jax.ShapeDtypeStruct((count * EXTRA, tok_rows), jnp.float32)
    sums = jax.ShapeDtypeStruct((8, rows), jnp.float32)
    return call(
        kernel,
        "lin",
        [*blocks, weight, gain, place],
        [whole(b) for b in blocks]
        + [whole(weight), whole(gain), pl.BlockSpec(memory_space=pltpu.SMEM)],
        [rows_of(step, tok_rows, cols), rows_of(step, tok_rows, width), whole(sums), whole(tags)],
        [
            jax.ShapeDtypeStruct((length, cols), jnp.float32),
            jax.ShapeDtypeStruct((length, width), jnp.bfloat16),
            sums,
            tags,
        ],
        earlier,
    )


def both_halves(cosine, sine_part):
    return (
        jnp.concatenate([cosine, cosine], axis=-1),
        jnp.concatenate([-sine_part, sine_part], axis=-1),
    )


def rotate_rows(lin, inverse, gains, cosine, sine_part):
    length, cols = lin.shape
    head = cols // 3
    rows = length // 4

    def kernel(lin_ref, inv_ref, gain_ref, cos_ref, sin_ref, q_ref, k_ref, v_ref):
        cos, sin = both_halves(cos_ref[...], sin_ref[...])
        for k, out_ref in enumerate((q_ref, k_ref)):
            part = lin_ref[:, k * head : (k + 1) * head] * inv_ref[:, k : k + 1]
            part = part * gain_ref[k : k + 1]
            turned = pltpu.roll(part, head // 2, 1)
            out_ref[...] = (part * cos + turned * sin).astype(jnp.bfloat16)
        v_ref[...] = lin_ref[:, 2 * head :].astype(jnp.bfloat16)

    row = lambda width: pl.BlockSpec((rows, width), lambda i: (i, 0))
    return call(
        kernel,
        "rotate",
        [lin, inverse, gains, cosine, sine_part],
        [row(cols), row(2), whole(gains), row(head // 2), row(head // 2)],
        [row(head)] * 3,
        [jax.ShapeDtypeStruct((length, head), jnp.bfloat16)] * 3,
        grid=(4,),
        mib=16,
    )


def attend_chunk(step, queries, keys, values, tok_rows, score_scale):
    count = 2 * CHUNKS[step][1]
    head = keys.shape[1]

    def kernel(q_ref, k_ref, v_ref, out_ref, lse_ref, mine_ref, other_ref):
        for i in range(0, count, 2):
            span = pl.ds(i * tok_rows, 2 * tok_rows)
            scores = contract_cols(q_ref[span], k_ref[...]) * score_scale
            row_max = jnp.max(scores, axis=-1, keepdims=True)
            raw = jnp.exp(scores - row_max)
            total = jnp.sum(raw, axis=-1, keepdims=True)
            probs = (raw / total).astype(jnp.bfloat16)
            mixed = product(probs, v_ref[...]).astype(jnp.bfloat16)
            out_ref[span] = mixed
            lse_ref[span] = row_max + jnp.log(total)
            half = pl.ds(i // 2 * tok_rows, tok_rows)
            mine_ref[half] = mixed[:tok_rows]
            other_ref[half] = mixed[tok_rows:]

    rows = count * tok_rows
    shapes = [
        jax.ShapeDtypeStruct((rows, head), jnp.bfloat16),
        jax.ShapeDtypeStruct((rows, 1), jnp.float32),
    ] + [jax.ShapeDtypeStruct((rows // 2, head), jnp.bfloat16)] * 2
    return call(
        kernel,
        "attend",
        [queries, keys, values],
        [rows_of(step, tok_rows, head), whole(keys), whole(values)],
        [whole(shape) for shape in shapes],
        shapes,
        mib=40,
    )


def pair_product(left, right, left_weight, right_weight, transposed, name, step=None):
    multiply = contract_cols if transposed else product
    width = left_weight.shape[0] if transposed else left_weight.shape[1]
    rows, block = left.shape[0], whole(left)
    if step is not None:
        first, count = CHUNKS[step]
        rows, index = rows * count // CHIPS, first // count
        block = pl.BlockSpec((rows, left.shape[1]), lambda i: (index, 0))

    def kernel(left_ref, right_ref, left_weight_ref, right_weight_ref, out_ref):
        total = multiply(left_ref[...], left_weight_ref[...])
        total = total + multiply(right_ref[...], right_weight_ref[...])
        out_ref[...] = total.astype(jnp.bfloat16)

    shape = jax.ShapeDtypeStruct((rows, width), jnp.bfloat16)
    arrays = [left, right, left_weight, right_weight]
    return call(
        kernel,
        name,
        arrays,
        [block, block, whole(left_weight), whole(right_weight)],
        [whole(shape)],
        [shape],
        mib=32,
    )[0]


def attend_back_chunk(
    step, blocks, queries, lse, keys, values, weight, lin, gains, cosine, sine_part, tok_rows,
    score_scale, earlier, final
):
    count = len(blocks)
    length, head = keys.shape
    width = weight.shape[1]
    rows = count * tok_rows

    def unspun(grad, cosine, sine_part, gain):
        cos, sin = both_halves(cosine, sine_part)
        return (grad * cos - pltpu.roll(grad, head // 2, 1) * sin) * gain

    def line_sums(values):
        ones = jnp.ones((8, head), jnp.float32)
        return lax.dot_general(
            ones,
            values,
            (((1,), (1,)), ((), ())),
            precision=lax.Precision.HIGHEST,
            preferred_element_type=jnp.float32,
        )

    def kernel(*refs):
        block_refs = refs[:count]
        q_ref, lse_ref, lin_ref, cos_ref, sin_ref = refs[count : count + 5]
        k_ref, v_ref, w_ref, gain_ref = refs[count + 5 : count + 9]
        rest = refs[count + 9 :]
        if final:
            k_lin_ref, cos_all, sin_all = rest[:3]
            rest = rest[3:]
        if earlier:
            dk, dv = rest[0][...], rest[1][...]
        else:
            dk, dv = 0.0, 0.0
        dq_ref, all_ref, dk_ref, dv_ref, q_sums = rest[-6:-1] if final else rest[-5:]
        for i in range(count):
            all_ref[i * tok_rows : (i + 1) * tok_rows] = block_refs[i][...]
        for i in range(0, count, 2):
            span = pl.ds(i * tok_rows, 2 * tok_rows)
            queries = q_ref[span]
            douts = contract_cols(all_ref[span], w_ref[...]).astype(jnp.bfloat16)
            probs = jnp.exp(contract_cols(queries, k_ref[...]) * score_scale - lse_ref[span])
            dprobs = contract_cols(douts, v_ref[...])
            delta = jnp.sum(probs * dprobs, axis=-1, keepdims=True)
            dscores = (probs * (dprobs - delta)).astype(jnp.bfloat16)
            dq = product(dscores, k_ref[...]) * score_scale
            dq = unspun(dq, cos_ref[span], sin_ref[span], gain_ref[:1])
            dq_ref[span] = dq
            q_sums[:, i * tok_rows : (i + 2) * tok_rows] = line_sums(dq * lin_ref[span])
            dk = dk + contract_rows(dscores, queries) * score_scale
            dv = dv + contract_rows(probs.astype(jnp.bfloat16), douts)
        if final:
            dk = unspun(dk, cos_all[...], sin_all[...], gain_ref[1:])
            rest[-1][...] = line_sums(dk * k_lin_ref[...])
        dk_ref[...] = dk
        dv_ref[...] = dv

    total = jax.ShapeDtypeStruct((length, head), jnp.float32)
    inputs = [*blocks, queries, lse, lin, cosine, sine_part, keys, values, weight, gains]
    ins = [whole(b) for b in blocks] + [
        rows_of(step, tok_rows, head),
        rows_of(step, tok_rows, 1),
        rows_of(step, tok_rows, head),
        rows_of(step, tok_rows, head // 2),
        rows_of(step, tok_rows, head // 2),
        whole(keys),
        whole(values),
        whole(weight),
        whole(gains),
    ]
    sums = [jax.ShapeDtypeStruct((8, rows), jnp.float32)]
    if final:
        inputs += [lin, cosine, sine_part]
        ins += [pl.BlockSpec((length, head), lambda i: (0, 1)), whole(cosine), whole(sine_part)]
        sums += [jax.ShapeDtypeStruct((8, length), jnp.float32)]
    so_far = list(earlier[2:4])
    return pl.pallas_call(
        kernel,
        grid=(1,),
        in_specs=ins
        + [whole(part) for part in so_far]
        + [pl.BlockSpec(memory_space=pl.ANY)] * len(earlier[:2]),
        out_specs=[
            rows_of(step, tok_rows, head),
            rows_of(step, tok_rows, width),
            whole(total),
            whole(total),
        ]
        + [whole(part) for part in sums],
        out_shape=[total, jax.ShapeDtypeStruct((length, width), jnp.bfloat16), total, total] + sums,
        input_output_aliases={
            len(ins): 2,
            len(ins) + 1: 3,
            len(ins) + 2: 0,
            len(ins) + 3: 1,
        }
        if earlier
        else {},
        compiler_params=pltpu.CompilerParams(vmem_limit_bytes=56 << 20),
        cost_estimate=BRIEF,
        name="attend_back",
    )(*in_hbm(inputs, ins), *so_far, *earlier[:2])


def lin_back_rows(dq, dk, dv, lin, inverse, along, tok_rows):
    length, cols = lin.shape
    head = cols // 3
    rows = 2 * tok_rows

    def kernel(dq_ref, dk_ref, dv_ref, lin_ref, inv_ref, along_ref, out_ref, mine_ref, other_ref):
        for k, grad_ref in enumerate((dq_ref, dk_ref)):
            span = slice(k * head, (k + 1) * head)
            inv = inv_ref[:, k : k + 1]
            slope = inv * inv * inv * along_ref[:, k : k + 1]
            out_ref[:, span] = (inv * grad_ref[...] - lin_ref[:, span] * slope).astype(jnp.bfloat16)
        out_ref[:, 2 * head :] = dv_ref[...].astype(jnp.bfloat16)
        mine_ref[...] = out_ref[:tok_rows]
        other_ref[...] = out_ref[tok_rows:]

    row = lambda width: pl.BlockSpec((rows, width), lambda i: (i, 0))
    half = jax.ShapeDtypeStruct((length // 2, cols), jnp.bfloat16)
    return call(
        kernel,
        "lin_back",
        [dq, dk, dv, lin, inverse, along],
        [row(head)] * 3 + [row(cols), row(2), row(2)],
        [row(cols)] + [pl.BlockSpec((tok_rows, cols), lambda i: (i, 0))] * 2,
        [jax.ShapeDtypeStruct((length, cols), jnp.bfloat16), half, half],
        grid=(CHIPS,),
        mib=16,
    )


EXPERT_COLS = 512


def expert_chunk(step, h_blocks, g_blocks, place, kept, router, gate, up, down, tok_rows, earlier):
    count = len(h_blocks)
    width, hidden = gate.shape
    cols = EXPERT_COLS
    rows = count * tok_rows
    length = 2 * CHIPS * tok_rows
    low = jnp.bfloat16
    first, places = WIDE_CHUNKS[step]
    index = first // places
    inner, outer = hidden // cols, width // cols
    long_rows = tok_rows + EXTRA
    per_tile = cols // tok_rows
    apart = places if step == LAST else 1
    together = places // apart

    def kernel(*refs):
        h_refs, g_refs = refs[:count], refs[count : 2 * count]
        place_ref, kept_ref, router_ref = refs[2 * count : 2 * count + 3]
        gate_ref, up_ref, down_ref, gate_rows, up_rows, down_cols = refs[
            2 * count + 3 : 2 * count + 9
        ]
        outs = refs[2 * count + 9 + len(earlier) : -8]
        row_outs, (act_ref, dgate_ref, dup_ref) = outs[:2], outs[2:5]
        mix_refs, dx_refs = outs[5 : 5 + 2 * apart], outs[5 + 2 * apart :]
        h_all, g_all, act_all, dgate_all, dup_all, share_ref, dshare_ref, sems = refs[-8:]
        turn = pl.program_id(0)

        def copies():
            span = pl.ds(index * rows, rows)
            return [
                pltpu.make_async_copy(source, out.at[span], sems.at[i])
                for i, (source, out) in enumerate(zip((h_all, g_all), row_outs))
            ]

        @pl.when(turn == 0)
        def _():
            for i in range(count):
                h_all[i * tok_rows : (i + 1) * tok_rows] = h_refs[i][...]
                g_all[i * tok_rows : (i + 1) * tok_rows] = g_refs[i][...]
            logits = contract_cols(h_all[...], router_ref[...])
            raw = jnp.exp(logits - jnp.max(logits, axis=-1, keepdims=True))
            probs = raw / jnp.sum(raw, axis=-1, keepdims=True)
            lanes = lax.broadcasted_iota(jnp.int32, probs.shape, 1)
            chosen = jnp.sum(
                jnp.where(lanes == place_ref[0], probs, 0.0), axis=-1, keepdims=True
            )
            share_ref[...] = chosen * kept_ref[...]
            dshare_ref[...] = jnp.zeros_like(dshare_ref)

        @pl.when(turn == 1)
        def _():
            for copy in copies():
                copy.start()

        @pl.when(turn < inner)
        def _():
            share = share_ref[...]
            gate_lin = product(h_all[...], gate_ref[...])
            up_lin = product(h_all[...], up_ref[...])
            back = contract_cols(g_all[...], down_ref[...])
            sig = jax.nn.sigmoid(gate_lin)
            silu = gate_lin * sig
            act = silu * up_lin
            dshare_ref[...] += jnp.sum(act * back, axis=-1, keepdims=True)
            act_low = (act * share).astype(low)
            back = back * share
            dgate = (back * up_lin * (sig * (1.0 + gate_lin * (1.0 - sig)))).astype(low)
            dup = (back * silu).astype(low)
            span = pl.ds(pl.multiple_of(turn * cols, cols), cols)
            for ref, everything, value in (
                (act_ref, act_all, act_low),
                (dgate_ref, dgate_all, dgate),
                (dup_ref, dup_all, dup),
            ):
                ref[...] = value
                everything[:, span] = value

        @pl.when(turn >= inner)
        def _():
            mix = product(act_all[...], down_cols[...]).astype(low)
            dx = contract_cols(dgate_all[...], gate_rows[...])
            dx = (dx + contract_cols(dup_all[...], up_rows[...])).astype(low)
            for i in range(count):
                span = slice(i * tok_rows, (i + 1) * tok_rows)
                to, at = i % 2 + i // 2 // together * 2, i // 2 % together
                mix_refs[to][at * tok_rows : (at + 1) * tok_rows] = mix[span]
                dx_refs[to][at * long_rows : at * long_rows + tok_rows] = dx[span]

            total = dshare_ref[...] * kept_ref[...]
            same = lax.broadcasted_iota(jnp.int32, (tok_rows, tok_rows), 0) == (
                lax.broadcasted_iota(jnp.int32, (tok_rows, tok_rows), 1)
            )
            tile_lanes = lax.broadcasted_iota(jnp.int32, (EXTRA, cols), 1) // tok_rows
            here = tile_lanes + (turn - inner) * per_tile == place_ref[0]
            for i in range(count):
                rest = jnp.sum(
                    jnp.where(same, total[i * tok_rows : (i + 1) * tok_rows], 0.0),
                    axis=0,
                    keepdims=True,
                )
                pieces = []
                for _ in range(3):
                    piece = rest.astype(low).astype(jnp.float32)
                    rest = rest - piece
                    pieces.append(piece)
                pieces.append(jnp.zeros((EXTRA - 3, tok_rows), jnp.float32))
                line = jnp.concatenate(pieces, axis=0)
                line = jnp.concatenate([line] * per_tile, axis=1)
                to, at = i % 2 + i // 2 // together * 2, i // 2 % together
                at = at * long_rows + tok_rows
                dx_refs[to][at : at + EXTRA] = jnp.where(here, line, 0.0).astype(low)

        @pl.when(turn == inner + outer - 1)
        def _():
            for copy in copies():
                copy.wait()

    def inner_at(t):
        return jnp.minimum(t, inner - 1)

    def outer_at(t):
        return jnp.maximum(t - inner, 0)

    tile = pl.BlockSpec((rows, cols), lambda t: (index, inner_at(t)))
    wide = jax.ShapeDtypeStruct((length, hidden), low)
    full = jax.ShapeDtypeStruct((length, width), low)
    half = jax.ShapeDtypeStruct((together * tok_rows, width), low)
    longer = jax.ShapeDtypeStruct((together * long_rows, width), low)
    anywhere = pl.BlockSpec(memory_space=pl.ANY)
    out_tile = lambda shape: pl.BlockSpec((shape.shape[0], cols), lambda t: (0, outer_at(t)))
    return call(
        kernel,
        "expert",
        [*h_blocks, *g_blocks, place, kept, router, gate, up, down, gate, up, down],
        [once(b) for b in [*h_blocks, *g_blocks]]
        + [
            pl.BlockSpec(memory_space=pltpu.SMEM),
            pl.BlockSpec((rows, 1), lambda t: (index, 0)),
            whole(router),
            pl.BlockSpec((width, cols), lambda t: (0, inner_at(t))),
            pl.BlockSpec((width, cols), lambda t: (0, inner_at(t))),
            pl.BlockSpec((cols, width), lambda t: (inner_at(t), 0)),
            pl.BlockSpec((cols, hidden), lambda t: (outer_at(t), 0)),
            pl.BlockSpec((cols, hidden), lambda t: (outer_at(t), 0)),
            pl.BlockSpec((hidden, cols), lambda t: (0, outer_at(t))),
        ],
        [anywhere] * 2
        + [tile] * 3
        + [out_tile(half)] * (2 * apart)
        + [out_tile(longer)] * (2 * apart),
        [full] * 2 + [wide] * 3 + [half] * (2 * apart) + [longer] * (2 * apart),
        earlier,
        grid=(inner + outer,),
        scratch=[pltpu.VMEM((rows, width), low)] * 2
        + [pltpu.VMEM((rows, hidden), low)] * 3
        + [pltpu.VMEM((rows, 1), jnp.float32)] * 2
        + [pltpu.SemaphoreType.DMA((2,))],
        mib=58,
    )


THIN = 128
HALF_THIN = THIN // 2


def split_parts(values):
    high = values.astype(jnp.bfloat16).astype(jnp.float32)
    return high, values - high


def dense_chunk(rows_h, grads, weight, columns, gain, narrow, part, own_rows):
    length, width = rows_h.shape
    cols = grads.shape[1]
    block = 256
    runs = block // (2 * own_rows)
    wide = narrow is not None
    first_col, count_col = columns

    def kernel(part_ref, h_ref, grads_ref, weight_ref, gain_ref, *refs):
        kept_ref, sent_ref = refs[-2:] if wide else refs[-3:-1]
        grads = contract_rows(h_ref[...], grads_ref[...])
        weight = weight_ref[...].astype(jnp.float32)[:, first_col : first_col + count_col]
        term = jnp.sum(grads * weight, axis=-1, keepdims=True) / gain_ref[...]
        both = plain = grads
        if wide:
            narrow = refs[0][...]
            lanes = lax.broadcasted_iota(jnp.int32, narrow.shape, 1)
            narrow = jnp.where(lanes == 17, refs[1][...] + term, narrow)
            high, rest = split_parts(narrow)
            both = jnp.concatenate([both, high, rest], axis=-1)
            plain = jnp.concatenate([plain, narrow, jnp.zeros_like(narrow)], axis=-1)
        else:
            refs[-1][...] = term
        second = part_ref[0] == 1
        for i in range(runs):
            at = 2 * i * own_rows
            first = slice(at, at + own_rows)
            other = slice(at + own_rows, at + 2 * own_rows)
            to = slice(i * own_rows, (i + 1) * own_rows)
            kept_ref[to] = jnp.where(second, plain[other], plain[first])
            sent_ref[to] = jnp.where(second, both[first], both[other]).astype(jnp.bfloat16)

    full = cols + (THIN if wide else 0)
    out = lambda kind: jax.ShapeDtypeStruct((width // 2, full), kind)
    row = lambda size: pl.BlockSpec((block // 2, size), lambda i: (i, 0))
    here = lambda size: pl.BlockSpec((block, size), lambda i: (i, 0))
    return call(
        kernel,
        "dense",
        [part, rows_h, grads, weight, gain] + (list(narrow) if wide else []),
        [
            pl.BlockSpec(memory_space=pltpu.SMEM),
            pl.BlockSpec((length, block), lambda i: (0, i)),
            whole(grads),
            here(weight.shape[1]),
            here(1),
        ]
        + ([here(HALF_THIN), here(1)] if wide else []),
        [row(full), row(full)] + ([] if wide else [here(1)]),
        [out(jnp.float32), out(jnp.bfloat16)]
        + ([] if wide else [jax.ShapeDtypeStruct((width, 1), jnp.float32)]),
        grid=(width // block,),
        mib=40,
    )


def dense_sum(kept, got):
    rows, full = kept.shape
    cols = full - THIN
    block = rows // 4

    def kernel(kept_ref, got_ref, out_ref):
        got = got_ref[...].astype(jnp.float32)
        out_ref[:, :cols] = (kept_ref[:, :cols] + got[:, :cols]).astype(jnp.bfloat16)
        narrow = kept_ref[:, cols : cols + HALF_THIN]
        narrow = narrow + got[:, cols : cols + HALF_THIN] + got[:, cols + HALF_THIN :]
        out_ref[:, cols:] = jnp.concatenate(split_parts(narrow), axis=-1).astype(jnp.bfloat16)

    row = pl.BlockSpec((block, full), lambda i: (i, 0))
    return call(
        kernel,
        "dense_sum",
        [kept, got],
        [row, row],
        [row],
        [jax.ShapeDtypeStruct((rows, full), jnp.bfloat16)],
        grid=(4,),
        mib=16,
    )[0]


def body(
    tokens,
    cotangent,
    attn_gain,
    w_query,
    w_key,
    w_value,
    w_out,
    query_gain,
    key_gain,
    ffn_gain,
    router,
    w_gate,
    w_up,
    w_down,
    routes,
    priority,
    positions,
):
    low = jnp.bfloat16
    ctx_count = 2 * CHIPS
    place = lax.axis_index("chip") * 2 + lax.axis_index("core")
    part = lax.axis_index("fsdp")
    tok_rows, model_width = tokens.shape[1:]
    half_width = model_width // 2
    head_dim = HEAD_DIM
    length = tok_rows * ctx_count
    capacity = 9 * tok_rows
    score_scale = head_dim ** (-0.5)
    per_half = ctx_count // 2
    expert_count = router.shape[1]

    def joined(mine, other, axis):
        return jnp.where(
            part == 0,
            jnp.concatenate([mine, other], axis=axis),
            jnp.concatenate([other, mine], axis=axis),
        )

    def head_rows(matrix, width):
        return lax.dynamic_slice_in_dim(matrix, (place % per_half) * width, width, 0)

    small = jnp.concatenate(
        [
            router.T,
            attn_gain[None],
            ffn_gain[None],
            jnp.concatenate(
                [
                    head_rows(query_gain, head_dim),
                    head_rows(key_gain, head_dim),
                    jnp.zeros((half_width - 2 * head_dim,), low),
                ]
            )[None],
        ],
        axis=0,
    )
    qkv_mine = jnp.concatenate(
        [
            lax.dynamic_slice_in_dim(w, place * head_dim, head_dim, 1)
            for w in (w_query, w_key, w_value)
        ],
        axis=1,
    )
    out_mine = head_rows(w_out, head_dim)

    hot = routes[0][:, :, None] == jnp.arange(expert_count, dtype=jnp.int32)[None, None, :]
    levels = jnp.sum(jnp.where(hot, priority[0][:, :, None] - LEVELS, 0), axis=1) + LEVELS
    spot = positions[0]
    line = jnp.concatenate(
        [spot // 128, spot % 128, jnp.full((model_width - 2 * tok_rows,), place, jnp.int32)]
    )
    tags = jnp.concatenate(
        [
            levels.T.reshape(1, model_width),
            line[None],
            jnp.zeros((EXTRA - 2, model_width), jnp.int32),
        ],
        axis=0,
    ).astype(low)

    inputs = tokens[0].astype(jnp.float32)
    inv_one = lax.rsqrt(jnp.mean(inputs * inputs, axis=-1, keepdims=True) + epsilon)
    first_rows = jnp.concatenate([tokens[0], tags], axis=0)
    place_one = place.astype(jnp.int32).reshape(1)
    ready = ()
    sum_parts, tag_parts = {}, {}

    def lin_job(step, blocks):
        def function():
            made = lin_chunk(
                step, blocks(), qkv_weight, g_attn[None], place_one, tok_rows, ready
            )
            return made

        return [], function

    def lin_keep(step, made):
        nonlocal ready
        ready = tuple(made[:2])
        sum_parts[step], tag_parts[step] = made[2][:2], made[3]

    def other_core(array):
        return (swap(array, "core"),)

    rows_one = Gather(first_rows)

    def to_other(*arrays):
        return [swap(array, "fsdp") for array in arrays]

    ((qkv_other, small_other),) = window([rows_one], loose=[([qkv_mine, small], to_other)])
    small_full = joined(small, small_other, 1)
    r_weight = small_full[:expert_count]
    g_attn = small_full[expert_count].astype(jnp.float32)
    g_ffn = small_full[expert_count + 1].astype(jnp.float32)
    here = part == place // per_half
    g_heads = jnp.where(here, small[expert_count + 2], small_other[expert_count + 2]).astype(
        jnp.float32
    )
    g_query, g_key = g_heads[:head_dim], g_heads[head_dim : 2 * head_dim]
    gain_col = g_attn[:, None]
    qkv_weight = joined(qkv_mine, qkv_other, 0)

    def expert_weights(_, *own):
        return [lax.all_gather(w, "fsdp", axis=k, tiled=True) for w, k in zip(own, (0, 0, 1))]

    made, expert_own = window(
        [rows_one],
        [lin_job(1, lambda: rows_one.now)],
        loose=[([qkv_other, w_gate[0], w_up[0], w_down[0]], expert_weights)],
    )
    gate_weight, up_weight, down_weight = expert_own
    lin_keep(1, made)
    made, (qkv_pair,) = window(
        [rows_one],
        [lin_job(2, lambda: rows_one.now), ([qkv_weight], other_core)],
    )
    lin_keep(2, made)
    made, (out_other,) = window(
        [rows_one], [lin_job(3, lambda: rows_one.now)], loose=[([out_mine], to_other)]
    )
    out_weight = jnp.where(here, out_mine, out_other)
    lin_keep(3, made)
    lin_keep(LAST, lin_job(LAST, lambda: rows_one.chunks[LAST])[1]())
    lin, all_h_one = ready
    all_tags = jnp.concatenate([tag_parts[step] for step in WIDE_CHUNKS], axis=0).reshape(
        ctx_count, EXTRA, tok_rows
    )

    def token_sums(lines, jobs):
        total, done = sum_all(by_place(lines.reshape(-1, CHIPS, 2, tok_rows), 1), jobs)
        return by_chunk(total, 1).reshape(-1, length).T / model_width, done

    def rank_job(all_tags):
        mine, owner = all_tags[:, 0], all_tags[:, 3, :1]
        order = owner * tok_rows + jnp.arange(tok_rows, dtype=jnp.float32)[None]
        mine = mine.reshape(length)
        code = mine * length + order.reshape(length)
        ranks = jnp.sum((code[None, :] < code[:, None]).astype(jnp.float32), axis=1)
        kept = (mine < LEVELS) & (ranks < capacity)
        return kept.astype(jnp.float32)[:, None], owner[:, 0].astype(jnp.int32)

    def rope_job(all_tags):
        spots = (all_tags[:, 1] * 128.0 + all_tags[:, 2]).reshape(-1)
        return [table[:, 0] for table in rope_tables(spots, head_dim)]

    square, ((cosine, sine_part),) = token_sums(
        jnp.concatenate([sum_parts[step] for step in WIDE_CHUNKS], axis=1),
        [([all_tags], rope_job)],
    )
    inverse = lax.rsqrt(square + epsilon)
    gains = jnp.stack([g_query, g_key], axis=0)
    q_rot, k_rot, v_low = rotate_rows(lin, inverse, gains, cosine, sine_part)

    heads = {}

    def attend_job(step):
        return [q_rot, k_rot, v_low], lambda queries, keys, values: attend_chunk(
            step, queries, keys, values, tok_rows, score_scale
        )

    def projected(step, made):
        return pair_product(
            made[2], swap(made[3], "core"), out_weight, out_pair, False, "project"
        )

    def first_job(queries, keys, values):
        made = attend_job(FAR)[1](queries, keys, values)
        return [*made, projected(FAR, made)]

    (out_pair,) = other_core(out_weight)
    grads_rows = Gather(cotangent[0])
    (*heads[FAR], far_terms), heads[FAR - 1], (kept, owners) = window(
        [grads_rows],
        [([q_rot, k_rot, v_low], first_job), attend_job(FAR - 1), ([all_tags], rank_job)],
    )

    def out_terms(step, *parts):
        return (far_terms if step == FAR else projected(step, parts)), None

    out_sum = Scatter(out_terms)
    for near in range(FAR - 1, -1, -1):
        out_sum.inputs = heads[near]
        jobs = [attend_job(near - 1)] if near else []
        held = [([gate_weight], lambda weight: (weight,))] if near == 2 else []
        made = window([out_sum], jobs + held)
        if held:
            (gate_weight,) = made[-1]
        if near:
            heads[near - 1] = made[0]
    mixed_low, lse = (
        jnp.concatenate([heads[step][k] for step in CHUNKS], axis=0) for k in range(2)
    )
    middle = inputs + out_sum.total

    h_two_f, inv_two = rms_forward(middle, g_ffn)
    h_two = h_two_f.astype(low)
    grad_out = cotangent[0].astype(jnp.float32)
    filled = ()
    mix_terms, dx_terms = {}, {}

    rows_two = Gather(h_two)
    window([rows_two])

    def expert_job(step, h_blocks, g_blocks):
        return [], lambda: expert_chunk(
            step,
            h_blocks(),
            g_blocks(),
            place_one,
            kept,
            r_weight,
            gate_weight,
            up_weight,
            down_weight,
            tok_rows,
            filled,
        )

    for step in list(range(1, FAR)) + [LAST]:
        if step == LAST:
            run = expert_job(step, lambda: rows_two.chunks[LAST], lambda: grads_rows.chunks[LAST])
            made = run[1]()
        else:
            run = expert_job(step, lambda: rows_two.now, lambda: grads_rows.now)
            (made,) = window([rows_two, grads_rows], [run])
        filled, terms = tuple(made[:5]), made[5:]
        if step == LAST:
            mix_terms[0], mix_terms[FAR] = terms[:2], terms[2:4]
            dx_terms[0], dx_terms[FAR] = terms[4:6], terms[6:]
        else:
            mix_terms[step], dx_terms[step] = terms[:2], terms[2:]
    all_h_two, all_grads, act_low, gate_grad, up_grad = filled

    def wgrad(left, right):
        return (contract_rows(left, right).astype(low),)

    def over_sequences(matrix, axis):
        return lax.psum_scatter(matrix, "fsdp", scatter_dimension=axis, tiled=True)

    logits = contract_cols(h_two, r_weight)
    row_max = jnp.max(logits, axis=-1, keepdims=True)
    exps_raw = jnp.exp(logits - row_max)
    router_probs = exps_raw / jnp.sum(exps_raw, axis=-1, keepdims=True)
    dx_sum = Scatter(lambda step: dx_terms[step])
    mix_sum = Scatter(lambda step: mix_terms[step])
    ((gate_wgrad,),) = window([dx_sum, mix_sum], [([all_h_two, gate_grad], wgrad)])
    s_gate = over_sequences(gate_wgrad, 0)
    ((up_wgrad,),) = window([dx_sum, mix_sum], [([all_h_two, up_grad], wgrad)])
    s_up = over_sequences(up_wgrad, 0)
    ((down_wgrad,),) = window([dx_sum], [([act_low, all_grads], wgrad)])
    s_down = over_sequences(down_wgrad, 1)
    window([dx_sum])
    hidden_sum = dx_sum.total

    prob_grad = jnp.sum(hidden_sum[tok_rows : tok_rows + 3], axis=0)
    prob_grad = prob_grad.reshape(expert_count, tok_rows).T
    logit_grad = router_probs * (
        prob_grad - jnp.sum(router_probs * prob_grad, axis=-1, keepdims=True)
    )
    hidden_grad = hidden_sum[:tok_rows] + precise(logit_grad, r_weight.astype(jnp.float32))
    norm_grad, ffn_gain_grad = rms_backward(middle, inv_two, g_ffn, hidden_grad)
    middle_grad = grad_out + norm_grad

    sofar = ()

    q_sums = {}
    rows_da = Gather(middle_grad.astype(low))

    def back_job(step, blocks):
        return [], lambda: attend_back_chunk(
            step,
            blocks(),
            q_rot,
            lse,
            k_rot,
            v_low,
            out_weight,
            lin,
            gains,
            cosine,
            sine_part,
            tok_rows,
            score_scale,
            sofar,
            step == FAR,
        )

    def widen(array):
        return (array.astype(jnp.float32),)

    def narrow_job(h_two, logit_grad, ffn_gain_grad):
        return (
            jnp.concatenate(
                [
                    precise(h_two.astype(jnp.float32).T, logit_grad),
                    ffn_gain_grad[:, None],
                    jnp.zeros((model_width, HALF_THIN - expert_count - 1), jnp.float32),
                ],
                axis=1,
            ),
        )

    besides = {0: [], 1: [mix_sum], 2: [], 3: []}
    also = {1: [([h_two, logit_grad, ffn_gain_grad], narrow_job), ([s_gate], widen)]}
    for step in range(FAR + 1):
        if step == FAR:
            *made, k_sums = back_job(step, lambda: rows_da.chunks[FAR])[1]()
        else:
            made, *wide = window(
                [rows_da] + besides[step], [back_job(step, lambda: rows_da.now)] + also.get(step, [])
            )
            if step == 1:
                (narrow,), (s_gate,) = wide
        sofar, q_sums[step] = tuple(made[:4]), made[4]
    dq, all_branch, dk, dv = sofar

    def out_job(mixed_low, all_branch):
        return (contract_rows(mixed_low, all_branch),)

    own_rows = model_width // (2 * ctx_count)
    part_one = part.astype(jnp.int32).reshape(1)

    def value_job(all_h_one, dv):
        return dense_chunk(
            all_h_one, dv.astype(low), qkv_weight, (2 * head_dim, head_dim), gain_col, None,
            part_one, own_rows,
        )

    along, ((v_kept, v_sent, v_term), mixed) = token_sums(
        jnp.stack(
            [jnp.concatenate([q_sums[step][0] for step in CHUNKS], axis=0), k_sums[0]], axis=0
        ),
        [
            ([all_h_one, dv], value_job),
            mix_sum.job(),
        ],
    )
    mix_sum.take(mixed)
    layer_out = (middle + mix_sum.total).astype(low)
    lin_grad, lin_mine, lin_theirs = lin_back_rows(dq, dk, dv, lin, inverse, along, tok_rows)
    lin_theirs = swap(lin_theirs, "core")


    def pick(blocks, index):
        return lax.dynamic_index_in_dim(blocks, index, 1, False)

    def dense_job(all_h_one, lin_grad, *narrow):
        return dense_chunk(
            all_h_one, lin_grad[:, : 2 * head_dim], qkv_weight, (0, 2 * head_dim), gain_col, narrow,
            part_one, own_rows,
        )

    def out_swap_job(out_sent, dq, dk, lin):
        gain_rows = jnp.stack(
            [
                jnp.sum(
                    grad * lin[:, k * head_dim : (k + 1) * head_dim] * inverse[:, k : k + 1], axis=0
                )
                for k, grad in enumerate((dq, dk))
            ],
            axis=0,
        )
        gain_rows = (gain_rows / gains).reshape(2, 2, own_rows)
        return swap(out_sent, "fsdp"), swap(pick(gain_rows, 1 - part), "fsdp"), pick(gain_rows, part)

    def h_terms(step, lin_mine, lin_theirs):
        return (
            pair_product(lin_mine, lin_theirs, qkv_weight, qkv_pair, True, "h_terms", step),
            None,
        )

    h_sum = Scatter(h_terms, [lin_mine, lin_theirs])
    def swap_job(sent):
        return (swap(sent, "fsdp"),)

    def owners_job(payload):
        blocks = payload.reshape(ctx_count, own_rows, -1)
        return (lax.all_to_all(blocks, ("chip", "core"), 0, 0, tiled=True),)

    (kept, sent), (s_down,), (v_got,) = window(
        [h_sum],
        [([all_h_one, lin_grad, narrow, v_term], dense_job), ([s_down], widen)],
        loose=[([v_sent], swap_job)],
    )
    (got,), (out_wgrad,), (v_received,) = window(
        [h_sum],
        [([sent], swap_job), ([mixed_low, all_branch], out_job)],
        loose=[([(v_kept + v_got.astype(jnp.float32)).astype(low)], owners_job)],
    )
    out_rows = out_wgrad.reshape(1, 2, own_rows, model_width)
    (s_up,), (received,), (out_got, gain_got, gain_kept) = window(
        [h_sum],
        [([s_up], widen)],
        loose=[
            ([kept, got], lambda kept, got: owners_job(dense_sum(kept, got))),
            ([pick(out_rows, 1 - part)[0].astype(low), dq, dk, lin], out_swap_job),
        ],
    )

    def out_done_job(own, out_got, gain_kept, gain_got):
        return own + out_got.astype(jnp.float32), gain_kept + gain_got

    (v_received,), (received,), (d_out, gain_sum) = window(
        [h_sum],
        [
            ([], lambda: (v_received,)),
            ([], lambda: (received,)),
            ([pick(out_rows, part)[0], out_got, gain_kept, gain_got], out_done_job),
        ],
    )
    h_grad = h_sum.total
    d_qgain, d_kgain = gain_sum[0], gain_sum[1]
    s_gate, s_up, s_down = s_gate[None], s_up[None], s_down[None]
    in_norm_grad, _ = rms_backward(inputs, inv_one, g_attn, h_grad)
    input_grad = (middle_grad + in_norm_grad).astype(low)
    d_query, d_key, d_value = (
        columns.transpose(1, 0, 2).reshape(own_rows, model_width).astype(jnp.float32)
        for columns in (received[:, :, :head_dim], received[:, :, head_dim : 2 * head_dim], v_received)
    )
    thin_sum = jnp.sum(received[:, :, 2 * head_dim :].astype(jnp.float32), axis=0)
    thin_sum = thin_sum[:, :HALF_THIN] + thin_sum[:, HALF_THIN:]
    d_router = thin_sum[:, :expert_count]
    d_ffn, d_attn = thin_sum[:, expert_count], thin_sum[:, expert_count + 1]
    return (
        layer_out[None],
        input_grad[None],
        d_attn,
        d_query,
        d_key,
        d_value,
        d_out,
        d_qgain,
        d_kgain,
        d_ffn,
        d_router,
        s_gate,
        s_up,
        s_down,
    )


def specs_of(ctx):
    rows, both = P("fsdp", ctx, None), ctx + ("fsdp",)
    dense = P("fsdp", None)
    ins = (
        rows,
        rows,
        P("fsdp"),
        dense,
        dense,
        dense,
        dense,
        P("fsdp"),
        P("fsdp"),
        P("fsdp"),
        dense,
        P(ctx, "fsdp", None),
        P(ctx, "fsdp", None),
        P(ctx, None, "fsdp"),
        rows,
        rows,
        P("fsdp", ctx),
    )
    line, matrix = P(both), P(both, None)
    outs = (
        rows,
        rows,
        line,
        matrix,
        matrix,
        matrix,
        matrix,
        line,
        line,
        line,
        matrix,
        P(ctx, "fsdp", None),
        P(ctx, "fsdp", None),
        P(ctx, None, "fsdp"),
    )
    return ins, outs


def solution(mesh):
    ctx_count, fsdp_count = mesh.shape["ctx"], mesh.shape["fsdp"]

    def whole(*arrays):
        heads = arrays[0].shape[2] // HEAD_DIM
        experts = arrays[10].shape[1]
        if ctx_count == 2 * CHIPS == heads == experts and fsdp_count == 2:
            chips = Mesh(mesh.devices.reshape(-1, 2, 2), ("chip", "core", "fsdp"))
            run, grid, ctx = body, chips, ("chip", "core")
        else:
            run, grid, ctx = general_body, mesh, ("ctx",)
        ins, outs = specs_of(ctx)
        return jax.shard_map(run, mesh=grid, in_specs=ins, out_specs=outs, check_vma=False)(*arrays)

    return whole
```

```python
import math

import jax
import jax.numpy as jnp
from jax import lax
from jax.experimental import pallas as pl
from jax.experimental.pallas import tpu as pltpu
from jax.sharding import Mesh
from jax.sharding import PartitionSpec as P

HEAD_DIM = 128
LEVELS = 4


epsilon = 1e-05
rope_base = 50000.0


def prefix(part, axis, combine, identity):
    place = lax.axis_index(axis)
    gathered = lax.all_gather(part, axis)
    state = jnp.zeros_like(part) + jnp.asarray(identity, part.dtype)

    def one(turn, state):
        return combine(state, lax.dynamic_index_in_dim(gathered, turn, 0, False))

    return lax.fori_loop(0, place, one, state)


def product(left, right):
    return jnp.dot(left, right, preferred_element_type=jnp.float32)


def precise(left, right):
    return jnp.dot(left, right, precision=lax.Precision.HIGHEST, preferred_element_type=jnp.float32)


def contract_rows(left, right):
    return lax.dot_general(
        left, right, (((0,), (0,)), ((), ())), preferred_element_type=jnp.float32
    )


def contract_cols(left, right):
    return lax.dot_general(
        left, right, (((1,), (1,)), ((), ())), preferred_element_type=jnp.float32
    )


def rms_forward(matrix, gain_row):
    inverse = lax.rsqrt(jnp.mean(matrix * matrix, axis=-1, keepdims=True) + epsilon)
    return (matrix * inverse * gain_row, inverse)


def rms_backward(matrix, inverse, gain_row, upstream):
    scaled = upstream * gain_row
    along = jnp.mean(scaled * matrix, axis=-1, keepdims=True)
    grad_rows = inverse * scaled - matrix * inverse * inverse * inverse * along
    grad_gain = jnp.sum(upstream * matrix * inverse, axis=0)
    return (grad_rows, grad_gain)


def rope_tables(position_ids, head_dim):
    half_dim = head_dim // 2
    inverse = rope_base ** (-(jnp.arange(half_dim, dtype=jnp.float32) * 2.0) / head_dim)
    angles = position_ids.astype(jnp.float32)[:, None] * inverse[None, :]
    return (jnp.cos(angles)[:, None, :], jnp.sin(angles)[:, None, :])


def rotate(matrix, cosine, sine_part, head_dim, turn_sign):
    count_rows = matrix.shape[0]
    by_head = matrix.reshape(count_rows, -1, head_dim)
    half_dim = head_dim // 2
    lower_half = by_head[..., :half_dim]
    upper_half = by_head[..., half_dim:]
    turned = jnp.concatenate(
        [
            lower_half * cosine - turn_sign * upper_half * sine_part,
            upper_half * cosine + turn_sign * lower_half * sine_part,
        ],
        axis=-1,
    )
    return turned.reshape(count_rows, -1)


def add_counts(earlier_part, later_part):
    return earlier_part + later_part


def score_block(query_part, key_part, score_scale):
    return (
        jnp.einsum("qhd,khd->hqk", query_part, key_part, preferred_element_type=jnp.float32)
        * score_scale
    )


def grad_block(query_part, dout_part, lse_part, delta_part, key_part, value_part, score_scale):
    probs = jnp.exp(score_block(query_part, key_part, score_scale) - lse_part)
    prob_low = probs.astype(jnp.bfloat16)
    dprob = jnp.einsum("qhd,khd->hqk", dout_part, value_part, preferred_element_type=jnp.float32)
    dscore = (probs * (dprob - delta_part)).astype(jnp.bfloat16)
    return (prob_low, dscore)


def general_body(
    tokens,
    cotangent,
    attn_gain,
    w_query,
    w_key,
    w_value,
    w_out,
    query_gain,
    key_gain,
    ffn_gain,
    router,
    w_gate,
    w_up,
    w_down,
    routes,
    priority,
    positions,
):
    ctx_count = lax.axis_size("ctx")
    (
        g_attn,
        q_weight,
        k_weight,
        v_weight,
        o_weight,
        g_query,
        g_key,
        g_ffn,
        r_weight,
        gate_full,
        up_full,
        down_full,
    ) = (
        lax.all_gather(attn_gain, "fsdp", axis=0, tiled=True),
        lax.all_gather(w_query, "fsdp", axis=0, tiled=True),
        lax.all_gather(w_key, "fsdp", axis=0, tiled=True),
        lax.all_gather(w_value, "fsdp", axis=0, tiled=True),
        lax.all_gather(w_out, "fsdp", axis=0, tiled=True),
        lax.all_gather(query_gain, "fsdp", axis=0, tiled=True),
        lax.all_gather(key_gain, "fsdp", axis=0, tiled=True),
        lax.all_gather(ffn_gain, "fsdp", axis=0, tiled=True),
        lax.all_gather(router, "fsdp", axis=0, tiled=True),
        lax.all_gather(w_gate, "fsdp", axis=1, tiled=True),
        lax.all_gather(w_up, "fsdp", axis=1, tiled=True),
        lax.all_gather(w_down, "fsdp", axis=2, tiled=True),
    )
    gate_weight = gate_full[0]
    up_weight = up_full[0]
    down_weight = down_full[0]
    tok_rows = tokens.shape[1]
    model_width = tokens.shape[2]
    head_dim = HEAD_DIM
    head_count = model_width // head_dim
    length = tok_rows * ctx_count
    top_k = routes.shape[2]
    capacity = 9 * tok_rows
    send_rows = 2 * tok_rows * top_k // ctx_count
    key_block = math.gcd(length, 1024)
    block_count = length // key_block
    score_scale = head_dim ** (-0.5)
    inputs = tokens[0].astype(jnp.float32)
    normed, inv_one = rms_forward(inputs, g_attn)
    h_one = normed.astype(jnp.bfloat16)
    q_lin = product(h_one, q_weight)
    k_lin = product(h_one, k_weight)
    v_lin = product(h_one, v_weight)
    cosine, sine_part = rope_tables(positions[0], head_dim)
    q_normed, inv_query = rms_forward(q_lin, g_query)
    k_normed, inv_key = rms_forward(k_lin, g_key)
    q_rot = rotate(q_normed, cosine, sine_part, head_dim, 1.0).astype(jnp.bfloat16)
    k_rot = rotate(k_normed, cosine, sine_part, head_dim, 1.0).astype(jnp.bfloat16)
    v_low = v_lin.astype(jnp.bfloat16)
    all_keys, all_values = (
        lax.all_gather(k_rot, "ctx", axis=0, tiled=True),
        lax.all_gather(v_low, "ctx", axis=0, tiled=True),
    )
    q_heads = q_rot.reshape(tok_rows, head_count, head_dim)

    def key_slice(block_id):
        start = block_id * key_block
        key_part = lax.dynamic_slice_in_dim(all_keys, start, key_block, 0).reshape(
            key_block, head_count, head_dim
        )
        value_part = lax.dynamic_slice_in_dim(all_values, start, key_block, 0).reshape(
            key_block, head_count, head_dim
        )
        return (key_part, value_part)

    def lse_step(carry, block_id):
        run_max, run_total = carry
        key_part, value_part = key_slice(block_id)
        scores = score_block(q_heads, key_part, score_scale)
        new_max = jnp.maximum(run_max, jnp.max(scores, axis=-1, keepdims=True))
        run_total = run_total * jnp.exp(run_max - new_max) + jnp.sum(
            jnp.exp(scores - new_max), axis=-1, keepdims=True
        )
        return ((new_max, run_total), None)

    start_max = jnp.full((head_count, tok_rows, 1), -jnp.inf, jnp.float32)
    start_total = jnp.zeros((head_count, tok_rows, 1), jnp.float32)
    (run_max, run_total), _ = lax.scan(lse_step, (start_max, start_total), jnp.arange(block_count))
    lse = run_max + jnp.log(run_total)

    def out_step(acc, block_id):
        key_part, value_part = key_slice(block_id)
        probs = jnp.exp(score_block(q_heads, key_part, score_scale) - lse).astype(jnp.bfloat16)
        return (
            acc + jnp.einsum("hqk,khd->qhd", probs, value_part, preferred_element_type=jnp.float32),
            None,
        )

    attended_heads, _ = lax.scan(
        out_step, jnp.zeros((tok_rows, head_count, head_dim), jnp.float32), jnp.arange(block_count)
    )
    attended = attended_heads.reshape(tok_rows, model_width)
    mixed_low = attended.astype(jnp.bfloat16)
    middle = inputs + product(mixed_low, o_weight)
    h_two_f, inv_two = rms_forward(middle, g_ffn)
    h_two = h_two_f.astype(jnp.bfloat16)
    logits = product(h_two, r_weight)
    row_max = jnp.max(logits, axis=-1, keepdims=True)
    exps_raw = jnp.exp(logits - row_max)
    router_probs = exps_raw / jnp.sum(exps_raw, axis=-1, keepdims=True)
    route_ids = routes[0]
    level_ids = priority[0]
    pair_code = level_ids * ctx_count + route_ids
    code_table = (
        pair_code[:, :, None] == jnp.arange(LEVELS * ctx_count, dtype=jnp.int32)[None, None, :]
    ).astype(jnp.float32)
    per_token = jnp.sum(code_table, axis=1)
    before_local = jnp.cumsum(per_token, axis=0) - per_token
    local_total = jnp.sum(per_token, axis=0)
    earlier = prefix(local_total, "ctx", add_counts, jnp.zeros_like(local_total))
    totals = lax.psum(local_total, "ctx")
    level_totals = totals.reshape(LEVELS, ctx_count)
    level_base = (jnp.cumsum(level_totals, axis=0) - level_totals).reshape(-1)
    offsets = before_local + (earlier + level_base)[None, :]
    pair_rank = jnp.sum(code_table * offsets[:, None, :], axis=-1).astype(jnp.int32)
    is_kept = pair_rank < capacity
    expert_hot = (
        route_ids[:, :, None] == jnp.arange(ctx_count, dtype=jnp.int32)[None, None, :]
    ).astype(jnp.float32)
    per_expert = jnp.sum(expert_hot, axis=1)
    local_before = jnp.cumsum(per_expert, axis=0) - per_expert
    local_slot = jnp.sum(expert_hot * local_before[:, None, :], axis=-1).astype(jnp.int32)
    send_index = (route_ids * send_rows + local_slot).reshape(-1)
    pair_count = tok_rows * top_k
    pair_of_slot = (
        jnp.full((ctx_count * send_rows,), pair_count, jnp.int32)
        .at[send_index]
        .set(jnp.arange(pair_count, dtype=jnp.int32))
    )
    slot_target = jnp.where(is_kept, pair_rank, capacity).reshape(-1)
    target_pad = jnp.concatenate([slot_target, jnp.full((1,), capacity, jnp.int32)], axis=0)
    send_slots = target_pad[pair_of_slot].reshape(ctx_count, send_rows)
    h_pad = jnp.concatenate([h_two, jnp.zeros((1, model_width), jnp.bfloat16)], axis=0)
    send_tokens = h_pad[pair_of_slot // top_k].reshape(ctx_count, send_rows, model_width)
    got_tokens, got_slots = (
        lax.all_to_all(send_tokens, "ctx", split_axis=0, concat_axis=0, tiled=True),
        lax.all_to_all(send_slots, "ctx", split_axis=0, concat_axis=0, tiled=True),
    )
    received_count = ctx_count * send_rows
    slots_flat = got_slots.reshape(-1)
    row_of_slot = (
        jnp.full((capacity,), received_count, jnp.int32)
        .at[slots_flat]
        .set(jnp.arange(received_count, dtype=jnp.int32), mode="drop")
    )
    got_pad = jnp.concatenate(
        [
            got_tokens.reshape(received_count, model_width),
            jnp.zeros((1, model_width), jnp.bfloat16),
        ],
        axis=0,
    )
    expert_in = got_pad[row_of_slot]
    gate_lin = product(expert_in, gate_weight)
    up_lin = product(expert_in, up_weight)
    sig_gate = jax.nn.sigmoid(gate_lin)
    silu_val = gate_lin * sig_gate
    swiglu = (silu_val * up_lin).astype(jnp.bfloat16)
    expert_out = product(swiglu, down_weight).astype(jnp.bfloat16)
    out_pad = jnp.concatenate([expert_out, jnp.zeros((1, model_width), jnp.bfloat16)], axis=0)
    back_rows = out_pad[slots_flat].reshape(ctx_count, send_rows, model_width)
    returned = lax.all_to_all(back_rows, "ctx", split_axis=0, concat_axis=0, tiled=True)
    returned_pad = jnp.concatenate(
        [
            returned.reshape(ctx_count * send_rows, model_width),
            jnp.zeros((1, model_width), jnp.bfloat16),
        ],
        axis=0,
    )
    pair_out = returned_pad[send_index].reshape(tok_rows, top_k, model_width)
    chosen = jnp.sum(router_probs[:, None, :] * expert_hot, axis=-1)
    share = jnp.where(is_kept, chosen, 0.0)
    mixture = jnp.einsum("tk,tkd->td", share, pair_out, preferred_element_type=jnp.float32)
    final_rows = middle + mixture
    layer_out = final_rows.astype(jnp.bfloat16)
    grad_out = cotangent[0].astype(jnp.float32)
    routed_grad = (share[:, :, None] * grad_out[:, None, :]).astype(jnp.bfloat16)
    share_grad = jnp.where(
        is_kept,
        jnp.einsum("tkd,td->tk", pair_out, grad_out, preferred_element_type=jnp.float32),
        0.0,
    )
    prob_grad = jnp.sum(expert_hot * share_grad[:, :, None], axis=1)
    logit_grad = router_probs * (
        prob_grad - jnp.sum(router_probs * prob_grad, axis=-1, keepdims=True)
    )
    routed_pad = jnp.concatenate(
        [routed_grad.reshape(pair_count, model_width), jnp.zeros((1, model_width), jnp.bfloat16)],
        axis=0,
    )
    send_grads = routed_pad[pair_of_slot].reshape(ctx_count, send_rows, model_width)
    got_grads = lax.all_to_all(send_grads, "ctx", split_axis=0, concat_axis=0, tiled=True)
    grad_pad = jnp.concatenate(
        [got_grads.reshape(received_count, model_width), jnp.zeros((1, model_width), jnp.bfloat16)],
        axis=0,
    )
    out_grad = grad_pad[row_of_slot]
    act_grad = contract_cols(out_grad, down_weight)
    down_wgrad = contract_rows(swiglu, out_grad)
    gate_grad = (act_grad * up_lin * sig_gate * (1.0 + gate_lin * (1.0 - sig_gate))).astype(
        jnp.bfloat16
    )
    up_grad = (act_grad * silu_val).astype(jnp.bfloat16)
    in_grad = (contract_cols(gate_grad, gate_weight) + contract_cols(up_grad, up_weight)).astype(
        jnp.bfloat16
    )
    gate_wgrad = contract_rows(expert_in, gate_grad)
    up_wgrad = contract_rows(expert_in, up_grad)
    in_pad = jnp.concatenate([in_grad, jnp.zeros((1, model_width), jnp.bfloat16)], axis=0)
    back_grads = in_pad[slots_flat].reshape(ctx_count, send_rows, model_width)
    pair_grads = lax.all_to_all(back_grads, "ctx", split_axis=0, concat_axis=0, tiled=True)
    pair_pad = jnp.concatenate(
        [
            pair_grads.reshape(ctx_count * send_rows, model_width),
            jnp.zeros((1, model_width), jnp.bfloat16),
        ],
        axis=0,
    )
    token_pair = pair_pad[send_index].reshape(tok_rows, top_k, model_width)
    hidden_grad = jnp.sum(token_pair.astype(jnp.float32), axis=1) + precise(
        logit_grad, r_weight.astype(jnp.float32).T
    )
    router_wgrad = precise(h_two.astype(jnp.float32).T, logit_grad)
    norm_grad, ffn_gain_grad = rms_backward(middle, inv_two, g_ffn, hidden_grad)
    middle_grad = grad_out + norm_grad
    branch_grad = middle_grad.astype(jnp.bfloat16)
    out_wgrad = contract_rows(mixed_low, branch_grad)
    mixed_grad = contract_cols(branch_grad, o_weight).astype(jnp.bfloat16)
    dout_heads = mixed_grad.reshape(tok_rows, head_count, head_dim)
    delta = jnp.sum(dout_heads.astype(jnp.float32) * attended_heads, axis=-1).T[:, :, None]

    def back_step(dq_acc, block_id):
        key_part, value_part = key_slice(block_id)
        prob_low, dscore = grad_block(
            q_heads, dout_heads, lse, delta, key_part, value_part, score_scale
        )
        dq_acc = dq_acc + jnp.einsum(
            "hqk,khd->qhd", dscore, key_part, preferred_element_type=jnp.float32
        )
        dk_part = jnp.einsum(
            "hqk,qhd->khd", dscore, q_heads, preferred_element_type=jnp.float32
        ).reshape(key_block, model_width)
        dv_part = jnp.einsum(
            "hqk,qhd->khd", prob_low, dout_heads, preferred_element_type=jnp.float32
        ).reshape(key_block, model_width)
        return (dq_acc, jnp.concatenate([dk_part, dv_part], axis=1))

    dq_heads, kv_terms = lax.scan(
        back_step, jnp.zeros((tok_rows, head_count, head_dim), jnp.float32), jnp.arange(block_count)
    )
    kv_mine = lax.psum_scatter(
        kv_terms.reshape(length, 2 * model_width), "ctx", scatter_dimension=0, tiled=True
    )
    key_grad = kv_mine[:, :model_width] * score_scale
    value_grad = kv_mine[:, model_width:]
    v_lin_low = value_grad.astype(jnp.bfloat16)
    q_grad = dq_heads.reshape(tok_rows, model_width) * score_scale
    q_back = rotate(q_grad, cosine, sine_part, head_dim, -1.0)
    k_back = rotate(key_grad, cosine, sine_part, head_dim, -1.0)
    q_lin_grad, query_gain_grad = rms_backward(q_lin, inv_query, g_query, q_back)
    k_lin_grad, key_gain_grad = rms_backward(k_lin, inv_key, g_key, k_back)
    q_lin_low = q_lin_grad.astype(jnp.bfloat16)
    k_lin_low = k_lin_grad.astype(jnp.bfloat16)
    h_grad = (
        contract_cols(q_lin_low, q_weight)
        + contract_cols(k_lin_low, k_weight)
        + contract_cols(v_lin_low, v_weight)
    )
    query_wgrad = contract_rows(h_one, q_lin_low)
    key_wgrad = contract_rows(h_one, k_lin_low)
    value_wgrad = contract_rows(h_one, v_lin_low)
    in_norm_grad, attn_gain_grad = rms_backward(inputs, inv_one, g_attn, h_grad)
    input_grad = (middle_grad + in_norm_grad).astype(jnp.bfloat16)
    s_gate, s_up, s_down = (
        lax.psum_scatter(
            gate_wgrad[None].astype(jnp.bfloat16), "fsdp", scatter_dimension=1, tiled=True
        ).astype(jnp.float32),
        lax.psum_scatter(
            up_wgrad[None].astype(jnp.bfloat16), "fsdp", scatter_dimension=1, tiled=True
        ).astype(jnp.float32),
        lax.psum_scatter(
            down_wgrad[None].astype(jnp.bfloat16), "fsdp", scatter_dimension=2, tiled=True
        ).astype(jnp.float32),
    )
    d_attn, d_query, d_key, d_value, d_out, d_qgain, d_kgain, d_ffn, d_router = (
        lax.psum_scatter(attn_gain_grad, ("ctx", "fsdp"), scatter_dimension=0, tiled=True),
        lax.psum_scatter(query_wgrad, ("ctx", "fsdp"), scatter_dimension=0, tiled=True),
        lax.psum_scatter(key_wgrad, ("ctx", "fsdp"), scatter_dimension=0, tiled=True),
        lax.psum_scatter(value_wgrad, ("ctx", "fsdp"), scatter_dimension=0, tiled=True),
        lax.psum_scatter(out_wgrad, ("ctx", "fsdp"), scatter_dimension=0, tiled=True),
        lax.psum_scatter(query_gain_grad, ("ctx", "fsdp"), scatter_dimension=0, tiled=True),
        lax.psum_scatter(key_gain_grad, ("ctx", "fsdp"), scatter_dimension=0, tiled=True),
        lax.psum_scatter(ffn_gain_grad, ("ctx", "fsdp"), scatter_dimension=0, tiled=True),
        lax.psum_scatter(router_wgrad, ("ctx", "fsdp"), scatter_dimension=0, tiled=True),
    )
    return (
        layer_out[None],
        input_grad[None],
        d_attn,
        d_query,
        d_key,
        d_value,
        d_out,
        d_qgain,
        d_kgain,
        d_ffn,
        d_router,
        s_gate,
        s_up,
        s_down,
    )


RING = [0, 2, 4, 6, 7, 5, 3, 1]
CHIPS = len(RING)
FAR = CHIPS // 2
EXTRA = 8
PLACES = [1, 7, 2, 6, 3, 5, 0, 4]
CHUNKS = {1: (0, 2), 2: (2, 2), 3: (4, 2), 0: (6, 1), FAR: (7, 1)}
LAST = -1
WIDE_CHUNKS = {1: (0, 2), 2: (2, 2), 3: (4, 2), LAST: (6, 2)}


BRIEF = pl.CostEstimate(flops=0, bytes_accessed=0, transcendentals=0)


def swap(array, axis):
    return lax.ppermute(array, axis, [(0, 1), (1, 0)])


def shift(array, by):
    pairs = [(RING[i], RING[(i + by) % CHIPS]) for i in range(CHIPS)]
    return lax.ppermute(array, "chip", pairs)


def fence(*groups):
    flat = lax.optimization_barrier(tuple(array for group in groups for array in group))
    out, at = [], 0
    for group in groups:
        out.append(list(flat[at : at + len(group)]))
        at += len(group)
    return out


def open_jobs(carried, jobs):
    opened = fence(carried, *[list(inputs) for inputs, _ in jobs])
    return opened[0], [(ins, function) for ins, (_, function) in zip(opened[1:], jobs)]


def run_jobs(jobs):
    return [list(function(*inputs)) for inputs, function in jobs]


class Gather:
    def __init__(self, block, far_by=0):
        self.moving = {1: block, -1: block}
        self.cut = block.shape[0] // 2 // 8 * 8
        self.far_by = far_by
        self.fresh = [block]
        self.step = 0
        self.chunks = {}

    def job(self):
        moving, ways = self.moving, [1, -1]
        if self.step + 1 == FAR and self.far_by:
            ways = [self.far_by]
        elif self.step + 1 == FAR:
            moving = {1: moving[1][: self.cut], -1: moving[-1][self.cut :]}

        def function(*arrays):
            moved = [shift(array, by) for array, by in zip(arrays, ways)]
            self.now = [x for block in arrays[len(ways) :] for x in (block, swap(block, "core"))]
            return [*moved, *self.now]

        return [moving[by] for by in ways] + self.fresh, function

    def take(self, results):
        self.step += 1
        if self.step == FAR:
            count = 1 if self.far_by else 2
            last, self.chunks[FAR - 1] = results[:count], list(results[count:])
            last = jnp.concatenate(last, axis=0) if count == 2 else last[0]
            self.chunks[FAR] = [last, swap(last, "core")]
            self.chunks[LAST] = self.chunks[0] + self.chunks[FAR]
            return
        self.moving[1], self.moving[-1], *self.chunks[self.step - 1] = results
        self.fresh = [self.moving[-1], self.moving[1]]


class Scatter:
    def __init__(self, make, inputs=(), ready=False, far_by=0):
        self.make, self.inputs, self.ready, self.far_by = make, list(inputs), ready, far_by
        self.step = 0
        mine, other = make(FAR, *self.inputs)
        first = mine
        if other is not None:
            first = mine.astype(jnp.float32) + swap(other, "core").astype(jnp.float32)
            first = first.astype(jnp.bfloat16)
        self.rows = first.shape[0]
        self.cut = self.rows // 2 // 8 * 8
        self.carried = [first] if far_by else [first[: self.cut], first[self.cut :]]

    def job(self):
        near = FAR - self.step - 1
        count = len(self.carried)
        ways = [self.far_by] if count == 1 else [1, -1]

        def function(*arrays):
            moved = [shift(array, by) for array, by in zip(arrays, ways)]
            mine, other = self.make(near, *arrays[count:])
            self.mine = mine
            terms = [] if self.ready else [mine]
            return moved + terms + ([] if other is None else [swap(other, "core")])

        return self.carried + self.inputs, function

    def take(self, results):
        self.step += 1
        count = len(self.carried)
        moved, terms = list(results[:count]), list(results[count:])
        if self.ready:
            terms = [self.mine] + terms

        def term(i):
            span = slice(i * self.rows, (i + 1) * self.rows)
            return sum(part[span].astype(jnp.float32) for part in terms)

        moved = [array.astype(jnp.float32) for array in moved]
        if self.step == FAR:
            self.last = [*results[:count], *terms]
            self.total = term(0) + moved[0] + moved[1]
            return
        if count == 1:
            moved = [moved[0], 0.0] if self.far_by == 1 else [0.0, moved[0]]
        elif self.step == 1:
            ahead, behind = moved
            ahead = jnp.concatenate([ahead, jnp.zeros_like(behind)], axis=0)
            behind = jnp.concatenate([jnp.zeros_like(ahead[: self.cut]), behind], axis=0)
            moved = [ahead, behind]
        self.carried = [
            (term(0) + moved[0]).astype(jnp.bfloat16),
            (term(1) + moved[1]).astype(jnp.bfloat16),
        ]


def window(items, jobs=(), loose=()):
    every = [item.job() for item in items] + list(jobs) + list(loose)
    _, opened = open_jobs([], every)
    results = run_jobs(opened)
    count = len(items) + len(jobs)
    results = fence(*results[:count]) + results[count:]
    for item, result in zip(items, results):
        item.take(result)
    return results[len(items) :]


def sum_all(values, jobs):
    (values,), jobs = open_jobs([values], jobs)
    core = lax.axis_index("core")
    both = values + swap(values[:, :, ::-1], "core")

    def heard(by):
        pairs = [
            (2 * RING[i] + c, 2 * RING[(i + (by if c == 0 else -by)) % CHIPS] + c)
            for i in range(CHIPS)
            for c in range(2)
        ]
        return lax.ppermute(both, ("chip", "core"), pairs)

    moved = [heard(by) for by in range(1, FAR + 1)]
    done = run_jobs(jobs)
    moved, *done = fence(moved, *done)
    total = jnp.where(core == 0, both, jnp.roll(moved[-1], -FAR, axis=1))
    for by in range(1, FAR):
        total = total + jnp.where(
            core == 0, jnp.roll(moved[by - 1], -by, axis=1), jnp.roll(moved[by - 1], by, axis=1)
        )
    return total + swap(total[:, :, ::-1], "core"), done


def by_place(values, axis):
    return jnp.stack(
        [lax.index_in_dim(values, PLACES.index(at), axis, False) for at in range(CHIPS)], axis
    )


def by_chunk(values, axis):
    return jnp.stack([lax.index_in_dim(values, at, axis, False) for at in PLACES], axis)


def in_hbm(arrays, specs=None):
    return [
        array
        if specs and specs[i].memory_space == pltpu.SMEM
        else pltpu.with_memory_space_constraint(array, pltpu.HBM)
        for i, array in enumerate(arrays)
    ]


def call(
    kernel, name, inputs, ins, outs, shapes, earlier=(), grid=(1,), scratch=(), mib=56, cost=None,
    free=0,
):
    return pl.pallas_call(
        kernel,
        grid=grid,
        in_specs=ins + [pl.BlockSpec(memory_space=pl.ANY)] * len(earlier),
        out_specs=outs,
        out_shape=shapes,
        scratch_shapes=list(scratch),
        input_output_aliases={len(ins) + i: i for i in range(len(earlier))},
        compiler_params=pltpu.CompilerParams(vmem_limit_bytes=mib << 20),
        cost_estimate=BRIEF if cost is None else cost,
        name=name,
    )(*inputs[:free], *in_hbm(inputs[free:], ins[free:]), *in_hbm(earlier))


def whole(array):
    return pl.BlockSpec(array.shape, lambda i: (0,) * len(array.shape))


def once(array):
    return pl.BlockSpec(
        array.shape, lambda i: (0,) * len(array.shape), pipeline_mode=pl.Buffered(1)
    )


def rows_of(step, tok_rows, cols):
    first, count = WIDE_CHUNKS[step] if step == LAST else CHUNKS[step]
    index = first // count
    return pl.BlockSpec((2 * count * tok_rows, cols), lambda i: (index, 0))


def lin_chunk(step, blocks, weight, gain, place, tok_rows, earlier):
    count, width, cols = len(blocks), weight.shape[0], weight.shape[1]
    length = 2 * CHIPS * tok_rows
    rows, head = count * tok_rows, weight.shape[1] // 3

    def kernel(*refs):
        block_refs, weight_ref, gain_ref, place_ref = refs[:count], *refs[count : count + 3]
        lin_ref, all_ref, sum_ref, tag_ref = refs[-4:]
        lanes = pl.ds(pl.multiple_of(place_ref[0] * tok_rows, tok_rows), tok_rows)
        for i in range(count):
            normed, _ = rms_forward(block_refs[i][:tok_rows].astype(jnp.float32), gain_ref[...])
            all_ref[i * tok_rows : (i + 1) * tok_rows] = normed.astype(jnp.bfloat16)
            levels = block_refs[i][tok_rows:, lanes].astype(jnp.float32)
            others = block_refs[i][tok_rows:, : 3 * tok_rows].astype(jnp.float32)
            tag_ref[i * EXTRA : (i + 1) * EXTRA] = jnp.concatenate(
                [levels[:1]]
                + [others[1:2, k * tok_rows : (k + 1) * tok_rows] for k in range(3)]
                + [jnp.zeros((EXTRA - 4, tok_rows), jnp.float32)],
                axis=0,
            )
        lin = product(all_ref[...], weight_ref[...])
        lin_ref[...] = lin
        line = lax.broadcasted_iota(jnp.int32, (8, head), 0)
        total = jnp.zeros((8, rows), jnp.float32)
        for k in range(2):
            part = lin[:, k * head : (k + 1) * head]
            total = total + lax.dot_general(
                (line == k).astype(jnp.float32),
                part * part,
                (((1,), (1,)), ((), ())),
                precision=lax.Precision.HIGHEST,
                preferred_element_type=jnp.float32,
            )
        sum_ref[...] = total

    tags = jax.ShapeDtypeStruct((count * EXTRA, tok_rows), jnp.float32)
    sums = jax.ShapeDtypeStruct((8, rows), jnp.float32)
    return call(
        kernel,
        "lin",
        [*blocks, weight, gain, place],
        [whole(b) for b in blocks]
        + [whole(weight), whole(gain), pl.BlockSpec(memory_space=pltpu.SMEM)],
        [rows_of(step, tok_rows, cols), rows_of(step, tok_rows, width), whole(sums), whole(tags)],
        [
            jax.ShapeDtypeStruct((length, cols), jnp.float32),
            jax.ShapeDtypeStruct((length, width), jnp.bfloat16),
            sums,
            tags,
        ],
        earlier,
        free=count,
        mib=36,
    )


def both_halves(cosine, sine_part):
    return (
        jnp.concatenate([cosine, cosine], axis=-1),
        jnp.concatenate([-sine_part, sine_part], axis=-1),
    )


def rotate_rows(lin, inverse, gains, cosine, sine_part):
    length, cols = lin.shape
    head = cols // 3
    rows = length // 4

    def kernel(lin_ref, inv_ref, gain_ref, cos_ref, sin_ref, q_ref, k_ref, v_ref):
        cos, sin = both_halves(cos_ref[...], sin_ref[...])
        for k, out_ref in enumerate((q_ref, k_ref)):
            part = lin_ref[:, k * head : (k + 1) * head] * inv_ref[:, k : k + 1]
            part = part * gain_ref[k : k + 1]
            turned = pltpu.roll(part, head // 2, 1)
            out_ref[...] = (part * cos + turned * sin).astype(jnp.bfloat16)
        v_ref[...] = lin_ref[:, 2 * head :].astype(jnp.bfloat16)

    row = lambda width: pl.BlockSpec((rows, width), lambda i: (i, 0))
    return call(
        kernel,
        "rotate",
        [lin, inverse, gains, cosine, sine_part],
        [row(cols), row(2), whole(gains), row(head // 2), row(head // 2)],
        [row(head)] * 3,
        [pltpu.HBM((length, head), jnp.bfloat16)] * 3,
        grid=(4,),
        mib=16,
    )


def attend_chunk(step, queries, keys, values, tok_rows, score_scale):
    count = 2 * CHUNKS[step][1]
    head = keys.shape[1]

    def kernel(q_ref, k_ref, v_ref, out_ref, lse_ref, mine_ref, other_ref):
        for i in range(0, count, 2):
            span = pl.ds(i * tok_rows, 2 * tok_rows)
            scores = contract_cols(q_ref[span], k_ref[...]) * score_scale
            row_max = jnp.max(scores, axis=-1, keepdims=True)
            raw = jnp.exp(scores - row_max)
            total = jnp.sum(raw, axis=-1, keepdims=True)
            probs = (raw / total).astype(jnp.bfloat16)
            mixed = product(probs, v_ref[...]).astype(jnp.bfloat16)
            out_ref[span] = mixed
            lse_ref[span] = row_max + jnp.log(total)
            half = pl.ds(i // 2 * tok_rows, tok_rows)
            mine_ref[half] = mixed[:tok_rows]
            other_ref[half] = mixed[tok_rows:]

    rows = count * tok_rows
    shapes = [
        jax.ShapeDtypeStruct((rows, head), jnp.bfloat16),
        jax.ShapeDtypeStruct((rows, 1), jnp.float32),
    ] + [jax.ShapeDtypeStruct((rows // 2, head), jnp.bfloat16)] * 2
    return call(
        kernel,
        "attend",
        [queries, keys, values],
        [rows_of(step, tok_rows, head), whole(keys), whole(values)],
        [whole(shape) for shape in shapes],
        shapes,
        mib=28,
    )


def pair_product(left, right, left_weight, right_weight, transposed, name, step=None):
    multiply = contract_cols if transposed else product
    width = left_weight.shape[0] if transposed else left_weight.shape[1]
    rows, block = left.shape[0], whole(left)
    if step is not None:
        first, count = CHUNKS[step]
        rows, index = rows * count // CHIPS, first // count
        block = pl.BlockSpec((rows, left.shape[1]), lambda i: (index, 0))

    def kernel(left_ref, right_ref, left_weight_ref, right_weight_ref, out_ref):
        total = multiply(left_ref[...], left_weight_ref[...])
        total = total + multiply(right_ref[...], right_weight_ref[...])
        out_ref[...] = total.astype(jnp.bfloat16)

    shape = jax.ShapeDtypeStruct((rows, width), jnp.bfloat16)
    arrays = [left, right, left_weight, right_weight]
    return call(
        kernel,
        name,
        arrays,
        [block, block, whole(left_weight), whole(right_weight)],
        [whole(shape)],
        [shape],
        mib=16,
    )[0]


def attend_back_chunk(
    step, blocks, queries, lse, keys, values, weight, lin, gains, cosine, sine_part, tok_rows,
    score_scale, earlier, final
):
    count = len(blocks)
    length, head = keys.shape
    width = weight.shape[1]
    rows = count * tok_rows

    def unspun(grad, cosine, sine_part, gain):
        cos, sin = both_halves(cosine, sine_part)
        return (grad * cos - pltpu.roll(grad, head // 2, 1) * sin) * gain

    def line_sums(values):
        ones = jnp.ones((8, head), jnp.float32)
        return lax.dot_general(
            ones,
            values,
            (((1,), (1,)), ((), ())),
            precision=lax.Precision.HIGHEST,
            preferred_element_type=jnp.float32,
        )

    def kernel(*refs):
        block_refs = refs[:count]
        q_ref, lse_ref, lin_ref, cos_ref, sin_ref = refs[count : count + 5]
        k_ref, v_ref, w_ref, gain_ref = refs[count + 5 : count + 9]
        rest = refs[count + 9 :]
        if final:
            k_lin_ref, cos_all, sin_all = rest[:3]
            rest = rest[3:]
        if earlier:
            dk, dv = rest[0][...], rest[1][...]
        else:
            dk, dv = 0.0, 0.0
        dq_ref, all_ref, dk_ref, dv_ref, q_sums = rest[-6:-1] if final else rest[-5:]
        for i in range(count):
            all_ref[i * tok_rows : (i + 1) * tok_rows] = block_refs[i][...]
        for i in range(0, count, 2):
            span = pl.ds(i * tok_rows, 2 * tok_rows)
            queries = q_ref[span]
            douts = contract_cols(all_ref[span], w_ref[...]).astype(jnp.bfloat16)
            probs = jnp.exp(contract_cols(queries, k_ref[...]) * score_scale - lse_ref[span])
            dprobs = contract_cols(douts, v_ref[...])
            delta = jnp.sum(probs * dprobs, axis=-1, keepdims=True)
            dscores = (probs * (dprobs - delta)).astype(jnp.bfloat16)
            dq = product(dscores, k_ref[...]) * score_scale
            dq = unspun(dq, cos_ref[span], sin_ref[span], gain_ref[:1])
            dq_ref[span] = dq
            q_sums[:, i * tok_rows : (i + 2) * tok_rows] = line_sums(dq * lin_ref[span])
            dk = dk + contract_rows(dscores, queries) * score_scale
            dv = dv + contract_rows(probs.astype(jnp.bfloat16), douts)
        if final:
            dk = unspun(dk, cos_all[...], sin_all[...], gain_ref[1:])
            rest[-1][...] = line_sums(dk * k_lin_ref[...])
        dk_ref[...] = dk
        dv_ref[...] = dv

    total = jax.ShapeDtypeStruct((length, head), jnp.float32)
    inputs = [*blocks, queries, lse, lin, cosine, sine_part, keys, values, weight, gains]
    ins = [whole(b) for b in blocks] + [
        rows_of(step, tok_rows, head),
        whole(lse),
        rows_of(step, tok_rows, head),
        rows_of(step, tok_rows, head // 2),
        rows_of(step, tok_rows, head // 2),
        whole(keys),
        whole(values),
        whole(weight),
        whole(gains),
    ]
    sums = [jax.ShapeDtypeStruct((8, rows), jnp.float32)]
    if final:
        inputs += [lin, cosine, sine_part]
        ins += [pl.BlockSpec((length, head), lambda i: (0, 1)), whole(cosine), whole(sine_part)]
        sums += [jax.ShapeDtypeStruct((8, length), jnp.float32)]
    so_far = list(earlier[2:4])
    return pl.pallas_call(
        kernel,
        grid=(1,),
        in_specs=ins
        + [whole(part) for part in so_far]
        + [pl.BlockSpec(memory_space=pl.ANY)] * len(earlier[:2]),
        out_specs=[
            rows_of(step, tok_rows, head),
            rows_of(step, tok_rows, width),
            whole(total),
            whole(total),
        ]
        + [whole(part) for part in sums],
        out_shape=[total, jax.ShapeDtypeStruct((length, width), jnp.bfloat16), total, total] + sums,
        input_output_aliases={
            len(ins): 2,
            len(ins) + 1: 3,
            len(ins) + 2: 0,
            len(ins) + 3: 1,
        }
        if earlier
        else {},
        compiler_params=pltpu.CompilerParams(vmem_limit_bytes=42 << 20),
        cost_estimate=BRIEF,
        name="attend_back",
    )(*blocks, *in_hbm(inputs[count:], ins[count:]), *so_far, *in_hbm(earlier[:2]))


def lin_back_rows(dq, dk, dv, lin, inverse, along, tok_rows):
    length, cols = lin.shape
    head = cols // 3
    places = 2
    rows = 2 * places * tok_rows

    def kernel(dq_ref, dk_ref, dv_ref, lin_ref, inv_ref, along_ref, out_ref, mine_ref, other_ref):
        for k, grad_ref in enumerate((dq_ref, dk_ref)):
            span = slice(k * head, (k + 1) * head)
            inv = inv_ref[:, k : k + 1]
            slope = inv * inv * inv * along_ref[:, k : k + 1]
            out_ref[:, span] = (inv * grad_ref[...] - lin_ref[:, span] * slope).astype(jnp.bfloat16)
        out_ref[:, 2 * head :] = dv_ref[...].astype(jnp.bfloat16)
        for i in range(places):
            to, at = slice(i * tok_rows, (i + 1) * tok_rows), 2 * i * tok_rows
            mine_ref[to] = out_ref[at : at + tok_rows]
            other_ref[to] = out_ref[at + tok_rows : at + 2 * tok_rows]

    row = lambda width: pl.BlockSpec((rows, width), lambda i: (i, 0))
    half = jax.ShapeDtypeStruct((length // 2, cols), jnp.bfloat16)
    return call(
        kernel,
        "lin_back",
        [dq, dk, dv, lin, inverse, along],
        [row(head)] * 3 + [row(cols), row(2), row(2)],
        [row(cols)] + [pl.BlockSpec((places * tok_rows, cols), lambda i: (i, 0))] * 2,
        [pltpu.HBM((length, cols), jnp.bfloat16), pltpu.HBM(half.shape, half.dtype), half],
        grid=(CHIPS // places,),
        mib=16,
    )


EXPERT_COLS = 512


def expert_chunk(step, h_blocks, g_blocks, place, kept, router, gate, up, down, tok_rows, earlier):
    count = len(h_blocks)
    width, hidden = gate.shape
    cols = EXPERT_COLS
    rows = count * tok_rows
    length = 2 * CHIPS * tok_rows
    low = jnp.bfloat16
    first, places = WIDE_CHUNKS[step]
    index = first // places
    inner, outer = hidden // cols, width // cols
    long_rows = tok_rows + EXTRA
    per_tile = cols // tok_rows
    apart = places if step == LAST else 1
    together = places // apart

    def kernel(*refs):
        h_refs, g_refs = refs[:count], refs[count : 2 * count]
        place_ref, kept_ref, router_ref = refs[2 * count : 2 * count + 3]
        gate_ref, up_ref, down_ref, gate_rows, up_rows, down_cols = refs[
            2 * count + 3 : 2 * count + 9
        ]
        outs = refs[2 * count + 9 + len(earlier) : -8]
        row_outs, (act_ref, dgate_ref, dup_ref) = outs[:2], outs[2:5]
        mix_refs, dx_refs = outs[5 : 5 + 2 * apart], outs[5 + 2 * apart :]
        h_all, g_all, act_all, dgate_all, dup_all, share_ref, dshare_ref, sems = refs[-8:]
        turn = pl.program_id(0)

        def copies():
            span = pl.ds(index * rows, rows)
            return [
                pltpu.make_async_copy(source, out.at[span], sems.at[i])
                for i, (source, out) in enumerate(zip((h_all, g_all), row_outs))
            ]

        @pl.when(turn == 0)
        def _():
            for i in range(count):
                h_all[i * tok_rows : (i + 1) * tok_rows] = h_refs[i][...]
                g_all[i * tok_rows : (i + 1) * tok_rows] = g_refs[i][...]
            logits = contract_cols(h_all[...], router_ref[...])
            raw = jnp.exp(logits - jnp.max(logits, axis=-1, keepdims=True))
            probs = raw / jnp.sum(raw, axis=-1, keepdims=True)
            lanes = lax.broadcasted_iota(jnp.int32, probs.shape, 1)
            chosen = jnp.sum(
                jnp.where(lanes == place_ref[0], probs, 0.0), axis=-1, keepdims=True
            )
            share_ref[...] = chosen * kept_ref[...]
            dshare_ref[...] = jnp.zeros_like(dshare_ref)

        @pl.when(turn == 1)
        def _():
            for copy in copies():
                copy.start()

        @pl.when(turn < inner)
        def _():
            share = share_ref[...]
            gate_lin = product(h_all[...], gate_ref[...])
            up_lin = product(h_all[...], up_ref[...])
            back = contract_cols(g_all[...], down_ref[...])
            sig = jax.nn.sigmoid(gate_lin)
            silu = gate_lin * sig
            act = silu * up_lin
            dshare_ref[...] += jnp.sum(act * back, axis=-1, keepdims=True)
            act_low = (act * share).astype(low)
            back = back * share
            dgate = (back * up_lin * (sig * (1.0 + gate_lin * (1.0 - sig)))).astype(low)
            dup = (back * silu).astype(low)
            span = pl.ds(pl.multiple_of(turn * cols, cols), cols)
            for ref, everything, value in (
                (act_ref, act_all, act_low),
                (dgate_ref, dgate_all, dgate),
                (dup_ref, dup_all, dup),
            ):
                ref[...] = value
                everything[:, span] = value

        @pl.when(turn >= inner)
        def _():
            mix = product(act_all[...], down_cols[...]).astype(low)
            dx = contract_cols(dgate_all[...], gate_rows[...])
            dx = (dx + contract_cols(dup_all[...], up_rows[...])).astype(low)
            for i in range(count):
                span = slice(i * tok_rows, (i + 1) * tok_rows)
                to, at = i % 2 + i // 2 // together * 2, i // 2 % together
                mix_refs[to][at * tok_rows : (at + 1) * tok_rows] = mix[span]
                dx_refs[to][at * long_rows : at * long_rows + tok_rows] = dx[span]

            total = dshare_ref[...] * kept_ref[...]
            same = lax.broadcasted_iota(jnp.int32, (tok_rows, tok_rows), 0) == (
                lax.broadcasted_iota(jnp.int32, (tok_rows, tok_rows), 1)
            )
            tile_lanes = lax.broadcasted_iota(jnp.int32, (EXTRA, cols), 1) // tok_rows
            here = tile_lanes + (turn - inner) * per_tile == place_ref[0]
            for i in range(count):
                rest = jnp.sum(
                    jnp.where(same, total[i * tok_rows : (i + 1) * tok_rows], 0.0),
                    axis=0,
                    keepdims=True,
                )
                pieces = []
                for _ in range(3):
                    piece = rest.astype(low).astype(jnp.float32)
                    rest = rest - piece
                    pieces.append(piece)
                pieces.append(jnp.zeros((EXTRA - 3, tok_rows), jnp.float32))
                line = jnp.concatenate(pieces, axis=0)
                line = jnp.concatenate([line] * per_tile, axis=1)
                to, at = i % 2 + i // 2 // together * 2, i // 2 % together
                at = at * long_rows + tok_rows
                dx_refs[to][at : at + EXTRA] = jnp.where(here, line, 0.0).astype(low)

        @pl.when(turn == inner + outer - 1)
        def _():
            for copy in copies():
                copy.wait()

    def inner_at(t):
        return jnp.minimum(t, inner - 1)

    def outer_at(t):
        return jnp.maximum(t - inner, 0)

    tile = pl.BlockSpec((rows, cols), lambda t: (index, inner_at(t)))
    wide = jax.ShapeDtypeStruct((length, hidden), low)
    full = jax.ShapeDtypeStruct((length, width), low)
    half = jax.ShapeDtypeStruct((together * tok_rows, width), low)
    longer = jax.ShapeDtypeStruct((together * long_rows, width), low)
    anywhere = pl.BlockSpec(memory_space=pl.ANY)
    out_tile = lambda shape: pl.BlockSpec((shape.shape[0], cols), lambda t: (0, outer_at(t)))
    return call(
        kernel,
        "expert",
        [*h_blocks, *g_blocks, place, kept, router, gate, up, down, gate, up, down],
        [once(b) for b in [*h_blocks, *g_blocks]]
        + [
            pl.BlockSpec(memory_space=pltpu.SMEM),
            pl.BlockSpec((rows, 1), lambda t: (index, 0)),
            whole(router),
            pl.BlockSpec((width, cols), lambda t: (0, inner_at(t))),
            pl.BlockSpec((width, cols), lambda t: (0, inner_at(t))),
            pl.BlockSpec((cols, width), lambda t: (inner_at(t), 0)),
            pl.BlockSpec((cols, hidden), lambda t: (outer_at(t), 0)),
            pl.BlockSpec((cols, hidden), lambda t: (outer_at(t), 0)),
            pl.BlockSpec((hidden, cols), lambda t: (0, outer_at(t))),
        ],
        [anywhere] * 2
        + [tile] * 3
        + [out_tile(half)] * (2 * apart)
        + [out_tile(longer)] * (2 * apart),
        [full] * 2 + [wide] * 3 + [half] * (2 * apart) + [longer] * (2 * apart),
        earlier,
        grid=(inner + outer,),
        scratch=[pltpu.VMEM((rows, width), low)] * 2
        + [pltpu.VMEM((rows, hidden), low)] * 3
        + [pltpu.VMEM((rows, 1), jnp.float32)] * 2
        + [pltpu.SemaphoreType.DMA((2,))],
        mib=46,
        free=2 * count,
    )


def input_grad_rows(parts, tokens, inverse, gain, grads):
    def kernel(ahead_ref, behind_ref, mine_ref, tokens_ref, inv_ref, gain_ref, grads_ref, out_ref):
        upstream = mine_ref[...].astype(jnp.float32) + ahead_ref[...].astype(jnp.float32)
        upstream = upstream + behind_ref[...].astype(jnp.float32)
        rows = tokens_ref[...].astype(jnp.float32)
        inv = inv_ref[...]
        scaled = upstream * gain_ref[...]
        along = jnp.mean(scaled * rows, axis=-1, keepdims=True)
        norm = inv * scaled - rows * inv * inv * inv * along
        out_ref[...] = (grads_ref[...] + norm).astype(jnp.bfloat16)

    arrays = [*parts, tokens, inverse, gain, grads]
    shape = jax.ShapeDtypeStruct(tokens.shape, jnp.bfloat16)
    return call(
        kernel,
        "input_grad",
        arrays,
        [whole(a) for a in arrays],
        [whole(shape)],
        [shape],
        mib=24,
        free=len(arrays),
    )[0]


THIN = 128
HALF_THIN = THIN // 2


def split_parts(values):
    high = values.astype(jnp.bfloat16).astype(jnp.float32)
    return high, values - high


def dense_chunk(rows_h, grads, weight, columns, narrow, part, own_rows):
    length, width = rows_h.shape
    cols = grads.shape[1]
    block = 256
    runs = block // (2 * own_rows)
    wide = narrow is not None
    first_col, count_col = columns

    def kernel(part_ref, h_ref, grads_ref, weight_ref, *refs):
        kept_ref, sent_ref = refs[-2:] if wide else refs[-3:-1]
        grads = contract_rows(h_ref[...], grads_ref[...].astype(jnp.bfloat16))
        weight = weight_ref[...].astype(jnp.float32)[:, first_col : first_col + count_col]
        term = jnp.sum(grads * weight, axis=-1, keepdims=True)
        both = plain = grads
        if wide:
            narrow = refs[0][...]
            lanes = lax.broadcasted_iota(jnp.int32, narrow.shape, 1)
            narrow = jnp.where(lanes == 17, refs[1][...] + term, narrow)
            high, rest = split_parts(narrow)
            both = jnp.concatenate([both, high, rest], axis=-1)
            plain = jnp.concatenate([plain, narrow, jnp.zeros_like(narrow)], axis=-1)
        else:
            refs[-1][...] = term
        second = part_ref[0] == 1
        for i in range(runs):
            at = 2 * i * own_rows
            first = slice(at, at + own_rows)
            other = slice(at + own_rows, at + 2 * own_rows)
            to = slice(i * own_rows, (i + 1) * own_rows)
            kept_ref[to] = jnp.where(second, plain[other], plain[first])
            sent_ref[to] = jnp.where(second, both[first], both[other]).astype(jnp.bfloat16)

    full = cols + (THIN if wide else 0)
    out = lambda kind: jax.ShapeDtypeStruct((width // 2, full), kind)
    row = lambda size: pl.BlockSpec((block // 2, size), lambda i: (i, 0))
    here = lambda size: pl.BlockSpec((block, size), lambda i: (i, 0))
    return call(
        kernel,
        "dense",
        [part, rows_h, grads, weight] + (list(narrow) if wide else []),
        [
            pl.BlockSpec(memory_space=pltpu.SMEM),
            pl.BlockSpec((length, block), lambda i: (0, i)),
            whole(grads),
            here(weight.shape[1]),
        ]
        + ([here(HALF_THIN), here(1)] if wide else []),
        [row(full), row(full)] + ([] if wide else [here(1)]),
        [out(jnp.float32), out(jnp.bfloat16)]
        + ([] if wide else [jax.ShapeDtypeStruct((width, 1), jnp.float32)]),
        grid=(width // block,),
        mib=24,
        cost=pl.CostEstimate(
            flops=2 * length * width * cols,
            bytes_accessed=2 * length * width + 6 * width * full,
            transcendentals=0,
        ),
    )


def dense_sum(kept, got):
    rows, full = kept.shape
    cols = full - THIN
    block = rows // 4

    def kernel(kept_ref, got_ref, out_ref):
        got = got_ref[...].astype(jnp.float32)
        out_ref[:, :cols] = (kept_ref[:, :cols] + got[:, :cols]).astype(jnp.bfloat16)
        narrow = kept_ref[:, cols : cols + HALF_THIN]
        narrow = narrow + got[:, cols : cols + HALF_THIN] + got[:, cols + HALF_THIN :]
        out_ref[:, cols:] = jnp.concatenate(split_parts(narrow), axis=-1).astype(jnp.bfloat16)

    row = pl.BlockSpec((block, full), lambda i: (i, 0))
    return call(
        kernel,
        "dense_sum",
        [kept, got],
        [row, row],
        [row],
        [jax.ShapeDtypeStruct((rows, full), jnp.bfloat16)],
        grid=(4,),
        mib=16,
    )[0]


def body(
    tokens,
    cotangent,
    attn_gain,
    w_query,
    w_key,
    w_value,
    w_out,
    query_gain,
    key_gain,
    ffn_gain,
    router,
    w_gate,
    w_up,
    w_down,
    routes,
    priority,
    positions,
):
    low = jnp.bfloat16
    ctx_count = 2 * CHIPS
    place = lax.axis_index("chip") * 2 + lax.axis_index("core")
    part = lax.axis_index("fsdp")
    tok_rows, model_width = tokens.shape[1:]
    half_width = model_width // 2
    head_dim = HEAD_DIM
    length = tok_rows * ctx_count
    capacity = 9 * tok_rows
    score_scale = head_dim ** (-0.5)
    per_half = ctx_count // 2
    expert_count = router.shape[1]

    def joined(mine, other, axis):
        return jnp.where(
            part == 0,
            jnp.concatenate([mine, other], axis=axis),
            jnp.concatenate([other, mine], axis=axis),
        )

    def head_rows(matrix, width):
        return lax.dynamic_slice_in_dim(matrix, (place % per_half) * width, width, 0)

    small = jnp.concatenate(
        [
            router.T,
            attn_gain[None],
            ffn_gain[None],
            jnp.concatenate(
                [
                    head_rows(query_gain, head_dim),
                    head_rows(key_gain, head_dim),
                    jnp.zeros((half_width - 2 * head_dim,), low),
                ]
            )[None],
        ],
        axis=0,
    )
    qkv_mine = jnp.concatenate(
        [
            lax.dynamic_slice_in_dim(w, place * head_dim, head_dim, 1)
            for w in (w_query, w_key, w_value)
        ],
        axis=1,
    )
    out_mine = head_rows(w_out, head_dim)

    hot = routes[0][:, :, None] == jnp.arange(expert_count, dtype=jnp.int32)[None, None, :]
    levels = jnp.sum(jnp.where(hot, priority[0][:, :, None] - LEVELS, 0), axis=1) + LEVELS
    spot = positions[0]
    line = jnp.concatenate(
        [spot // 128, spot % 128, jnp.full((model_width - 2 * tok_rows,), place, jnp.int32)]
    )
    tags = jnp.concatenate(
        [
            levels.T.reshape(1, model_width),
            line[None],
            jnp.zeros((EXTRA - 2, model_width), jnp.int32),
        ],
        axis=0,
    ).astype(low)

    inputs = tokens[0].astype(jnp.float32)
    inv_one = lax.rsqrt(jnp.mean(inputs * inputs, axis=-1, keepdims=True) + epsilon)
    first_rows = jnp.concatenate([tokens[0], tags], axis=0)
    place_one = place.astype(jnp.int32).reshape(1)
    ready = ()
    sum_parts, tag_parts = {}, {}

    def lin_job(step, blocks):
        def function():
            made = lin_chunk(
                step, blocks(), qkv_weight, g_attn[None], place_one, tok_rows, ready
            )
            return made

        return [], function

    def lin_keep(step, made):
        nonlocal ready
        ready = tuple(made[:2])
        sum_parts[step], tag_parts[step] = made[2][:2], made[3]

    def other_core(array):
        return (swap(array, "core"),)

    rows_one = Gather(first_rows)

    def to_other(*arrays):
        return [swap(array, "fsdp") for array in arrays]

    (small_other,), (qkv_other,) = window(
        [rows_one], [([small], to_other)], loose=[([qkv_mine], to_other)]
    )
    small_full = joined(small, small_other, 1)
    r_weight = small_full[:expert_count]
    g_attn = small_full[expert_count].astype(jnp.float32)
    g_ffn = small_full[expert_count + 1].astype(jnp.float32)
    here = part == place // per_half
    g_heads = jnp.where(here, small[expert_count + 2], small_other[expert_count + 2]).astype(
        jnp.float32
    )
    g_query, g_key = g_heads[:head_dim], g_heads[head_dim : 2 * head_dim]
    qkv_weight = joined(qkv_mine, qkv_other, 0)

    def expert_weights(_, *own):
        return [lax.all_gather(w, "fsdp", axis=k, tiled=True) for w, k in zip(own, (0, 0, 1))]

    made, expert_own = window(
        [rows_one],
        [lin_job(1, lambda: rows_one.now)],
        loose=[([qkv_other, w_gate[0], w_up[0], w_down[0]], expert_weights)],
    )
    gate_weight, up_weight, down_weight = expert_own
    lin_keep(1, made)
    made, (qkv_pair,) = window(
        [rows_one],
        [lin_job(2, lambda: rows_one.now), ([qkv_weight], other_core)],
    )
    lin_keep(2, made)
    made, (out_other,) = window(
        [rows_one], [lin_job(3, lambda: rows_one.now)], loose=[([out_mine], to_other)]
    )
    out_weight = jnp.where(here, out_mine, out_other)
    lin_keep(3, made)
    lin_keep(LAST, lin_job(LAST, lambda: rows_one.chunks[LAST])[1]())
    lin, all_h_one = ready
    all_tags = jnp.concatenate([tag_parts[step] for step in WIDE_CHUNKS], axis=0).reshape(
        ctx_count, EXTRA, tok_rows
    )

    def token_sums(lines, jobs):
        total, done = sum_all(by_place(lines.reshape(-1, CHIPS, 2, tok_rows), 1), jobs)
        return by_chunk(total, 1).reshape(-1, length).T / model_width, done

    def rank_job(all_tags):
        mine, owner = all_tags[:, 0], all_tags[:, 3, :1]
        order = owner * tok_rows + jnp.arange(tok_rows, dtype=jnp.float32)[None]
        mine = mine.reshape(length)
        code = mine * length + order.reshape(length)
        ranks = jnp.sum((code[None, :] < code[:, None]).astype(jnp.float32), axis=1)
        kept = (mine < LEVELS) & (ranks < capacity)
        return (kept.astype(jnp.float32)[:, None],)

    def rope_job(all_tags):
        spots = (all_tags[:, 1] * 128.0 + all_tags[:, 2]).reshape(-1)
        return [table[:, 0] for table in rope_tables(spots, head_dim)]

    square, ((cosine, sine_part),) = token_sums(
        jnp.concatenate([sum_parts[step] for step in WIDE_CHUNKS], axis=1),
        [([all_tags], rope_job)],
    )
    inverse = lax.rsqrt(square + epsilon)
    gains = jnp.stack([g_query, g_key], axis=0)
    q_rot, k_rot, v_low = rotate_rows(lin, inverse, gains, cosine, sine_part)

    heads = {}

    def attend_job(step):
        return [q_rot, k_rot, v_low], lambda queries, keys, values: attend_chunk(
            step, queries, keys, values, tok_rows, score_scale
        )

    def projected(step, made):
        return pair_product(
            made[2], swap(made[3], "core"), out_weight, out_pair, False, "project"
        )

    def first_job(queries, keys, values):
        made = attend_job(FAR)[1](queries, keys, values)
        return [*made, projected(FAR, made)]

    (out_pair,) = other_core(out_weight)
    grads_rows = Gather(cotangent[0], -1)
    (*heads[FAR], far_terms), heads[FAR - 1] = window(
        [grads_rows], [([q_rot, k_rot, v_low], first_job), attend_job(FAR - 1)]
    )

    def out_terms(step, *parts):
        return (far_terms if step == FAR else projected(step, parts)), None

    out_sum = Scatter(out_terms)
    for near in range(FAR - 1, -1, -1):
        out_sum.inputs = heads[near]
        jobs = [attend_job(near - 1)] if near else []
        held = [([gate_weight], lambda weight: (weight,)), ([all_tags], rank_job)]
        made = window([out_sum], jobs + (held if near == 2 else []))
        if near == 2:
            (gate_weight,), (kept,) = made[-2:]
        if near:
            heads[near - 1] = made[0]
    mixed_low = jnp.concatenate([heads[step][0] for step in CHUNKS], axis=0)
    middle = inputs + out_sum.total

    h_two_f, inv_two = rms_forward(middle, g_ffn)
    h_two = h_two_f.astype(low)
    grad_out = cotangent[0].astype(jnp.float32)
    filled = ()
    mix_terms, dx_terms = {}, {}

    rows_two = Gather(h_two, 1)
    window([rows_two])

    def expert_job(step, h_blocks, g_blocks):
        return [], lambda: expert_chunk(
            step,
            h_blocks(),
            g_blocks(),
            place_one,
            kept,
            r_weight,
            gate_weight,
            up_weight,
            down_weight,
            tok_rows,
            filled,
        )

    for step in list(range(1, FAR)) + [LAST]:
        if step == LAST:
            run = expert_job(step, lambda: rows_two.chunks[LAST], lambda: grads_rows.chunks[LAST])
            made = run[1]()
        else:
            run = expert_job(step, lambda: rows_two.now, lambda: grads_rows.now)
            (made,) = window([rows_two, grads_rows], [run])
        filled, terms = tuple(made[:5]), made[5:]
        if step == LAST:
            mix_terms[0], mix_terms[FAR] = terms[:2], terms[2:4]
            dx_terms[0], dx_terms[FAR] = terms[4:6], terms[6:]
        else:
            mix_terms[step], dx_terms[step] = terms[:2], terms[2:]
    all_h_two, all_grads, act_low, gate_grad, up_grad = filled

    def wgrad(left, right):
        return (contract_rows(left, right).astype(low),)

    def over_sequences(matrix, axis):
        return lax.psum_scatter(matrix, "fsdp", scatter_dimension=axis, tiled=True)

    logits = contract_cols(h_two, r_weight)
    row_max = jnp.max(logits, axis=-1, keepdims=True)
    exps_raw = jnp.exp(logits - row_max)
    router_probs = exps_raw / jnp.sum(exps_raw, axis=-1, keepdims=True)
    dx_sum = Scatter(lambda step: dx_terms[step], ready=True, far_by=1)
    mix_sum = Scatter(lambda step: mix_terms[step], ready=True, far_by=-1)
    ((gate_wgrad,),) = window([dx_sum, mix_sum], [([all_h_two, gate_grad], wgrad)])
    s_gate = over_sequences(gate_wgrad, 0)
    ((up_wgrad,),) = window([dx_sum, mix_sum], [([all_h_two, up_grad], wgrad)])
    s_up = over_sequences(up_wgrad, 0)
    ((down_wgrad,),) = window([dx_sum], [([act_low, all_grads], wgrad)])
    s_down = over_sequences(down_wgrad, 1)
    window([dx_sum])
    hidden_sum = dx_sum.total

    prob_grad = jnp.sum(hidden_sum[tok_rows : tok_rows + 3], axis=0)
    prob_grad = prob_grad.reshape(expert_count, tok_rows).T
    logit_grad = router_probs * (
        prob_grad - jnp.sum(router_probs * prob_grad, axis=-1, keepdims=True)
    )
    hidden_grad = hidden_sum[:tok_rows] + precise(logit_grad, r_weight.astype(jnp.float32))
    norm_grad, ffn_gain_grad = rms_backward(middle, inv_two, g_ffn, hidden_grad)
    middle_grad = grad_out + norm_grad

    sofar = ()

    q_sums = {}
    rows_da = Gather(middle_grad.astype(low))

    def back_job(step, blocks):
        return [], lambda: attend_back_chunk(
            step,
            blocks(),
            q_rot,
            heads[step][1],
            k_rot,
            v_low,
            out_weight,
            lin,
            gains,
            cosine,
            sine_part,
            tok_rows,
            score_scale,
            sofar,
            step == FAR,
        )

    def widen(array):
        return (array.astype(jnp.float32),)

    def narrow_job(h_two, logit_grad, ffn_gain_grad):
        return (
            jnp.concatenate(
                [
                    precise(h_two.astype(jnp.float32).T, logit_grad),
                    ffn_gain_grad[:, None],
                    jnp.zeros((model_width, HALF_THIN - expert_count - 1), jnp.float32),
                ],
                axis=1,
            ),
        )

    besides = {0: [], 1: [mix_sum], 2: [], 3: [mix_sum]}
    also = {1: [([h_two, logit_grad, ffn_gain_grad], narrow_job), ([s_gate], widen)]}
    for step in range(FAR + 1):
        if step == FAR:
            *made, k_sums = back_job(step, lambda: rows_da.chunks[FAR])[1]()
        else:
            made, *wide = window(
                [rows_da] + besides[step], [back_job(step, lambda: rows_da.now)] + also.get(step, [])
            )
            if step == 1:
                (narrow,), (s_gate,) = wide
        sofar, q_sums[step] = tuple(made[:4]), made[4]
    dq, all_branch, dk, dv = sofar

    def out_job(mixed_low, all_branch):
        return (contract_rows(mixed_low, all_branch),)

    own_rows = model_width // (2 * ctx_count)
    part_one = part.astype(jnp.int32).reshape(1)

    def value_job(all_h_one, dv):
        return dense_chunk(
            all_h_one, dv, qkv_weight, (2 * head_dim, head_dim), None,
            part_one, own_rows,
        )

    along, ((v_kept, v_sent, v_term),) = token_sums(
        jnp.stack(
            [jnp.concatenate([q_sums[step][0] for step in CHUNKS], axis=0), k_sums[0]], axis=0
        ),
        [
            ([all_h_one, dv], value_job),
        ],
    )
    layer_out = (middle + mix_sum.total).astype(low)
    lin_grad, lin_mine, lin_theirs = lin_back_rows(dq, dk, dv, lin, inverse, along, tok_rows)
    lin_theirs = swap(lin_theirs, "core")


    def pick(blocks, index):
        return lax.dynamic_index_in_dim(blocks, index, 1, False)

    def dense_job(all_h_one, lin_grad, *narrow):
        return dense_chunk(
            all_h_one, lin_grad[:, : 2 * head_dim], qkv_weight, (0, 2 * head_dim), narrow,
            part_one, own_rows,
        )

    def out_swap_job(out_sent, dq, dk, lin):
        gain_rows = jnp.stack(
            [
                jnp.sum(
                    grad * lin[:, k * head_dim : (k + 1) * head_dim] * inverse[:, k : k + 1], axis=0
                )
                for k, grad in enumerate((dq, dk))
            ],
            axis=0,
        )
        gain_rows = (gain_rows / gains).reshape(2, 2, own_rows)
        return swap(out_sent, "fsdp"), swap(pick(gain_rows, 1 - part), "fsdp"), pick(gain_rows, part)

    def h_terms(step, lin_mine, lin_theirs):
        return (
            pair_product(lin_mine, lin_theirs, qkv_weight, qkv_pair, True, "h_terms", step),
            None,
        )

    h_sum = Scatter(h_terms, [lin_mine, lin_theirs])
    def swap_job(sent):
        return (swap(sent, "fsdp"),)

    def owners_job(payload):
        blocks = payload.reshape(ctx_count, own_rows, -1)
        return (lax.all_to_all(blocks, ("chip", "core"), 0, 0, tiled=True),)

    (kept, sent), (v_got,) = window(
        [h_sum],
        [([all_h_one, lin_grad, narrow, v_term], dense_job)],
        loose=[([v_sent], swap_job)],
    )
    (got,), (out_wgrad,), (v_received,) = window(
        [h_sum],
        [([sent], swap_job), ([mixed_low, all_branch], out_job)],
        loose=[([(v_kept + v_got.astype(jnp.float32)).astype(low)], owners_job)],
    )
    out_rows = out_wgrad.reshape(1, 2, own_rows, model_width)
    (received,), (out_got, gain_got, gain_kept) = window(
        [h_sum],
        loose=[
            ([kept, got], lambda kept, got: owners_job(dense_sum(kept, got))),
            ([pick(out_rows, 1 - part)[0].astype(low), dq, dk, lin], out_swap_job),
        ],
    )

    (v_received,), (received,), (out_got, gain_got), (s_up,), (s_down,) = window(
        [h_sum],
        [
            ([], lambda: (v_received,)),
            ([], lambda: (received,)),
            ([], lambda: (out_got, gain_got)),
            ([s_up], widen),
            ([s_down], widen),
        ],
    )
    d_out = pick(out_rows, part)[0] + out_got.astype(jnp.float32)
    gain_sum = gain_kept + gain_got
    d_qgain, d_kgain = gain_sum[0], gain_sum[1]
    s_gate, s_up, s_down = s_gate[None], s_up[None], s_down[None]
    input_grad = input_grad_rows(h_sum.last, tokens[0], inv_one, g_attn[None], middle_grad)
    d_query, d_key, d_value = (
        columns.transpose(1, 0, 2).reshape(own_rows, model_width).astype(jnp.float32)
        for columns in (received[:, :, :head_dim], received[:, :, head_dim : 2 * head_dim], v_received)
    )
    thin_sum = jnp.sum(received[:, :, 2 * head_dim :].astype(jnp.float32), axis=0)
    thin_sum = thin_sum[:, :HALF_THIN] + thin_sum[:, HALF_THIN:]
    d_router = thin_sum[:, :expert_count]
    own_gain = lax.dynamic_slice_in_dim(g_attn, (2 * place + part) * own_rows, own_rows, 0)
    d_ffn, d_attn = thin_sum[:, expert_count], thin_sum[:, expert_count + 1] / own_gain
    return (
        layer_out[None],
        input_grad[None],
        d_attn,
        d_query,
        d_key,
        d_value,
        d_out,
        d_qgain,
        d_kgain,
        d_ffn,
        d_router,
        s_gate,
        s_up,
        s_down,
    )


def specs_of(ctx):
    rows, both = P("fsdp", ctx, None), ctx + ("fsdp",)
    dense = P("fsdp", None)
    ins = (
        rows,
        rows,
        P("fsdp"),
        dense,
        dense,
        dense,
        dense,
        P("fsdp"),
        P("fsdp"),
        P("fsdp"),
        dense,
        P(ctx, "fsdp", None),
        P(ctx, "fsdp", None),
        P(ctx, None, "fsdp"),
        rows,
        rows,
        P("fsdp", ctx),
    )
    line, matrix = P(both), P(both, None)
    outs = (
        rows,
        rows,
        line,
        matrix,
        matrix,
        matrix,
        matrix,
        line,
        line,
        line,
        matrix,
        P(ctx, "fsdp", None),
        P(ctx, "fsdp", None),
        P(ctx, None, "fsdp"),
    )
    return ins, outs


def solution(mesh):
    ctx_count, fsdp_count = mesh.shape["ctx"], mesh.shape["fsdp"]

    def whole(*arrays):
        heads = arrays[0].shape[2] // HEAD_DIM
        experts = arrays[10].shape[1]
        if ctx_count == 2 * CHIPS == heads == experts and fsdp_count == 2:
            chips = Mesh(mesh.devices.reshape(-1, 2, 2), ("chip", "core", "fsdp"))
            run, grid, ctx = body, chips, ("chip", "core")
        else:
            run, grid, ctx = general_body, mesh, ("ctx",)
        ins, outs = specs_of(ctx)
        return jax.shard_map(run, mesh=grid, in_specs=ins, out_specs=outs, check_vma=False)(*arrays)

    return whole
```

```python
import math

import jax
import jax.numpy as jnp
from jax import lax
from jax.experimental import pallas as pl
from jax.experimental.pallas import tpu as pltpu
from jax.sharding import Mesh
from jax.sharding import PartitionSpec as P

HEAD_DIM = 128
LEVELS = 4


epsilon = 1e-05
rope_base = 50000.0


def prefix(part, axis, combine, identity):
    place = lax.axis_index(axis)
    gathered = lax.all_gather(part, axis)
    state = jnp.zeros_like(part) + jnp.asarray(identity, part.dtype)

    def one(turn, state):
        return combine(state, lax.dynamic_index_in_dim(gathered, turn, 0, False))

    return lax.fori_loop(0, place, one, state)


def product(left, right):
    return jnp.dot(left, right, preferred_element_type=jnp.float32)


def precise(left, right):
    return jnp.dot(left, right, precision=lax.Precision.HIGHEST, preferred_element_type=jnp.float32)


def contract_rows(left, right):
    return lax.dot_general(
        left, right, (((0,), (0,)), ((), ())), preferred_element_type=jnp.float32
    )


def contract_cols(left, right):
    return lax.dot_general(
        left, right, (((1,), (1,)), ((), ())), preferred_element_type=jnp.float32
    )


def rms_forward(matrix, gain_row):
    inverse = lax.rsqrt(jnp.mean(matrix * matrix, axis=-1, keepdims=True) + epsilon)
    return (matrix * inverse * gain_row, inverse)


def rms_backward(matrix, inverse, gain_row, upstream):
    scaled = upstream * gain_row
    along = jnp.mean(scaled * matrix, axis=-1, keepdims=True)
    grad_rows = inverse * scaled - matrix * inverse * inverse * inverse * along
    grad_gain = jnp.sum(upstream * matrix * inverse, axis=0)
    return (grad_rows, grad_gain)


def rope_tables(position_ids, head_dim):
    half_dim = head_dim // 2
    inverse = rope_base ** (-(jnp.arange(half_dim, dtype=jnp.float32) * 2.0) / head_dim)
    angles = position_ids.astype(jnp.float32)[:, None] * inverse[None, :]
    return (jnp.cos(angles)[:, None, :], jnp.sin(angles)[:, None, :])


def rotate(matrix, cosine, sine_part, head_dim, turn_sign):
    count_rows = matrix.shape[0]
    by_head = matrix.reshape(count_rows, -1, head_dim)
    half_dim = head_dim // 2
    lower_half = by_head[..., :half_dim]
    upper_half = by_head[..., half_dim:]
    turned = jnp.concatenate(
        [
            lower_half * cosine - turn_sign * upper_half * sine_part,
            upper_half * cosine + turn_sign * lower_half * sine_part,
        ],
        axis=-1,
    )
    return turned.reshape(count_rows, -1)


def add_counts(earlier_part, later_part):
    return earlier_part + later_part


def score_block(query_part, key_part, score_scale):
    return (
        jnp.einsum("qhd,khd->hqk", query_part, key_part, preferred_element_type=jnp.float32)
        * score_scale
    )


def grad_block(query_part, dout_part, lse_part, delta_part, key_part, value_part, score_scale):
    probs = jnp.exp(score_block(query_part, key_part, score_scale) - lse_part)
    prob_low = probs.astype(jnp.bfloat16)
    dprob = jnp.einsum("qhd,khd->hqk", dout_part, value_part, preferred_element_type=jnp.float32)
    dscore = (probs * (dprob - delta_part)).astype(jnp.bfloat16)
    return (prob_low, dscore)


def general_body(
    tokens,
    cotangent,
    attn_gain,
    w_query,
    w_key,
    w_value,
    w_out,
    query_gain,
    key_gain,
    ffn_gain,
    router,
    w_gate,
    w_up,
    w_down,
    routes,
    priority,
    positions,
):
    ctx_count = lax.axis_size("ctx")
    (
        g_attn,
        q_weight,
        k_weight,
        v_weight,
        o_weight,
        g_query,
        g_key,
        g_ffn,
        r_weight,
        gate_full,
        up_full,
        down_full,
    ) = (
        lax.all_gather(attn_gain, "fsdp", axis=0, tiled=True),
        lax.all_gather(w_query, "fsdp", axis=0, tiled=True),
        lax.all_gather(w_key, "fsdp", axis=0, tiled=True),
        lax.all_gather(w_value, "fsdp", axis=0, tiled=True),
        lax.all_gather(w_out, "fsdp", axis=0, tiled=True),
        lax.all_gather(query_gain, "fsdp", axis=0, tiled=True),
        lax.all_gather(key_gain, "fsdp", axis=0, tiled=True),
        lax.all_gather(ffn_gain, "fsdp", axis=0, tiled=True),
        lax.all_gather(router, "fsdp", axis=0, tiled=True),
        lax.all_gather(w_gate, "fsdp", axis=1, tiled=True),
        lax.all_gather(w_up, "fsdp", axis=1, tiled=True),
        lax.all_gather(w_down, "fsdp", axis=2, tiled=True),
    )
    gate_weight = gate_full[0]
    up_weight = up_full[0]
    down_weight = down_full[0]
    tok_rows = tokens.shape[1]
    model_width = tokens.shape[2]
    head_dim = HEAD_DIM
    head_count = model_width // head_dim
    length = tok_rows * ctx_count
    top_k = routes.shape[2]
    capacity = 9 * tok_rows
    send_rows = 2 * tok_rows * top_k // ctx_count
    key_block = math.gcd(length, 1024)
    block_count = length // key_block
    score_scale = head_dim ** (-0.5)
    inputs = tokens[0].astype(jnp.float32)
    normed, inv_one = rms_forward(inputs, g_attn)
    h_one = normed.astype(jnp.bfloat16)
    q_lin = product(h_one, q_weight)
    k_lin = product(h_one, k_weight)
    v_lin = product(h_one, v_weight)
    cosine, sine_part = rope_tables(positions[0], head_dim)
    q_normed, inv_query = rms_forward(q_lin, g_query)
    k_normed, inv_key = rms_forward(k_lin, g_key)
    q_rot = rotate(q_normed, cosine, sine_part, head_dim, 1.0).astype(jnp.bfloat16)
    k_rot = rotate(k_normed, cosine, sine_part, head_dim, 1.0).astype(jnp.bfloat16)
    v_low = v_lin.astype(jnp.bfloat16)
    all_keys, all_values = (
        lax.all_gather(k_rot, "ctx", axis=0, tiled=True),
        lax.all_gather(v_low, "ctx", axis=0, tiled=True),
    )
    q_heads = q_rot.reshape(tok_rows, head_count, head_dim)

    def key_slice(block_id):
        start = block_id * key_block
        key_part = lax.dynamic_slice_in_dim(all_keys, start, key_block, 0).reshape(
            key_block, head_count, head_dim
        )
        value_part = lax.dynamic_slice_in_dim(all_values, start, key_block, 0).reshape(
            key_block, head_count, head_dim
        )
        return (key_part, value_part)

    def lse_step(carry, block_id):
        run_max, run_total = carry
        key_part, value_part = key_slice(block_id)
        scores = score_block(q_heads, key_part, score_scale)
        new_max = jnp.maximum(run_max, jnp.max(scores, axis=-1, keepdims=True))
        run_total = run_total * jnp.exp(run_max - new_max) + jnp.sum(
            jnp.exp(scores - new_max), axis=-1, keepdims=True
        )
        return ((new_max, run_total), None)

    start_max = jnp.full((head_count, tok_rows, 1), -jnp.inf, jnp.float32)
    start_total = jnp.zeros((head_count, tok_rows, 1), jnp.float32)
    (run_max, run_total), _ = lax.scan(lse_step, (start_max, start_total), jnp.arange(block_count))
    lse = run_max + jnp.log(run_total)

    def out_step(acc, block_id):
        key_part, value_part = key_slice(block_id)
        probs = jnp.exp(score_block(q_heads, key_part, score_scale) - lse).astype(jnp.bfloat16)
        return (
            acc + jnp.einsum("hqk,khd->qhd", probs, value_part, preferred_element_type=jnp.float32),
            None,
        )

    attended_heads, _ = lax.scan(
        out_step, jnp.zeros((tok_rows, head_count, head_dim), jnp.float32), jnp.arange(block_count)
    )
    attended = attended_heads.reshape(tok_rows, model_width)
    mixed_low = attended.astype(jnp.bfloat16)
    middle = inputs + product(mixed_low, o_weight)
    h_two_f, inv_two = rms_forward(middle, g_ffn)
    h_two = h_two_f.astype(jnp.bfloat16)
    logits = product(h_two, r_weight)
    row_max = jnp.max(logits, axis=-1, keepdims=True)
    exps_raw = jnp.exp(logits - row_max)
    router_probs = exps_raw / jnp.sum(exps_raw, axis=-1, keepdims=True)
    route_ids = routes[0]
    level_ids = priority[0]
    pair_code = level_ids * ctx_count + route_ids
    code_table = (
        pair_code[:, :, None] == jnp.arange(LEVELS * ctx_count, dtype=jnp.int32)[None, None, :]
    ).astype(jnp.float32)
    per_token = jnp.sum(code_table, axis=1)
    before_local = jnp.cumsum(per_token, axis=0) - per_token
    local_total = jnp.sum(per_token, axis=0)
    earlier = prefix(local_total, "ctx", add_counts, jnp.zeros_like(local_total))
    totals = lax.psum(local_total, "ctx")
    level_totals = totals.reshape(LEVELS, ctx_count)
    level_base = (jnp.cumsum(level_totals, axis=0) - level_totals).reshape(-1)
    offsets = before_local + (earlier + level_base)[None, :]
    pair_rank = jnp.sum(code_table * offsets[:, None, :], axis=-1).astype(jnp.int32)
    is_kept = pair_rank < capacity
    expert_hot = (
        route_ids[:, :, None] == jnp.arange(ctx_count, dtype=jnp.int32)[None, None, :]
    ).astype(jnp.float32)
    per_expert = jnp.sum(expert_hot, axis=1)
    local_before = jnp.cumsum(per_expert, axis=0) - per_expert
    local_slot = jnp.sum(expert_hot * local_before[:, None, :], axis=-1).astype(jnp.int32)
    send_index = (route_ids * send_rows + local_slot).reshape(-1)
    pair_count = tok_rows * top_k
    pair_of_slot = (
        jnp.full((ctx_count * send_rows,), pair_count, jnp.int32)
        .at[send_index]
        .set(jnp.arange(pair_count, dtype=jnp.int32))
    )
    slot_target = jnp.where(is_kept, pair_rank, capacity).reshape(-1)
    target_pad = jnp.concatenate([slot_target, jnp.full((1,), capacity, jnp.int32)], axis=0)
    send_slots = target_pad[pair_of_slot].reshape(ctx_count, send_rows)
    h_pad = jnp.concatenate([h_two, jnp.zeros((1, model_width), jnp.bfloat16)], axis=0)
    send_tokens = h_pad[pair_of_slot // top_k].reshape(ctx_count, send_rows, model_width)
    got_tokens, got_slots = (
        lax.all_to_all(send_tokens, "ctx", split_axis=0, concat_axis=0, tiled=True),
        lax.all_to_all(send_slots, "ctx", split_axis=0, concat_axis=0, tiled=True),
    )
    received_count = ctx_count * send_rows
    slots_flat = got_slots.reshape(-1)
    row_of_slot = (
        jnp.full((capacity,), received_count, jnp.int32)
        .at[slots_flat]
        .set(jnp.arange(received_count, dtype=jnp.int32), mode="drop")
    )
    got_pad = jnp.concatenate(
        [
            got_tokens.reshape(received_count, model_width),
            jnp.zeros((1, model_width), jnp.bfloat16),
        ],
        axis=0,
    )
    expert_in = got_pad[row_of_slot]
    gate_lin = product(expert_in, gate_weight)
    up_lin = product(expert_in, up_weight)
    sig_gate = jax.nn.sigmoid(gate_lin)
    silu_val = gate_lin * sig_gate
    swiglu = (silu_val * up_lin).astype(jnp.bfloat16)
    expert_out = product(swiglu, down_weight).astype(jnp.bfloat16)
    out_pad = jnp.concatenate([expert_out, jnp.zeros((1, model_width), jnp.bfloat16)], axis=0)
    back_rows = out_pad[slots_flat].reshape(ctx_count, send_rows, model_width)
    returned = lax.all_to_all(back_rows, "ctx", split_axis=0, concat_axis=0, tiled=True)
    returned_pad = jnp.concatenate(
        [
            returned.reshape(ctx_count * send_rows, model_width),
            jnp.zeros((1, model_width), jnp.bfloat16),
        ],
        axis=0,
    )
    pair_out = returned_pad[send_index].reshape(tok_rows, top_k, model_width)
    chosen = jnp.sum(router_probs[:, None, :] * expert_hot, axis=-1)
    share = jnp.where(is_kept, chosen, 0.0)
    mixture = jnp.einsum("tk,tkd->td", share, pair_out, preferred_element_type=jnp.float32)
    final_rows = middle + mixture
    layer_out = final_rows.astype(jnp.bfloat16)
    grad_out = cotangent[0].astype(jnp.float32)
    routed_grad = (share[:, :, None] * grad_out[:, None, :]).astype(jnp.bfloat16)
    share_grad = jnp.where(
        is_kept,
        jnp.einsum("tkd,td->tk", pair_out, grad_out, preferred_element_type=jnp.float32),
        0.0,
    )
    prob_grad = jnp.sum(expert_hot * share_grad[:, :, None], axis=1)
    logit_grad = router_probs * (
        prob_grad - jnp.sum(router_probs * prob_grad, axis=-1, keepdims=True)
    )
    routed_pad = jnp.concatenate(
        [routed_grad.reshape(pair_count, model_width), jnp.zeros((1, model_width), jnp.bfloat16)],
        axis=0,
    )
    send_grads = routed_pad[pair_of_slot].reshape(ctx_count, send_rows, model_width)
    got_grads = lax.all_to_all(send_grads, "ctx", split_axis=0, concat_axis=0, tiled=True)
    grad_pad = jnp.concatenate(
        [got_grads.reshape(received_count, model_width), jnp.zeros((1, model_width), jnp.bfloat16)],
        axis=0,
    )
    out_grad = grad_pad[row_of_slot]
    act_grad = contract_cols(out_grad, down_weight)
    down_wgrad = contract_rows(swiglu, out_grad)
    gate_grad = (act_grad * up_lin * sig_gate * (1.0 + gate_lin * (1.0 - sig_gate))).astype(
        jnp.bfloat16
    )
    up_grad = (act_grad * silu_val).astype(jnp.bfloat16)
    in_grad = (contract_cols(gate_grad, gate_weight) + contract_cols(up_grad, up_weight)).astype(
        jnp.bfloat16
    )
    gate_wgrad = contract_rows(expert_in, gate_grad)
    up_wgrad = contract_rows(expert_in, up_grad)
    in_pad = jnp.concatenate([in_grad, jnp.zeros((1, model_width), jnp.bfloat16)], axis=0)
    back_grads = in_pad[slots_flat].reshape(ctx_count, send_rows, model_width)
    pair_grads = lax.all_to_all(back_grads, "ctx", split_axis=0, concat_axis=0, tiled=True)
    pair_pad = jnp.concatenate(
        [
            pair_grads.reshape(ctx_count * send_rows, model_width),
            jnp.zeros((1, model_width), jnp.bfloat16),
        ],
        axis=0,
    )
    token_pair = pair_pad[send_index].reshape(tok_rows, top_k, model_width)
    hidden_grad = jnp.sum(token_pair.astype(jnp.float32), axis=1) + precise(
        logit_grad, r_weight.astype(jnp.float32).T
    )
    router_wgrad = precise(h_two.astype(jnp.float32).T, logit_grad)
    norm_grad, ffn_gain_grad = rms_backward(middle, inv_two, g_ffn, hidden_grad)
    middle_grad = grad_out + norm_grad
    branch_grad = middle_grad.astype(jnp.bfloat16)
    out_wgrad = contract_rows(mixed_low, branch_grad)
    mixed_grad = contract_cols(branch_grad, o_weight).astype(jnp.bfloat16)
    dout_heads = mixed_grad.reshape(tok_rows, head_count, head_dim)
    delta = jnp.sum(dout_heads.astype(jnp.float32) * attended_heads, axis=-1).T[:, :, None]

    def back_step(dq_acc, block_id):
        key_part, value_part = key_slice(block_id)
        prob_low, dscore = grad_block(
            q_heads, dout_heads, lse, delta, key_part, value_part, score_scale
        )
        dq_acc = dq_acc + jnp.einsum(
            "hqk,khd->qhd", dscore, key_part, preferred_element_type=jnp.float32
        )
        dk_part = jnp.einsum(
            "hqk,qhd->khd", dscore, q_heads, preferred_element_type=jnp.float32
        ).reshape(key_block, model_width)
        dv_part = jnp.einsum(
            "hqk,qhd->khd", prob_low, dout_heads, preferred_element_type=jnp.float32
        ).reshape(key_block, model_width)
        return (dq_acc, jnp.concatenate([dk_part, dv_part], axis=1))

    dq_heads, kv_terms = lax.scan(
        back_step, jnp.zeros((tok_rows, head_count, head_dim), jnp.float32), jnp.arange(block_count)
    )
    kv_mine = lax.psum_scatter(
        kv_terms.reshape(length, 2 * model_width), "ctx", scatter_dimension=0, tiled=True
    )
    key_grad = kv_mine[:, :model_width] * score_scale
    value_grad = kv_mine[:, model_width:]
    v_lin_low = value_grad.astype(jnp.bfloat16)
    q_grad = dq_heads.reshape(tok_rows, model_width) * score_scale
    q_back = rotate(q_grad, cosine, sine_part, head_dim, -1.0)
    k_back = rotate(key_grad, cosine, sine_part, head_dim, -1.0)
    q_lin_grad, query_gain_grad = rms_backward(q_lin, inv_query, g_query, q_back)
    k_lin_grad, key_gain_grad = rms_backward(k_lin, inv_key, g_key, k_back)
    q_lin_low = q_lin_grad.astype(jnp.bfloat16)
    k_lin_low = k_lin_grad.astype(jnp.bfloat16)
    h_grad = (
        contract_cols(q_lin_low, q_weight)
        + contract_cols(k_lin_low, k_weight)
        + contract_cols(v_lin_low, v_weight)
    )
    query_wgrad = contract_rows(h_one, q_lin_low)
    key_wgrad = contract_rows(h_one, k_lin_low)
    value_wgrad = contract_rows(h_one, v_lin_low)
    in_norm_grad, attn_gain_grad = rms_backward(inputs, inv_one, g_attn, h_grad)
    input_grad = (middle_grad + in_norm_grad).astype(jnp.bfloat16)
    s_gate, s_up, s_down = (
        lax.psum_scatter(
            gate_wgrad[None].astype(jnp.bfloat16), "fsdp", scatter_dimension=1, tiled=True
        ).astype(jnp.float32),
        lax.psum_scatter(
            up_wgrad[None].astype(jnp.bfloat16), "fsdp", scatter_dimension=1, tiled=True
        ).astype(jnp.float32),
        lax.psum_scatter(
            down_wgrad[None].astype(jnp.bfloat16), "fsdp", scatter_dimension=2, tiled=True
        ).astype(jnp.float32),
    )
    d_attn, d_query, d_key, d_value, d_out, d_qgain, d_kgain, d_ffn, d_router = (
        lax.psum_scatter(attn_gain_grad, ("ctx", "fsdp"), scatter_dimension=0, tiled=True),
        lax.psum_scatter(query_wgrad, ("ctx", "fsdp"), scatter_dimension=0, tiled=True),
        lax.psum_scatter(key_wgrad, ("ctx", "fsdp"), scatter_dimension=0, tiled=True),
        lax.psum_scatter(value_wgrad, ("ctx", "fsdp"), scatter_dimension=0, tiled=True),
        lax.psum_scatter(out_wgrad, ("ctx", "fsdp"), scatter_dimension=0, tiled=True),
        lax.psum_scatter(query_gain_grad, ("ctx", "fsdp"), scatter_dimension=0, tiled=True),
        lax.psum_scatter(key_gain_grad, ("ctx", "fsdp"), scatter_dimension=0, tiled=True),
        lax.psum_scatter(ffn_gain_grad, ("ctx", "fsdp"), scatter_dimension=0, tiled=True),
        lax.psum_scatter(router_wgrad, ("ctx", "fsdp"), scatter_dimension=0, tiled=True),
    )
    return (
        layer_out[None],
        input_grad[None],
        d_attn,
        d_query,
        d_key,
        d_value,
        d_out,
        d_qgain,
        d_kgain,
        d_ffn,
        d_router,
        s_gate,
        s_up,
        s_down,
    )


RING = [0, 2, 4, 6, 7, 5, 3, 1]
CHIPS = len(RING)
FAR = CHIPS // 2
EXTRA = 8
PLACES = [1, 7, 2, 6, 3, 5, 0, 4]
CHUNKS = {1: (0, 2), 2: (2, 2), 3: (4, 2), 0: (6, 1), FAR: (7, 1)}
LAST = -1
WIDE_CHUNKS = {1: (0, 2), 2: (2, 2), 3: (4, 2), LAST: (6, 2)}


BRIEF = pl.CostEstimate(flops=0, bytes_accessed=0, transcendentals=0)


def swap(array, axis):
    return lax.ppermute(array, axis, [(0, 1), (1, 0)])


def shift(array, by):
    pairs = [(RING[i], RING[(i + by) % CHIPS]) for i in range(CHIPS)]
    return lax.ppermute(array, "chip", pairs)


def fence(*groups):
    flat = lax.optimization_barrier(tuple(array for group in groups for array in group))
    out, at = [], 0
    for group in groups:
        out.append(list(flat[at : at + len(group)]))
        at += len(group)
    return out


def open_jobs(carried, jobs):
    opened = fence(carried, *[list(inputs) for inputs, _ in jobs])
    return opened[0], [(ins, function) for ins, (_, function) in zip(opened[1:], jobs)]


def run_jobs(jobs):
    return [list(function(*inputs)) for inputs, function in jobs]


class Gather:
    def __init__(self, block, far_by=0):
        self.moving = {1: block, -1: block}
        self.cut = block.shape[0] // 2 // 8 * 8
        self.far_by = far_by
        self.fresh = [block]
        self.step = 0
        self.chunks = {}

    def job(self):
        moving, ways = self.moving, [1, -1]
        if self.step + 1 == FAR and self.far_by:
            ways = [self.far_by]
        elif self.step + 1 == FAR:
            moving = {1: moving[1][: self.cut], -1: moving[-1][self.cut :]}

        def function(*arrays):
            moved = [shift(array, by) for array, by in zip(arrays, ways)]
            self.now = [x for block in arrays[len(ways) :] for x in (block, swap(block, "core"))]
            return [*moved, *self.now]

        return [moving[by] for by in ways] + self.fresh, function

    def take(self, results):
        self.step += 1
        if self.step == FAR:
            count = 1 if self.far_by else 2
            last, self.chunks[FAR - 1] = results[:count], list(results[count:])
            last = jnp.concatenate(last, axis=0) if count == 2 else last[0]
            self.chunks[FAR] = [last, swap(last, "core")]
            self.chunks[LAST] = self.chunks[0] + self.chunks[FAR]
            return
        self.moving[1], self.moving[-1], *self.chunks[self.step - 1] = results
        self.fresh = [self.moving[-1], self.moving[1]]


class Scatter:
    def __init__(self, make, inputs=(), ready=False, far_by=0):
        self.make, self.inputs, self.ready, self.far_by = make, list(inputs), ready, far_by
        self.step = 0
        mine, other = make(FAR, *self.inputs)
        first = mine
        if other is not None:
            first = mine.astype(jnp.float32) + swap(other, "core").astype(jnp.float32)
            first = first.astype(jnp.bfloat16)
        self.rows = first.shape[0]
        self.cut = self.rows // 2 // 8 * 8
        self.carried = [first] if far_by else [first[: self.cut], first[self.cut :]]

    def job(self):
        near = FAR - self.step - 1
        count = len(self.carried)
        ways = [self.far_by] if count == 1 else [1, -1]

        def function(*arrays):
            moved = [shift(array, by) for array, by in zip(arrays, ways)]
            mine, other = self.make(near, *arrays[count:])
            self.mine = mine
            terms = [] if self.ready else [mine]
            return moved + terms + ([] if other is None else [swap(other, "core")])

        return self.carried + self.inputs, function

    def take(self, results):
        self.step += 1
        count = len(self.carried)
        moved, terms = list(results[:count]), list(results[count:])
        if self.ready:
            terms = [self.mine] + terms

        def term(i):
            span = slice(i * self.rows, (i + 1) * self.rows)
            return sum(part[span].astype(jnp.float32) for part in terms)

        moved = [array.astype(jnp.float32) for array in moved]
        if self.step == FAR:
            self.last = [*results[:count], *terms]
            self.total = term(0) + moved[0] + moved[1]
            return
        if count == 1:
            moved = [moved[0], 0.0] if self.far_by == 1 else [0.0, moved[0]]
        elif self.step == 1:
            ahead, behind = moved
            ahead = jnp.concatenate([ahead, jnp.zeros_like(behind)], axis=0)
            behind = jnp.concatenate([jnp.zeros_like(ahead[: self.cut]), behind], axis=0)
            moved = [ahead, behind]
        self.carried = [
            (term(0) + moved[0]).astype(jnp.bfloat16),
            (term(1) + moved[1]).astype(jnp.bfloat16),
        ]


def window(items, jobs=(), loose=()):
    every = [item.job() for item in items] + list(jobs) + list(loose)
    _, opened = open_jobs([], every)
    results = run_jobs(opened)
    count = len(items) + len(jobs)
    results = fence(*results[:count]) + results[count:]
    for item, result in zip(items, results):
        item.take(result)
    return results[len(items) :]


def sum_all(values, jobs):
    (values,), jobs = open_jobs([values], jobs)
    core = lax.axis_index("core")
    both = values + swap(values[:, :, ::-1], "core")

    def heard(by):
        pairs = [
            (2 * RING[i] + c, 2 * RING[(i + (by if c == 0 else -by)) % CHIPS] + c)
            for i in range(CHIPS)
            for c in range(2)
        ]
        return lax.ppermute(both, ("chip", "core"), pairs)

    moved = [heard(by) for by in range(1, FAR + 1)]
    done = run_jobs(jobs)
    moved, *done = fence(moved, *done)
    total = jnp.where(core == 0, both, jnp.roll(moved[-1], -FAR, axis=1))
    for by in range(1, FAR):
        total = total + jnp.where(
            core == 0, jnp.roll(moved[by - 1], -by, axis=1), jnp.roll(moved[by - 1], by, axis=1)
        )
    return total + swap(total[:, :, ::-1], "core"), done


def by_place(values, axis):
    return jnp.stack(
        [lax.index_in_dim(values, PLACES.index(at), axis, False) for at in range(CHIPS)], axis
    )


def by_chunk(values, axis):
    return jnp.stack([lax.index_in_dim(values, at, axis, False) for at in PLACES], axis)


def in_hbm(arrays, specs=None):
    return [
        array
        if specs and specs[i].memory_space == pltpu.SMEM
        else pltpu.with_memory_space_constraint(array, pltpu.HBM)
        for i, array in enumerate(arrays)
    ]


def call(
    kernel, name, inputs, ins, outs, shapes, earlier=(), grid=(1,), scratch=(), mib=56, cost=None,
    free=0,
):
    return pl.pallas_call(
        kernel,
        grid=grid,
        in_specs=ins + [pl.BlockSpec(memory_space=pl.ANY)] * len(earlier),
        out_specs=outs,
        out_shape=shapes,
        scratch_shapes=list(scratch),
        input_output_aliases={len(ins) + i: i for i in range(len(earlier))},
        compiler_params=pltpu.CompilerParams(vmem_limit_bytes=mib << 20),
        cost_estimate=BRIEF if cost is None else cost,
        name=name,
    )(*inputs[:free], *in_hbm(inputs[free:], ins[free:]), *in_hbm(earlier))


def whole(array):
    return pl.BlockSpec(array.shape, lambda i: (0,) * len(array.shape))


def once(array):
    return pl.BlockSpec(
        array.shape, lambda i: (0,) * len(array.shape), pipeline_mode=pl.Buffered(1)
    )


def rows_of(step, tok_rows, cols):
    first, count = WIDE_CHUNKS[step] if step == LAST else CHUNKS[step]
    index = first // count
    return pl.BlockSpec((2 * count * tok_rows, cols), lambda i: (index, 0))


def lin_chunk(step, blocks, weight, gain, place, tok_rows, earlier):
    count, width, cols = len(blocks), weight.shape[0], weight.shape[1]
    length = 2 * CHIPS * tok_rows
    rows, head = count * tok_rows, weight.shape[1] // 3

    def kernel(*refs):
        block_refs, weight_ref, gain_ref, place_ref = refs[:count], *refs[count : count + 3]
        lin_ref, all_ref, sum_ref, tag_ref = refs[-4:]
        lanes = pl.ds(pl.multiple_of(place_ref[0] * tok_rows, tok_rows), tok_rows)
        for i in range(count):
            normed, _ = rms_forward(block_refs[i][:tok_rows].astype(jnp.float32), gain_ref[...])
            all_ref[i * tok_rows : (i + 1) * tok_rows] = normed.astype(jnp.bfloat16)
            levels = block_refs[i][tok_rows:, lanes].astype(jnp.float32)
            others = block_refs[i][tok_rows:, : 3 * tok_rows].astype(jnp.float32)
            tag_ref[i * EXTRA : (i + 1) * EXTRA] = jnp.concatenate(
                [levels[:1]]
                + [others[1:2, k * tok_rows : (k + 1) * tok_rows] for k in range(3)]
                + [jnp.zeros((EXTRA - 4, tok_rows), jnp.float32)],
                axis=0,
            )
        lin = product(all_ref[...], weight_ref[...])
        lin_ref[...] = lin
        line = lax.broadcasted_iota(jnp.int32, (8, head), 0)
        total = jnp.zeros((8, rows), jnp.float32)
        for k in range(2):
            part = lin[:, k * head : (k + 1) * head]
            total = total + lax.dot_general(
                (line == k).astype(jnp.float32),
                part * part,
                (((1,), (1,)), ((), ())),
                precision=lax.Precision.HIGHEST,
                preferred_element_type=jnp.float32,
            )
        sum_ref[...] = total

    tags = jax.ShapeDtypeStruct((count * EXTRA, tok_rows), jnp.float32)
    sums = jax.ShapeDtypeStruct((8, rows), jnp.float32)
    return call(
        kernel,
        "lin",
        [*blocks, weight, gain, place],
        [whole(b) for b in blocks]
        + [whole(weight), whole(gain), pl.BlockSpec(memory_space=pltpu.SMEM)],
        [rows_of(step, tok_rows, cols), rows_of(step, tok_rows, width), whole(sums), whole(tags)],
        [
            jax.ShapeDtypeStruct((length, cols), jnp.float32),
            jax.ShapeDtypeStruct((length, width), jnp.bfloat16),
            sums,
            tags,
        ],
        earlier,
        free=count,
        mib=36,
    )


def both_halves(cosine, sine_part):
    return (
        jnp.concatenate([cosine, cosine], axis=-1),
        jnp.concatenate([-sine_part, sine_part], axis=-1),
    )


def rotate_rows(lin, inverse, gains, cosine, sine_part):
    length, cols = lin.shape
    head = cols // 3
    rows = length // 4

    def kernel(lin_ref, inv_ref, gain_ref, cos_ref, sin_ref, q_ref, k_ref, v_ref):
        cos, sin = both_halves(cos_ref[...], sin_ref[...])
        for k, out_ref in enumerate((q_ref, k_ref)):
            part = lin_ref[:, k * head : (k + 1) * head] * inv_ref[:, k : k + 1]
            part = part * gain_ref[k : k + 1]
            turned = pltpu.roll(part, head // 2, 1)
            out_ref[...] = (part * cos + turned * sin).astype(jnp.bfloat16)
        v_ref[...] = lin_ref[:, 2 * head :].astype(jnp.bfloat16)

    row = lambda width: pl.BlockSpec((rows, width), lambda i: (i, 0))
    return call(
        kernel,
        "rotate",
        [lin, inverse, gains, cosine, sine_part],
        [row(cols), row(2), whole(gains), row(head // 2), row(head // 2)],
        [row(head)] * 3,
        [pltpu.HBM((length, head), jnp.bfloat16)] * 3,
        grid=(4,),
        mib=16,
    )


def attend_chunk(step, queries, keys, values, tok_rows, score_scale):
    count = 2 * CHUNKS[step][1]
    head = keys.shape[1]

    def kernel(q_ref, k_ref, v_ref, out_ref, lse_ref, mine_ref, other_ref):
        for i in range(0, count, 2):
            span = pl.ds(i * tok_rows, 2 * tok_rows)
            scores = contract_cols(q_ref[span], k_ref[...]) * score_scale
            row_max = jnp.max(scores, axis=-1, keepdims=True)
            raw = jnp.exp(scores - row_max)
            total = jnp.sum(raw, axis=-1, keepdims=True)
            probs = (raw / total).astype(jnp.bfloat16)
            mixed = product(probs, v_ref[...]).astype(jnp.bfloat16)
            out_ref[span] = mixed
            lse_ref[span] = row_max + jnp.log(total)
            half = pl.ds(i // 2 * tok_rows, tok_rows)
            mine_ref[half] = mixed[:tok_rows]
            other_ref[half] = mixed[tok_rows:]

    rows = count * tok_rows
    shapes = [
        jax.ShapeDtypeStruct((rows, head), jnp.bfloat16),
        jax.ShapeDtypeStruct((rows, 1), jnp.float32),
    ] + [jax.ShapeDtypeStruct((rows // 2, head), jnp.bfloat16)] * 2
    return call(
        kernel,
        "attend",
        [queries, keys, values],
        [rows_of(step, tok_rows, head), whole(keys), whole(values)],
        [whole(shape) for shape in shapes],
        shapes,
        mib=28,
    )


def pair_product(left, right, left_weight, right_weight, transposed, name, step=None):
    multiply = contract_cols if transposed else product
    width = left_weight.shape[0] if transposed else left_weight.shape[1]
    rows, block = left.shape[0], whole(left)
    if step is not None:
        first, count = CHUNKS[step]
        rows, index = rows * count // CHIPS, first // count
        block = pl.BlockSpec((rows, left.shape[1]), lambda i: (index, 0))

    def kernel(left_ref, right_ref, left_weight_ref, right_weight_ref, out_ref):
        total = multiply(left_ref[...], left_weight_ref[...])
        total = total + multiply(right_ref[...], right_weight_ref[...])
        out_ref[...] = total.astype(jnp.bfloat16)

    shape = jax.ShapeDtypeStruct((rows, width), jnp.bfloat16)
    arrays = [left, right, left_weight, right_weight]
    return call(
        kernel,
        name,
        arrays,
        [block, block, whole(left_weight), whole(right_weight)],
        [whole(shape)],
        [shape],
        mib=16,
    )[0]


def attend_back_chunk(
    step, blocks, queries, lse, keys, values, weight, lin, gains, cosine, sine_part, tok_rows,
    score_scale, earlier, final
):
    count = len(blocks)
    length, head = keys.shape
    width = weight.shape[1]
    rows = count * tok_rows

    def unspun(grad, cosine, sine_part, gain):
        cos, sin = both_halves(cosine, sine_part)
        return (grad * cos - pltpu.roll(grad, head // 2, 1) * sin) * gain

    def line_sums(values):
        ones = jnp.ones((8, head), jnp.float32)
        return lax.dot_general(
            ones,
            values,
            (((1,), (1,)), ((), ())),
            precision=lax.Precision.HIGHEST,
            preferred_element_type=jnp.float32,
        )

    def kernel(*refs):
        block_refs = refs[:count]
        q_ref, lse_ref, lin_ref, cos_ref, sin_ref = refs[count : count + 5]
        k_ref, v_ref, w_ref, gain_ref = refs[count + 5 : count + 9]
        rest = refs[count + 9 :]
        if final:
            k_lin_ref, cos_all, sin_all = rest[:3]
            rest = rest[3:]
        if earlier:
            dk, dv = rest[0][...], rest[1][...]
        else:
            dk, dv = 0.0, 0.0
        dq_ref, all_ref, dk_ref, dv_ref, q_sums = rest[-6:-1] if final else rest[-5:]
        for i in range(count):
            all_ref[i * tok_rows : (i + 1) * tok_rows] = block_refs[i][...]
        for i in range(0, count, 2):
            span = pl.ds(i * tok_rows, 2 * tok_rows)
            queries = q_ref[span]
            douts = contract_cols(all_ref[span], w_ref[...]).astype(jnp.bfloat16)
            probs = jnp.exp(contract_cols(queries, k_ref[...]) * score_scale - lse_ref[span])
            dprobs = contract_cols(douts, v_ref[...])
            delta = jnp.sum(probs * dprobs, axis=-1, keepdims=True)
            dscores = (probs * (dprobs - delta)).astype(jnp.bfloat16)
            dq = product(dscores, k_ref[...]) * score_scale
            dq = unspun(dq, cos_ref[span], sin_ref[span], gain_ref[:1])
            dq_ref[span] = dq
            q_sums[:, i * tok_rows : (i + 2) * tok_rows] = line_sums(dq * lin_ref[span])
            dk = dk + contract_rows(dscores, queries) * score_scale
            dv = dv + contract_rows(probs.astype(jnp.bfloat16), douts)
        if final:
            dk = unspun(dk, cos_all[...], sin_all[...], gain_ref[1:])
            rest[-1][...] = line_sums(dk * k_lin_ref[...])
        dk_ref[...] = dk
        dv_ref[...] = dv

    total = jax.ShapeDtypeStruct((length, head), jnp.float32)
    inputs = [*blocks, queries, lse, lin, cosine, sine_part, keys, values, weight, gains]
    ins = [whole(b) for b in blocks] + [
        rows_of(step, tok_rows, head),
        whole(lse),
        rows_of(step, tok_rows, head),
        rows_of(step, tok_rows, head // 2),
        rows_of(step, tok_rows, head // 2),
        whole(keys),
        whole(values),
        whole(weight),
        whole(gains),
    ]
    sums = [jax.ShapeDtypeStruct((8, rows), jnp.float32)]
    if final:
        inputs += [lin, cosine, sine_part]
        ins += [pl.BlockSpec((length, head), lambda i: (0, 1)), whole(cosine), whole(sine_part)]
        sums += [jax.ShapeDtypeStruct((8, length), jnp.float32)]
    so_far = list(earlier[2:4])
    return pl.pallas_call(
        kernel,
        grid=(1,),
        in_specs=ins
        + [whole(part) for part in so_far]
        + [pl.BlockSpec(memory_space=pl.ANY)] * len(earlier[:2]),
        out_specs=[
            rows_of(step, tok_rows, head),
            rows_of(step, tok_rows, width),
            whole(total),
            whole(total),
        ]
        + [whole(part) for part in sums],
        out_shape=[total, jax.ShapeDtypeStruct((length, width), jnp.bfloat16), total, total] + sums,
        input_output_aliases={
            len(ins): 2,
            len(ins) + 1: 3,
            len(ins) + 2: 0,
            len(ins) + 3: 1,
        }
        if earlier
        else {},
        compiler_params=pltpu.CompilerParams(vmem_limit_bytes=42 << 20),
        cost_estimate=BRIEF,
        name="attend_back",
    )(*blocks, *in_hbm(inputs[count:], ins[count:]), *so_far, *in_hbm(earlier[:2]))


def lin_back_rows(dq, dk, dv, lin, inverse, along, tok_rows):
    length, cols = lin.shape
    head = cols // 3
    places = 2
    rows = 2 * places * tok_rows

    def kernel(dq_ref, dk_ref, dv_ref, lin_ref, inv_ref, along_ref, out_ref, mine_ref, other_ref):
        for k, grad_ref in enumerate((dq_ref, dk_ref)):
            span = slice(k * head, (k + 1) * head)
            inv = inv_ref[:, k : k + 1]
            slope = inv * inv * inv * along_ref[:, k : k + 1]
            out_ref[:, span] = (inv * grad_ref[...] - lin_ref[:, span] * slope).astype(jnp.bfloat16)
        out_ref[:, 2 * head :] = dv_ref[...].astype(jnp.bfloat16)
        for i in range(places):
            to, at = slice(i * tok_rows, (i + 1) * tok_rows), 2 * i * tok_rows
            mine_ref[to] = out_ref[at : at + tok_rows]
            other_ref[to] = out_ref[at + tok_rows : at + 2 * tok_rows]

    row = lambda width: pl.BlockSpec((rows, width), lambda i: (i, 0))
    half = jax.ShapeDtypeStruct((length // 2, cols), jnp.bfloat16)
    return call(
        kernel,
        "lin_back",
        [dq, dk, dv, lin, inverse, along],
        [row(head)] * 3 + [row(cols), row(2), row(2)],
        [row(cols)] + [pl.BlockSpec((places * tok_rows, cols), lambda i: (i, 0))] * 2,
        [pltpu.HBM((length, cols), jnp.bfloat16), pltpu.HBM(half.shape, half.dtype), half],
        grid=(CHIPS // places,),
        mib=16,
    )


EXPERT_COLS = 512


def expert_chunk(step, h_blocks, g_blocks, place, kept, router, gate, up, down, tok_rows, earlier):
    count = len(h_blocks)
    width, hidden = gate.shape
    cols = EXPERT_COLS
    rows = count * tok_rows
    length = 2 * CHIPS * tok_rows
    low = jnp.bfloat16
    first, places = WIDE_CHUNKS[step]
    index = first // places
    inner, outer = hidden // cols, width // cols
    long_rows = tok_rows + EXTRA
    per_tile = cols // tok_rows
    apart = places if step == LAST else 1
    together = places // apart

    def kernel(*refs):
        h_refs, g_refs = refs[:count], refs[count : 2 * count]
        place_ref, kept_ref, router_ref = refs[2 * count : 2 * count + 3]
        gate_ref, up_ref, down_ref, gate_rows, up_rows, down_cols = refs[
            2 * count + 3 : 2 * count + 9
        ]
        outs = refs[2 * count + 9 + len(earlier) : -8]
        row_outs, (act_ref, dgate_ref, dup_ref) = outs[:2], outs[2:5]
        mix_refs, dx_refs = outs[5 : 5 + 2 * apart], outs[5 + 2 * apart :]
        h_all, g_all, act_all, dgate_all, dup_all, share_ref, dshare_ref, sems = refs[-8:]
        turn = pl.program_id(0)

        def copies():
            span = pl.ds(index * rows, rows)
            return [
                pltpu.make_async_copy(source, out.at[span], sems.at[i])
                for i, (source, out) in enumerate(zip((h_all, g_all), row_outs))
            ]

        @pl.when(turn == 0)
        def _():
            for i in range(count):
                h_all[i * tok_rows : (i + 1) * tok_rows] = h_refs[i][...]
                g_all[i * tok_rows : (i + 1) * tok_rows] = g_refs[i][...]
            logits = contract_cols(h_all[...], router_ref[...])
            raw = jnp.exp(logits - jnp.max(logits, axis=-1, keepdims=True))
            probs = raw / jnp.sum(raw, axis=-1, keepdims=True)
            lanes = lax.broadcasted_iota(jnp.int32, probs.shape, 1)
            chosen = jnp.sum(
                jnp.where(lanes == place_ref[0], probs, 0.0), axis=-1, keepdims=True
            )
            share_ref[...] = chosen * kept_ref[...]
            dshare_ref[...] = jnp.zeros_like(dshare_ref)

        @pl.when(turn == 1)
        def _():
            for copy in copies():
                copy.start()

        @pl.when(turn < inner)
        def _():
            share = share_ref[...]
            gate_lin = product(h_all[...], gate_ref[...])
            up_lin = product(h_all[...], up_ref[...])
            back = contract_cols(g_all[...], down_ref[...])
            sig = jax.nn.sigmoid(gate_lin)
            silu = gate_lin * sig
            act = silu * up_lin
            dshare_ref[...] += jnp.sum(act * back, axis=-1, keepdims=True)
            act_low = (act * share).astype(low)
            back = back * share
            dgate = (back * up_lin * (sig * (1.0 + gate_lin * (1.0 - sig)))).astype(low)
            dup = (back * silu).astype(low)
            span = pl.ds(pl.multiple_of(turn * cols, cols), cols)
            for ref, everything, value in (
                (act_ref, act_all, act_low),
                (dgate_ref, dgate_all, dgate),
                (dup_ref, dup_all, dup),
            ):
                ref[...] = value
                everything[:, span] = value

        @pl.when(turn >= inner)
        def _():
            mix = product(act_all[...], down_cols[...]).astype(low)
            dx = contract_cols(dgate_all[...], gate_rows[...])
            dx = (dx + contract_cols(dup_all[...], up_rows[...])).astype(low)
            for i in range(count):
                span = slice(i * tok_rows, (i + 1) * tok_rows)
                to, at = i % 2 + i // 2 // together * 2, i // 2 % together
                mix_refs[to][at * tok_rows : (at + 1) * tok_rows] = mix[span]
                dx_refs[to][at * long_rows : at * long_rows + tok_rows] = dx[span]

            total = dshare_ref[...] * kept_ref[...]
            same = lax.broadcasted_iota(jnp.int32, (tok_rows, tok_rows), 0) == (
                lax.broadcasted_iota(jnp.int32, (tok_rows, tok_rows), 1)
            )
            tile_lanes = lax.broadcasted_iota(jnp.int32, (EXTRA, cols), 1) // tok_rows
            here = tile_lanes + (turn - inner) * per_tile == place_ref[0]
            for i in range(count):
                rest = jnp.sum(
                    jnp.where(same, total[i * tok_rows : (i + 1) * tok_rows], 0.0),
                    axis=0,
                    keepdims=True,
                )
                pieces = []
                for _ in range(3):
                    piece = rest.astype(low).astype(jnp.float32)
                    rest = rest - piece
                    pieces.append(piece)
                pieces.append(jnp.zeros((EXTRA - 3, tok_rows), jnp.float32))
                line = jnp.concatenate(pieces, axis=0)
                line = jnp.concatenate([line] * per_tile, axis=1)
                to, at = i % 2 + i // 2 // together * 2, i // 2 % together
                at = at * long_rows + tok_rows
                dx_refs[to][at : at + EXTRA] = jnp.where(here, line, 0.0).astype(low)

        @pl.when(turn == inner + outer - 1)
        def _():
            for copy in copies():
                copy.wait()

    def inner_at(t):
        return jnp.minimum(t, inner - 1)

    def outer_at(t):
        return jnp.maximum(t - inner, 0)

    tile = pl.BlockSpec((rows, cols), lambda t: (index, inner_at(t)))
    wide = jax.ShapeDtypeStruct((length, hidden), low)
    full = jax.ShapeDtypeStruct((length, width), low)
    half = jax.ShapeDtypeStruct((together * tok_rows, width), low)
    longer = jax.ShapeDtypeStruct((together * long_rows, width), low)
    anywhere = pl.BlockSpec(memory_space=pl.ANY)
    out_tile = lambda shape: pl.BlockSpec((shape.shape[0], cols), lambda t: (0, outer_at(t)))
    return call(
        kernel,
        "expert",
        [*h_blocks, *g_blocks, place, kept, router, gate, up, down, gate, up, down],
        [once(b) for b in [*h_blocks, *g_blocks]]
        + [
            pl.BlockSpec(memory_space=pltpu.SMEM),
            pl.BlockSpec((rows, 1), lambda t: (index, 0)),
            whole(router),
            pl.BlockSpec((width, cols), lambda t: (0, inner_at(t))),
            pl.BlockSpec((width, cols), lambda t: (0, inner_at(t))),
            pl.BlockSpec((cols, width), lambda t: (inner_at(t), 0)),
            pl.BlockSpec((cols, hidden), lambda t: (outer_at(t), 0)),
            pl.BlockSpec((cols, hidden), lambda t: (outer_at(t), 0)),
            pl.BlockSpec((hidden, cols), lambda t: (0, outer_at(t))),
        ],
        [anywhere] * 2
        + [tile] * 3
        + [out_tile(half)] * (2 * apart)
        + [out_tile(longer)] * (2 * apart),
        [full] * 2 + [wide] * 3 + [half] * (2 * apart) + [longer] * (2 * apart),
        earlier,
        grid=(inner + outer,),
        scratch=[pltpu.VMEM((rows, width), low)] * 2
        + [pltpu.VMEM((rows, hidden), low)] * 3
        + [pltpu.VMEM((rows, 1), jnp.float32)] * 2
        + [pltpu.SemaphoreType.DMA((2,))],
        mib=46,
        free=2 * count,
    )


def input_grad_rows(parts, tokens, inverse, gain, grads):
    def kernel(ahead_ref, behind_ref, mine_ref, tokens_ref, inv_ref, gain_ref, grads_ref, out_ref):
        upstream = mine_ref[...].astype(jnp.float32) + ahead_ref[...].astype(jnp.float32)
        upstream = upstream + behind_ref[...].astype(jnp.float32)
        rows = tokens_ref[...].astype(jnp.float32)
        inv = inv_ref[...]
        scaled = upstream * gain_ref[...]
        along = jnp.mean(scaled * rows, axis=-1, keepdims=True)
        norm = inv * scaled - rows * inv * inv * inv * along
        out_ref[...] = (grads_ref[...] + norm).astype(jnp.bfloat16)

    arrays = [*parts, tokens, inverse, gain, grads]
    shape = jax.ShapeDtypeStruct(tokens.shape, jnp.bfloat16)
    return call(
        kernel,
        "input_grad",
        arrays,
        [whole(a) for a in arrays],
        [whole(shape)],
        [shape],
        mib=24,
        free=len(arrays),
    )[0]


THIN = 128
HALF_THIN = THIN // 2


def split_parts(values):
    high = values.astype(jnp.bfloat16).astype(jnp.float32)
    return high, values - high


def dense_chunk(rows_h, grads, weight, columns, narrow, part, own_rows):
    length, width = rows_h.shape
    cols = grads.shape[1]
    block = 256
    runs = block // (2 * own_rows)
    wide = narrow is not None
    first_col, count_col = columns

    def kernel(part_ref, h_ref, grads_ref, weight_ref, *refs):
        kept_ref, sent_ref = refs[-2:] if wide else refs[-3:-1]
        grads = contract_rows(h_ref[...], grads_ref[...].astype(jnp.bfloat16))
        weight = weight_ref[...].astype(jnp.float32)[:, first_col : first_col + count_col]
        term = jnp.sum(grads * weight, axis=-1, keepdims=True)
        both = plain = grads
        if wide:
            narrow = refs[0][...]
            lanes = lax.broadcasted_iota(jnp.int32, narrow.shape, 1)
            narrow = jnp.where(lanes == 17, refs[1][...] + term, narrow)
            high, rest = split_parts(narrow)
            both = jnp.concatenate([both, high, rest], axis=-1)
            plain = jnp.concatenate([plain, narrow, jnp.zeros_like(narrow)], axis=-1)
        else:
            refs[-1][...] = term
        second = part_ref[0] == 1
        for i in range(runs):
            at = 2 * i * own_rows
            first = slice(at, at + own_rows)
            other = slice(at + own_rows, at + 2 * own_rows)
            to = slice(i * own_rows, (i + 1) * own_rows)
            kept_ref[to] = jnp.where(second, plain[other], plain[first])
            sent_ref[to] = jnp.where(second, both[first], both[other]).astype(jnp.bfloat16)

    full = cols + (THIN if wide else 0)
    out = lambda kind: jax.ShapeDtypeStruct((width // 2, full), kind)
    row = lambda size: pl.BlockSpec((block // 2, size), lambda i: (i, 0))
    here = lambda size: pl.BlockSpec((block, size), lambda i: (i, 0))
    return call(
        kernel,
        "dense",
        [part, rows_h, grads, weight] + (list(narrow) if wide else []),
        [
            pl.BlockSpec(memory_space=pltpu.SMEM),
            pl.BlockSpec((length, block), lambda i: (0, i)),
            whole(grads),
            here(weight.shape[1]),
        ]
        + ([here(HALF_THIN), here(1)] if wide else []),
        [row(full), row(full)] + ([] if wide else [here(1)]),
        [out(jnp.float32), out(jnp.bfloat16)]
        + ([] if wide else [jax.ShapeDtypeStruct((width, 1), jnp.float32)]),
        grid=(width // block,),
        mib=24,
        cost=pl.CostEstimate(
            flops=2 * length * width * cols,
            bytes_accessed=2 * length * width + 6 * width * full,
            transcendentals=0,
        ),
    )


def dense_sum(kept, got):
    rows, full = kept.shape
    cols = full - THIN
    block = rows // 4

    def kernel(kept_ref, got_ref, out_ref):
        got = got_ref[...].astype(jnp.float32)
        out_ref[:, :cols] = (kept_ref[:, :cols] + got[:, :cols]).astype(jnp.bfloat16)
        narrow = kept_ref[:, cols : cols + HALF_THIN]
        narrow = narrow + got[:, cols : cols + HALF_THIN] + got[:, cols + HALF_THIN :]
        out_ref[:, cols:] = jnp.concatenate(split_parts(narrow), axis=-1).astype(jnp.bfloat16)

    row = pl.BlockSpec((block, full), lambda i: (i, 0))
    return call(
        kernel,
        "dense_sum",
        [kept, got],
        [row, row],
        [row],
        [jax.ShapeDtypeStruct((rows, full), jnp.bfloat16)],
        grid=(4,),
        mib=16,
    )[0]


def body(
    tokens,
    cotangent,
    attn_gain,
    w_query,
    w_key,
    w_value,
    w_out,
    query_gain,
    key_gain,
    ffn_gain,
    router,
    w_gate,
    w_up,
    w_down,
    routes,
    priority,
    positions,
):
    low = jnp.bfloat16
    ctx_count = 2 * CHIPS
    place = lax.axis_index("chip") * 2 + lax.axis_index("core")
    part = lax.axis_index("fsdp")
    tok_rows, model_width = tokens.shape[1:]
    half_width = model_width // 2
    head_dim = HEAD_DIM
    length = tok_rows * ctx_count
    capacity = 9 * tok_rows
    score_scale = head_dim ** (-0.5)
    per_half = ctx_count // 2
    expert_count = router.shape[1]

    def joined(mine, other, axis):
        return jnp.where(
            part == 0,
            jnp.concatenate([mine, other], axis=axis),
            jnp.concatenate([other, mine], axis=axis),
        )

    def head_rows(matrix, width):
        return lax.dynamic_slice_in_dim(matrix, (place % per_half) * width, width, 0)

    small = jnp.concatenate(
        [
            router.T,
            attn_gain[None],
            ffn_gain[None],
            jnp.concatenate(
                [
                    head_rows(query_gain, head_dim),
                    head_rows(key_gain, head_dim),
                    jnp.zeros((half_width - 2 * head_dim,), low),
                ]
            )[None],
        ],
        axis=0,
    )
    qkv_mine = jnp.concatenate(
        [
            lax.dynamic_slice_in_dim(w, place * head_dim, head_dim, 1)
            for w in (w_query, w_key, w_value)
        ],
        axis=1,
    )
    out_mine = head_rows(w_out, head_dim)

    hot = routes[0][:, :, None] == jnp.arange(expert_count, dtype=jnp.int32)[None, None, :]
    levels = jnp.sum(jnp.where(hot, priority[0][:, :, None] - LEVELS, 0), axis=1) + LEVELS
    spot = positions[0]
    line = jnp.concatenate(
        [spot // 128, spot % 128, jnp.full((model_width - 2 * tok_rows,), place, jnp.int32)]
    )
    tags = jnp.concatenate(
        [
            levels.T.reshape(1, model_width),
            line[None],
            jnp.zeros((EXTRA - 2, model_width), jnp.int32),
        ],
        axis=0,
    ).astype(low)

    inputs = tokens[0].astype(jnp.float32)
    inv_one = lax.rsqrt(jnp.mean(inputs * inputs, axis=-1, keepdims=True) + epsilon)
    first_rows = jnp.concatenate([tokens[0], tags], axis=0)
    place_one = place.astype(jnp.int32).reshape(1)
    ready = ()
    sum_parts, tag_parts = {}, {}

    def lin_job(step, blocks):
        def function():
            made = lin_chunk(
                step, blocks(), qkv_weight, g_attn[None], place_one, tok_rows, ready
            )
            return made

        return [], function

    def lin_keep(step, made):
        nonlocal ready
        ready = tuple(made[:2])
        sum_parts[step], tag_parts[step] = made[2][:2], made[3]

    def other_core(array):
        return (swap(array, "core"),)

    rows_one = Gather(first_rows)

    def to_other(*arrays):
        return [swap(array, "fsdp") for array in arrays]

    (small_other,), (qkv_other,) = window(
        [rows_one], [([small], to_other)], loose=[([qkv_mine], to_other)]
    )
    small_full = joined(small, small_other, 1)
    r_weight = small_full[:expert_count]
    g_attn = small_full[expert_count].astype(jnp.float32)
    g_ffn = small_full[expert_count + 1].astype(jnp.float32)
    here = part == place // per_half
    g_heads = jnp.where(here, small[expert_count + 2], small_other[expert_count + 2]).astype(
        jnp.float32
    )
    g_query, g_key = g_heads[:head_dim], g_heads[head_dim : 2 * head_dim]
    qkv_weight = joined(qkv_mine, qkv_other, 0)

    def expert_weights(_, *own):
        return [lax.all_gather(w, "fsdp", axis=k, tiled=True) for w, k in zip(own, (0, 0, 1))]

    made, expert_own = window(
        [rows_one],
        [lin_job(1, lambda: rows_one.now)],
        loose=[([qkv_other, w_gate[0], w_up[0], w_down[0]], expert_weights)],
    )
    gate_weight, up_weight, down_weight = expert_own
    lin_keep(1, made)
    made, (qkv_pair,) = window(
        [rows_one],
        [lin_job(2, lambda: rows_one.now), ([qkv_weight], other_core)],
    )
    lin_keep(2, made)
    made, (out_other,) = window(
        [rows_one], [lin_job(3, lambda: rows_one.now)], loose=[([out_mine], to_other)]
    )
    out_weight = jnp.where(here, out_mine, out_other)
    lin_keep(3, made)
    lin_keep(LAST, lin_job(LAST, lambda: rows_one.chunks[LAST])[1]())
    lin, all_h_one = ready
    all_tags = jnp.concatenate([tag_parts[step] for step in WIDE_CHUNKS], axis=0).reshape(
        ctx_count, EXTRA, tok_rows
    )

    def token_sums(lines, jobs):
        total, done = sum_all(by_place(lines.reshape(-1, CHIPS, 2, tok_rows), 1), jobs)
        return by_chunk(total, 1).reshape(-1, length).T / model_width, done

    def rank_job(all_tags):
        mine, owner = all_tags[:, 0], all_tags[:, 3, :1]
        order = owner * tok_rows + jnp.arange(tok_rows, dtype=jnp.float32)[None]
        mine = mine.reshape(length)
        code = mine * length + order.reshape(length)
        ranks = jnp.sum((code[None, :] < code[:, None]).astype(jnp.float32), axis=1)
        kept = (mine < LEVELS) & (ranks < capacity)
        return (kept.astype(jnp.float32)[:, None],)

    def rope_job(all_tags):
        spots = (all_tags[:, 1] * 128.0 + all_tags[:, 2]).reshape(-1)
        return [table[:, 0] for table in rope_tables(spots, head_dim)]

    square, ((cosine, sine_part),) = token_sums(
        jnp.concatenate([sum_parts[step] for step in WIDE_CHUNKS], axis=1),
        [([all_tags], rope_job)],
    )
    grads_rows = Gather(cotangent[0], -1)
    grads_inputs, grads_step = grads_rows.job()
    (square,), grads_inputs = fence([square], grads_inputs)
    grads_moved = grads_step(*grads_inputs)
    inverse = lax.rsqrt(square + epsilon)
    gains = jnp.stack([g_query, g_key], axis=0)
    q_rot, k_rot, v_low = rotate_rows(lin, inverse, gains, cosine, sine_part)

    heads = {}

    def attend_job(step):
        return [q_rot, k_rot, v_low], lambda queries, keys, values: attend_chunk(
            step, queries, keys, values, tok_rows, score_scale
        )

    def projected(step, made):
        return pair_product(
            made[2], swap(made[3], "core"), out_weight, out_pair, False, "project"
        )

    def first_job(queries, keys, values):
        made = attend_job(FAR)[1](queries, keys, values)
        return [*made, projected(FAR, made)]

    (out_pair,) = other_core(out_weight)
    (*heads[FAR], far_terms), heads[FAR - 1], grads_moved = window(
        [],
        [
            ([q_rot, k_rot, v_low], first_job),
            attend_job(FAR - 1),
            ([], lambda: grads_moved),
        ],
    )
    grads_rows.take(grads_moved)

    def out_terms(step, *parts):
        return (far_terms if step == FAR else projected(step, parts)), None

    out_sum = Scatter(out_terms)
    for near in range(FAR - 1, -1, -1):
        out_sum.inputs = heads[near]
        jobs = [attend_job(near - 1)] if near else []
        held = [([gate_weight], lambda weight: (weight,)), ([all_tags], rank_job)]
        made = window([out_sum], jobs + (held if near == 2 else []))
        if near == 2:
            (gate_weight,), (kept,) = made[-2:]
        if near:
            heads[near - 1] = made[0]
    mixed_low = jnp.concatenate([heads[step][0] for step in CHUNKS], axis=0)
    middle = inputs + out_sum.total

    h_two_f, inv_two = rms_forward(middle, g_ffn)
    h_two = h_two_f.astype(low)
    grad_out = cotangent[0].astype(jnp.float32)
    filled = ()
    mix_terms, dx_terms = {}, {}

    rows_two = Gather(h_two, 1)
    window([rows_two])

    def expert_job(step, h_blocks, g_blocks):
        return [], lambda: expert_chunk(
            step,
            h_blocks(),
            g_blocks(),
            place_one,
            kept,
            r_weight,
            gate_weight,
            up_weight,
            down_weight,
            tok_rows,
            filled,
        )

    for step in list(range(1, FAR)) + [LAST]:
        if step == LAST:
            run = expert_job(step, lambda: rows_two.chunks[LAST], lambda: grads_rows.chunks[LAST])
            made = run[1]()
        else:
            run = expert_job(step, lambda: rows_two.now, lambda: grads_rows.now)
            (made,) = window([rows_two, grads_rows], [run])
        filled, terms = tuple(made[:5]), made[5:]
        if step == LAST:
            mix_terms[0], mix_terms[FAR] = terms[:2], terms[2:4]
            dx_terms[0], dx_terms[FAR] = terms[4:6], terms[6:]
        else:
            mix_terms[step], dx_terms[step] = terms[:2], terms[2:]
    all_h_two, all_grads, act_low, gate_grad, up_grad = filled

    def wgrad(left, right):
        return (contract_rows(left, right).astype(low),)

    def over_sequences(matrix, axis):
        return lax.psum_scatter(matrix, "fsdp", scatter_dimension=axis, tiled=True)

    logits = contract_cols(h_two, r_weight)
    row_max = jnp.max(logits, axis=-1, keepdims=True)
    exps_raw = jnp.exp(logits - row_max)
    router_probs = exps_raw / jnp.sum(exps_raw, axis=-1, keepdims=True)
    dx_sum = Scatter(lambda step: dx_terms[step], ready=True, far_by=1)
    mix_sum = Scatter(lambda step: mix_terms[step], ready=True, far_by=-1)
    ((gate_wgrad,),) = window([dx_sum, mix_sum], [([all_h_two, gate_grad], wgrad)])
    s_gate = over_sequences(gate_wgrad, 0)
    ((up_wgrad,),) = window([dx_sum], [([all_h_two, up_grad], wgrad)])
    s_up = over_sequences(up_wgrad, 0)
    ((down_wgrad,),) = window([dx_sum], [([act_low, all_grads], wgrad)])
    s_down = over_sequences(down_wgrad, 1)
    window([dx_sum])
    hidden_sum = dx_sum.total

    prob_grad = jnp.sum(hidden_sum[tok_rows : tok_rows + 3], axis=0)
    prob_grad = prob_grad.reshape(expert_count, tok_rows).T
    logit_grad = router_probs * (
        prob_grad - jnp.sum(router_probs * prob_grad, axis=-1, keepdims=True)
    )
    hidden_grad = hidden_sum[:tok_rows] + precise(logit_grad, r_weight.astype(jnp.float32))
    norm_grad, ffn_gain_grad = rms_backward(middle, inv_two, g_ffn, hidden_grad)
    middle_grad = grad_out + norm_grad

    sofar = ()

    q_sums = {}
    rows_da = Gather(middle_grad.astype(low))

    def back_job(step, blocks):
        return [], lambda: attend_back_chunk(
            step,
            blocks(),
            q_rot,
            heads[step][1],
            k_rot,
            v_low,
            out_weight,
            lin,
            gains,
            cosine,
            sine_part,
            tok_rows,
            score_scale,
            sofar,
            step == FAR,
        )

    def widen(array):
        return (array.astype(jnp.float32),)

    def narrow_job(h_two, logit_grad, ffn_gain_grad):
        return (
            jnp.concatenate(
                [
                    precise(h_two.astype(jnp.float32).T, logit_grad),
                    ffn_gain_grad[:, None],
                    jnp.zeros((model_width, HALF_THIN - expert_count - 1), jnp.float32),
                ],
                axis=1,
            ),
        )

    besides = {0: [], 1: [mix_sum], 2: [], 3: [mix_sum]}
    also = {0: [([s_gate], widen)], 1: [([h_two, logit_grad, ffn_gain_grad], narrow_job)]}
    for step in range(FAR + 1):
        if step == FAR:
            *made, k_sums = back_job(step, lambda: rows_da.chunks[FAR])[1]()
        else:
            made, *wide = window(
                [rows_da] + besides[step], [back_job(step, lambda: rows_da.now)] + also.get(step, [])
            )
            if step == 0:
                ((s_gate,),) = wide
            if step == 1:
                ((narrow,),) = wide
        sofar, q_sums[step] = tuple(made[:4]), made[4]
    dq, all_branch, dk, dv = sofar

    def out_job(mixed_low, all_branch):
        return (contract_rows(mixed_low, all_branch),)

    own_rows = model_width // (2 * ctx_count)
    part_one = part.astype(jnp.int32).reshape(1)

    def value_job(all_h_one, dv):
        return dense_chunk(
            all_h_one, dv, qkv_weight, (2 * head_dim, head_dim), None,
            part_one, own_rows,
        )

    along, ((v_kept, v_sent, v_term),) = token_sums(
        jnp.stack(
            [jnp.concatenate([q_sums[step][0] for step in CHUNKS], axis=0), k_sums[0]], axis=0
        ),
        [
            ([all_h_one, dv], value_job),
        ],
    )
    mix_inputs, mix_step = mix_sum.job()
    (along,), mix_inputs = fence([along], mix_inputs)
    mix_moved = mix_step(*mix_inputs)
    lin_grad, lin_mine, lin_theirs = lin_back_rows(dq, dk, dv, lin, inverse, along, tok_rows)
    lin_theirs = swap(lin_theirs, "core")


    def pick(blocks, index):
        return lax.dynamic_index_in_dim(blocks, index, 1, False)

    def dense_job(all_h_one, lin_grad, *narrow):
        return dense_chunk(
            all_h_one, lin_grad[:, : 2 * head_dim], qkv_weight, (0, 2 * head_dim), narrow,
            part_one, own_rows,
        )

    def out_swap_job(out_sent, dq, dk, lin):
        gain_rows = jnp.stack(
            [
                jnp.sum(
                    grad * lin[:, k * head_dim : (k + 1) * head_dim] * inverse[:, k : k + 1], axis=0
                )
                for k, grad in enumerate((dq, dk))
            ],
            axis=0,
        )
        gain_rows = (gain_rows / gains).reshape(2, 2, own_rows)
        return swap(out_sent, "fsdp"), swap(pick(gain_rows, 1 - part), "fsdp"), pick(gain_rows, part)

    def h_terms(step, lin_mine, lin_theirs):
        return (
            pair_product(lin_mine, lin_theirs, qkv_weight, qkv_pair, True, "h_terms", step),
            None,
        )

    h_sum = Scatter(h_terms, [lin_mine, lin_theirs])
    def swap_job(sent):
        return (swap(sent, "fsdp"),)

    def owners_job(payload):
        blocks = payload.reshape(ctx_count, own_rows, -1)
        return (lax.all_to_all(blocks, ("chip", "core"), 0, 0, tiled=True),)

    (kept, sent), mix_moved, (v_got,) = window(
        [h_sum],
        [([all_h_one, lin_grad, narrow, v_term], dense_job), ([], lambda: mix_moved)],
        loose=[([v_sent], swap_job)],
    )
    mix_sum.take(mix_moved)
    layer_out = (middle + mix_sum.total).astype(low)
    (got,), (out_wgrad,), (v_received,) = window(
        [h_sum],
        [([sent], swap_job), ([mixed_low, all_branch], out_job)],
        loose=[([(v_kept + v_got.astype(jnp.float32)).astype(low)], owners_job)],
    )
    out_rows = out_wgrad.reshape(1, 2, own_rows, model_width)
    (received,), (out_got, gain_got, gain_kept) = window(
        [h_sum],
        loose=[
            ([kept, got], lambda kept, got: owners_job(dense_sum(kept, got))),
            ([pick(out_rows, 1 - part)[0].astype(low), dq, dk, lin], out_swap_job),
        ],
    )

    (v_received,), (received,), (out_got, gain_got), (s_up,), (s_down,) = window(
        [h_sum],
        [
            ([], lambda: (v_received,)),
            ([], lambda: (received,)),
            ([], lambda: (out_got, gain_got)),
            ([s_up], widen),
            ([s_down], widen),
        ],
    )
    d_out = pick(out_rows, part)[0] + out_got.astype(jnp.float32)
    gain_sum = gain_kept + gain_got
    d_qgain, d_kgain = gain_sum[0], gain_sum[1]
    s_gate, s_up, s_down = s_gate[None], s_up[None], s_down[None]
    input_grad = input_grad_rows(h_sum.last, tokens[0], inv_one, g_attn[None], middle_grad)
    d_query, d_key, d_value = (
        columns.transpose(1, 0, 2).reshape(own_rows, model_width).astype(jnp.float32)
        for columns in (received[:, :, :head_dim], received[:, :, head_dim : 2 * head_dim], v_received)
    )
    thin_sum = jnp.sum(received[:, :, 2 * head_dim :].astype(jnp.float32), axis=0)
    thin_sum = thin_sum[:, :HALF_THIN] + thin_sum[:, HALF_THIN:]
    d_router = thin_sum[:, :expert_count]
    own_gain = lax.dynamic_slice_in_dim(g_attn, (2 * place + part) * own_rows, own_rows, 0)
    d_ffn, d_attn = thin_sum[:, expert_count], thin_sum[:, expert_count + 1] / own_gain
    return (
        layer_out[None],
        input_grad[None],
        d_attn,
        d_query,
        d_key,
        d_value,
        d_out,
        d_qgain,
        d_kgain,
        d_ffn,
        d_router,
        s_gate,
        s_up,
        s_down,
    )


def specs_of(ctx):
    rows, both = P("fsdp", ctx, None), ctx + ("fsdp",)
    dense = P("fsdp", None)
    ins = (
        rows,
        rows,
        P("fsdp"),
        dense,
        dense,
        dense,
        dense,
        P("fsdp"),
        P("fsdp"),
        P("fsdp"),
        dense,
        P(ctx, "fsdp", None),
        P(ctx, "fsdp", None),
        P(ctx, None, "fsdp"),
        rows,
        rows,
        P("fsdp", ctx),
    )
    line, matrix = P(both), P(both, None)
    outs = (
        rows,
        rows,
        line,
        matrix,
        matrix,
        matrix,
        matrix,
        line,
        line,
        line,
        matrix,
        P(ctx, "fsdp", None),
        P(ctx, "fsdp", None),
        P(ctx, None, "fsdp"),
    )
    return ins, outs


def solution(mesh):
    ctx_count, fsdp_count = mesh.shape["ctx"], mesh.shape["fsdp"]

    def whole(*arrays):
        heads = arrays[0].shape[2] // HEAD_DIM
        experts = arrays[10].shape[1]
        if ctx_count == 2 * CHIPS == heads == experts and fsdp_count == 2:
            chips = Mesh(mesh.devices.reshape(-1, 2, 2), ("chip", "core", "fsdp"))
            run, grid, ctx = body, chips, ("chip", "core")
        else:
            run, grid, ctx = general_body, mesh, ("ctx",)
        ins, outs = specs_of(ctx)
        return jax.shard_map(run, mesh=grid, in_specs=ins, out_specs=outs, check_vma=False)(*arrays)

    return whole
```

```python
import math

import jax
import jax.numpy as jnp
from jax import lax
from jax.experimental import pallas as pl
from jax.experimental.pallas import tpu as pltpu
from jax.sharding import Mesh
from jax.sharding import PartitionSpec as P

HEAD_DIM = 128
LEVELS = 4


epsilon = 1e-05
rope_base = 50000.0


def prefix(part, axis, combine, identity):
    place = lax.axis_index(axis)
    gathered = lax.all_gather(part, axis)
    state = jnp.zeros_like(part) + jnp.asarray(identity, part.dtype)

    def one(turn, state):
        return combine(state, lax.dynamic_index_in_dim(gathered, turn, 0, False))

    return lax.fori_loop(0, place, one, state)


def product(left, right):
    return jnp.dot(left, right, preferred_element_type=jnp.float32)


def precise(left, right):
    return jnp.dot(left, right, precision=lax.Precision.HIGHEST, preferred_element_type=jnp.float32)


def contract_rows(left, right):
    return lax.dot_general(
        left, right, (((0,), (0,)), ((), ())), preferred_element_type=jnp.float32
    )


def contract_cols(left, right):
    return lax.dot_general(
        left, right, (((1,), (1,)), ((), ())), preferred_element_type=jnp.float32
    )


def rms_forward(matrix, gain_row):
    inverse = lax.rsqrt(jnp.mean(matrix * matrix, axis=-1, keepdims=True) + epsilon)
    return (matrix * inverse * gain_row, inverse)


def rms_backward(matrix, inverse, gain_row, upstream):
    scaled = upstream * gain_row
    along = jnp.mean(scaled * matrix, axis=-1, keepdims=True)
    grad_rows = inverse * scaled - matrix * inverse * inverse * inverse * along
    grad_gain = jnp.sum(upstream * matrix * inverse, axis=0)
    return (grad_rows, grad_gain)


def rope_tables(position_ids, head_dim):
    half_dim = head_dim // 2
    inverse = rope_base ** (-(jnp.arange(half_dim, dtype=jnp.float32) * 2.0) / head_dim)
    angles = position_ids.astype(jnp.float32)[:, None] * inverse[None, :]
    return (jnp.cos(angles)[:, None, :], jnp.sin(angles)[:, None, :])


def rotate(matrix, cosine, sine_part, head_dim, turn_sign):
    count_rows = matrix.shape[0]
    by_head = matrix.reshape(count_rows, -1, head_dim)
    half_dim = head_dim // 2
    lower_half = by_head[..., :half_dim]
    upper_half = by_head[..., half_dim:]
    turned = jnp.concatenate(
        [
            lower_half * cosine - turn_sign * upper_half * sine_part,
            upper_half * cosine + turn_sign * lower_half * sine_part,
        ],
        axis=-1,
    )
    return turned.reshape(count_rows, -1)


def add_counts(earlier_part, later_part):
    return earlier_part + later_part


def score_block(query_part, key_part, score_scale):
    return (
        jnp.einsum("qhd,khd->hqk", query_part, key_part, preferred_element_type=jnp.float32)
        * score_scale
    )


def grad_block(query_part, dout_part, lse_part, delta_part, key_part, value_part, score_scale):
    probs = jnp.exp(score_block(query_part, key_part, score_scale) - lse_part)
    prob_low = probs.astype(jnp.bfloat16)
    dprob = jnp.einsum("qhd,khd->hqk", dout_part, value_part, preferred_element_type=jnp.float32)
    dscore = (probs * (dprob - delta_part)).astype(jnp.bfloat16)
    return (prob_low, dscore)


def general_body(
    tokens,
    cotangent,
    attn_gain,
    w_query,
    w_key,
    w_value,
    w_out,
    query_gain,
    key_gain,
    ffn_gain,
    router,
    w_gate,
    w_up,
    w_down,
    routes,
    priority,
    positions,
):
    ctx_count = lax.axis_size("ctx")
    (
        g_attn,
        q_weight,
        k_weight,
        v_weight,
        o_weight,
        g_query,
        g_key,
        g_ffn,
        r_weight,
        gate_full,
        up_full,
        down_full,
    ) = (
        lax.all_gather(attn_gain, "fsdp", axis=0, tiled=True),
        lax.all_gather(w_query, "fsdp", axis=0, tiled=True),
        lax.all_gather(w_key, "fsdp", axis=0, tiled=True),
        lax.all_gather(w_value, "fsdp", axis=0, tiled=True),
        lax.all_gather(w_out, "fsdp", axis=0, tiled=True),
        lax.all_gather(query_gain, "fsdp", axis=0, tiled=True),
        lax.all_gather(key_gain, "fsdp", axis=0, tiled=True),
        lax.all_gather(ffn_gain, "fsdp", axis=0, tiled=True),
        lax.all_gather(router, "fsdp", axis=0, tiled=True),
        lax.all_gather(w_gate, "fsdp", axis=1, tiled=True),
        lax.all_gather(w_up, "fsdp", axis=1, tiled=True),
        lax.all_gather(w_down, "fsdp", axis=2, tiled=True),
    )
    gate_weight = gate_full[0]
    up_weight = up_full[0]
    down_weight = down_full[0]
    tok_rows = tokens.shape[1]
    model_width = tokens.shape[2]
    head_dim = HEAD_DIM
    head_count = model_width // head_dim
    length = tok_rows * ctx_count
    top_k = routes.shape[2]
    capacity = 9 * tok_rows
    send_rows = 2 * tok_rows * top_k // ctx_count
    key_block = math.gcd(length, 1024)
    block_count = length // key_block
    score_scale = head_dim ** (-0.5)
    inputs = tokens[0].astype(jnp.float32)
    normed, inv_one = rms_forward(inputs, g_attn)
    h_one = normed.astype(jnp.bfloat16)
    q_lin = product(h_one, q_weight)
    k_lin = product(h_one, k_weight)
    v_lin = product(h_one, v_weight)
    cosine, sine_part = rope_tables(positions[0], head_dim)
    q_normed, inv_query = rms_forward(q_lin, g_query)
    k_normed, inv_key = rms_forward(k_lin, g_key)
    q_rot = rotate(q_normed, cosine, sine_part, head_dim, 1.0).astype(jnp.bfloat16)
    k_rot = rotate(k_normed, cosine, sine_part, head_dim, 1.0).astype(jnp.bfloat16)
    v_low = v_lin.astype(jnp.bfloat16)
    all_keys, all_values = (
        lax.all_gather(k_rot, "ctx", axis=0, tiled=True),
        lax.all_gather(v_low, "ctx", axis=0, tiled=True),
    )
    q_heads = q_rot.reshape(tok_rows, head_count, head_dim)

    def key_slice(block_id):
        start = block_id * key_block
        key_part = lax.dynamic_slice_in_dim(all_keys, start, key_block, 0).reshape(
            key_block, head_count, head_dim
        )
        value_part = lax.dynamic_slice_in_dim(all_values, start, key_block, 0).reshape(
            key_block, head_count, head_dim
        )
        return (key_part, value_part)

    def lse_step(carry, block_id):
        run_max, run_total = carry
        key_part, value_part = key_slice(block_id)
        scores = score_block(q_heads, key_part, score_scale)
        new_max = jnp.maximum(run_max, jnp.max(scores, axis=-1, keepdims=True))
        run_total = run_total * jnp.exp(run_max - new_max) + jnp.sum(
            jnp.exp(scores - new_max), axis=-1, keepdims=True
        )
        return ((new_max, run_total), None)

    start_max = jnp.full((head_count, tok_rows, 1), -jnp.inf, jnp.float32)
    start_total = jnp.zeros((head_count, tok_rows, 1), jnp.float32)
    (run_max, run_total), _ = lax.scan(lse_step, (start_max, start_total), jnp.arange(block_count))
    lse = run_max + jnp.log(run_total)

    def out_step(acc, block_id):
        key_part, value_part = key_slice(block_id)
        probs = jnp.exp(score_block(q_heads, key_part, score_scale) - lse).astype(jnp.bfloat16)
        return (
            acc + jnp.einsum("hqk,khd->qhd", probs, value_part, preferred_element_type=jnp.float32),
            None,
        )

    attended_heads, _ = lax.scan(
        out_step, jnp.zeros((tok_rows, head_count, head_dim), jnp.float32), jnp.arange(block_count)
    )
    attended = attended_heads.reshape(tok_rows, model_width)
    mixed_low = attended.astype(jnp.bfloat16)
    middle = inputs + product(mixed_low, o_weight)
    h_two_f, inv_two = rms_forward(middle, g_ffn)
    h_two = h_two_f.astype(jnp.bfloat16)
    logits = product(h_two, r_weight)
    row_max = jnp.max(logits, axis=-1, keepdims=True)
    exps_raw = jnp.exp(logits - row_max)
    router_probs = exps_raw / jnp.sum(exps_raw, axis=-1, keepdims=True)
    route_ids = routes[0]
    level_ids = priority[0]
    pair_code = level_ids * ctx_count + route_ids
    code_table = (
        pair_code[:, :, None] == jnp.arange(LEVELS * ctx_count, dtype=jnp.int32)[None, None, :]
    ).astype(jnp.float32)
    per_token = jnp.sum(code_table, axis=1)
    before_local = jnp.cumsum(per_token, axis=0) - per_token
    local_total = jnp.sum(per_token, axis=0)
    earlier = prefix(local_total, "ctx", add_counts, jnp.zeros_like(local_total))
    totals = lax.psum(local_total, "ctx")
    level_totals = totals.reshape(LEVELS, ctx_count)
    level_base = (jnp.cumsum(level_totals, axis=0) - level_totals).reshape(-1)
    offsets = before_local + (earlier + level_base)[None, :]
    pair_rank = jnp.sum(code_table * offsets[:, None, :], axis=-1).astype(jnp.int32)
    is_kept = pair_rank < capacity
    expert_hot = (
        route_ids[:, :, None] == jnp.arange(ctx_count, dtype=jnp.int32)[None, None, :]
    ).astype(jnp.float32)
    per_expert = jnp.sum(expert_hot, axis=1)
    local_before = jnp.cumsum(per_expert, axis=0) - per_expert
    local_slot = jnp.sum(expert_hot * local_before[:, None, :], axis=-1).astype(jnp.int32)
    send_index = (route_ids * send_rows + local_slot).reshape(-1)
    pair_count = tok_rows * top_k
    pair_of_slot = (
        jnp.full((ctx_count * send_rows,), pair_count, jnp.int32)
        .at[send_index]
        .set(jnp.arange(pair_count, dtype=jnp.int32))
    )
    slot_target = jnp.where(is_kept, pair_rank, capacity).reshape(-1)
    target_pad = jnp.concatenate([slot_target, jnp.full((1,), capacity, jnp.int32)], axis=0)
    send_slots = target_pad[pair_of_slot].reshape(ctx_count, send_rows)
    h_pad = jnp.concatenate([h_two, jnp.zeros((1, model_width), jnp.bfloat16)], axis=0)
    send_tokens = h_pad[pair_of_slot // top_k].reshape(ctx_count, send_rows, model_width)
    got_tokens, got_slots = (
        lax.all_to_all(send_tokens, "ctx", split_axis=0, concat_axis=0, tiled=True),
        lax.all_to_all(send_slots, "ctx", split_axis=0, concat_axis=0, tiled=True),
    )
    received_count = ctx_count * send_rows
    slots_flat = got_slots.reshape(-1)
    row_of_slot = (
        jnp.full((capacity,), received_count, jnp.int32)
        .at[slots_flat]
        .set(jnp.arange(received_count, dtype=jnp.int32), mode="drop")
    )
    got_pad = jnp.concatenate(
        [
            got_tokens.reshape(received_count, model_width),
            jnp.zeros((1, model_width), jnp.bfloat16),
        ],
        axis=0,
    )
    expert_in = got_pad[row_of_slot]
    gate_lin = product(expert_in, gate_weight)
    up_lin = product(expert_in, up_weight)
    sig_gate = jax.nn.sigmoid(gate_lin)
    silu_val = gate_lin * sig_gate
    swiglu = (silu_val * up_lin).astype(jnp.bfloat16)
    expert_out = product(swiglu, down_weight).astype(jnp.bfloat16)
    out_pad = jnp.concatenate([expert_out, jnp.zeros((1, model_width), jnp.bfloat16)], axis=0)
    back_rows = out_pad[slots_flat].reshape(ctx_count, send_rows, model_width)
    returned = lax.all_to_all(back_rows, "ctx", split_axis=0, concat_axis=0, tiled=True)
    returned_pad = jnp.concatenate(
        [
            returned.reshape(ctx_count * send_rows, model_width),
            jnp.zeros((1, model_width), jnp.bfloat16),
        ],
        axis=0,
    )
    pair_out = returned_pad[send_index].reshape(tok_rows, top_k, model_width)
    chosen = jnp.sum(router_probs[:, None, :] * expert_hot, axis=-1)
    share = jnp.where(is_kept, chosen, 0.0)
    mixture = jnp.einsum("tk,tkd->td", share, pair_out, preferred_element_type=jnp.float32)
    final_rows = middle + mixture
    layer_out = final_rows.astype(jnp.bfloat16)
    grad_out = cotangent[0].astype(jnp.float32)
    routed_grad = (share[:, :, None] * grad_out[:, None, :]).astype(jnp.bfloat16)
    share_grad = jnp.where(
        is_kept,
        jnp.einsum("tkd,td->tk", pair_out, grad_out, preferred_element_type=jnp.float32),
        0.0,
    )
    prob_grad = jnp.sum(expert_hot * share_grad[:, :, None], axis=1)
    logit_grad = router_probs * (
        prob_grad - jnp.sum(router_probs * prob_grad, axis=-1, keepdims=True)
    )
    routed_pad = jnp.concatenate(
        [routed_grad.reshape(pair_count, model_width), jnp.zeros((1, model_width), jnp.bfloat16)],
        axis=0,
    )
    send_grads = routed_pad[pair_of_slot].reshape(ctx_count, send_rows, model_width)
    got_grads = lax.all_to_all(send_grads, "ctx", split_axis=0, concat_axis=0, tiled=True)
    grad_pad = jnp.concatenate(
        [got_grads.reshape(received_count, model_width), jnp.zeros((1, model_width), jnp.bfloat16)],
        axis=0,
    )
    out_grad = grad_pad[row_of_slot]
    act_grad = contract_cols(out_grad, down_weight)
    down_wgrad = contract_rows(swiglu, out_grad)
    gate_grad = (act_grad * up_lin * sig_gate * (1.0 + gate_lin * (1.0 - sig_gate))).astype(
        jnp.bfloat16
    )
    up_grad = (act_grad * silu_val).astype(jnp.bfloat16)
    in_grad = (contract_cols(gate_grad, gate_weight) + contract_cols(up_grad, up_weight)).astype(
        jnp.bfloat16
    )
    gate_wgrad = contract_rows(expert_in, gate_grad)
    up_wgrad = contract_rows(expert_in, up_grad)
    in_pad = jnp.concatenate([in_grad, jnp.zeros((1, model_width), jnp.bfloat16)], axis=0)
    back_grads = in_pad[slots_flat].reshape(ctx_count, send_rows, model_width)
    pair_grads = lax.all_to_all(back_grads, "ctx", split_axis=0, concat_axis=0, tiled=True)
    pair_pad = jnp.concatenate(
        [
            pair_grads.reshape(ctx_count * send_rows, model_width),
            jnp.zeros((1, model_width), jnp.bfloat16),
        ],
        axis=0,
    )
    token_pair = pair_pad[send_index].reshape(tok_rows, top_k, model_width)
    hidden_grad = jnp.sum(token_pair.astype(jnp.float32), axis=1) + precise(
        logit_grad, r_weight.astype(jnp.float32).T
    )
    router_wgrad = precise(h_two.astype(jnp.float32).T, logit_grad)
    norm_grad, ffn_gain_grad = rms_backward(middle, inv_two, g_ffn, hidden_grad)
    middle_grad = grad_out + norm_grad
    branch_grad = middle_grad.astype(jnp.bfloat16)
    out_wgrad = contract_rows(mixed_low, branch_grad)
    mixed_grad = contract_cols(branch_grad, o_weight).astype(jnp.bfloat16)
    dout_heads = mixed_grad.reshape(tok_rows, head_count, head_dim)
    delta = jnp.sum(dout_heads.astype(jnp.float32) * attended_heads, axis=-1).T[:, :, None]

    def back_step(dq_acc, block_id):
        key_part, value_part = key_slice(block_id)
        prob_low, dscore = grad_block(
            q_heads, dout_heads, lse, delta, key_part, value_part, score_scale
        )
        dq_acc = dq_acc + jnp.einsum(
            "hqk,khd->qhd", dscore, key_part, preferred_element_type=jnp.float32
        )
        dk_part = jnp.einsum(
            "hqk,qhd->khd", dscore, q_heads, preferred_element_type=jnp.float32
        ).reshape(key_block, model_width)
        dv_part = jnp.einsum(
            "hqk,qhd->khd", prob_low, dout_heads, preferred_element_type=jnp.float32
        ).reshape(key_block, model_width)
        return (dq_acc, jnp.concatenate([dk_part, dv_part], axis=1))

    dq_heads, kv_terms = lax.scan(
        back_step, jnp.zeros((tok_rows, head_count, head_dim), jnp.float32), jnp.arange(block_count)
    )
    kv_mine = lax.psum_scatter(
        kv_terms.reshape(length, 2 * model_width), "ctx", scatter_dimension=0, tiled=True
    )
    key_grad = kv_mine[:, :model_width] * score_scale
    value_grad = kv_mine[:, model_width:]
    v_lin_low = value_grad.astype(jnp.bfloat16)
    q_grad = dq_heads.reshape(tok_rows, model_width) * score_scale
    q_back = rotate(q_grad, cosine, sine_part, head_dim, -1.0)
    k_back = rotate(key_grad, cosine, sine_part, head_dim, -1.0)
    q_lin_grad, query_gain_grad = rms_backward(q_lin, inv_query, g_query, q_back)
    k_lin_grad, key_gain_grad = rms_backward(k_lin, inv_key, g_key, k_back)
    q_lin_low = q_lin_grad.astype(jnp.bfloat16)
    k_lin_low = k_lin_grad.astype(jnp.bfloat16)
    h_grad = (
        contract_cols(q_lin_low, q_weight)
        + contract_cols(k_lin_low, k_weight)
        + contract_cols(v_lin_low, v_weight)
    )
    query_wgrad = contract_rows(h_one, q_lin_low)
    key_wgrad = contract_rows(h_one, k_lin_low)
    value_wgrad = contract_rows(h_one, v_lin_low)
    in_norm_grad, attn_gain_grad = rms_backward(inputs, inv_one, g_attn, h_grad)
    input_grad = (middle_grad + in_norm_grad).astype(jnp.bfloat16)
    s_gate, s_up, s_down = (
        lax.psum_scatter(
            gate_wgrad[None].astype(jnp.bfloat16), "fsdp", scatter_dimension=1, tiled=True
        ).astype(jnp.float32),
        lax.psum_scatter(
            up_wgrad[None].astype(jnp.bfloat16), "fsdp", scatter_dimension=1, tiled=True
        ).astype(jnp.float32),
        lax.psum_scatter(
            down_wgrad[None].astype(jnp.bfloat16), "fsdp", scatter_dimension=2, tiled=True
        ).astype(jnp.float32),
    )
    d_attn, d_query, d_key, d_value, d_out, d_qgain, d_kgain, d_ffn, d_router = (
        lax.psum_scatter(attn_gain_grad, ("ctx", "fsdp"), scatter_dimension=0, tiled=True),
        lax.psum_scatter(query_wgrad, ("ctx", "fsdp"), scatter_dimension=0, tiled=True),
        lax.psum_scatter(key_wgrad, ("ctx", "fsdp"), scatter_dimension=0, tiled=True),
        lax.psum_scatter(value_wgrad, ("ctx", "fsdp"), scatter_dimension=0, tiled=True),
        lax.psum_scatter(out_wgrad, ("ctx", "fsdp"), scatter_dimension=0, tiled=True),
        lax.psum_scatter(query_gain_grad, ("ctx", "fsdp"), scatter_dimension=0, tiled=True),
        lax.psum_scatter(key_gain_grad, ("ctx", "fsdp"), scatter_dimension=0, tiled=True),
        lax.psum_scatter(ffn_gain_grad, ("ctx", "fsdp"), scatter_dimension=0, tiled=True),
        lax.psum_scatter(router_wgrad, ("ctx", "fsdp"), scatter_dimension=0, tiled=True),
    )
    return (
        layer_out[None],
        input_grad[None],
        d_attn,
        d_query,
        d_key,
        d_value,
        d_out,
        d_qgain,
        d_kgain,
        d_ffn,
        d_router,
        s_gate,
        s_up,
        s_down,
    )


RING = [0, 2, 4, 6, 7, 5, 3, 1]
CHIPS = len(RING)
FAR = CHIPS // 2
EXTRA = 8
PLACES = [1, 7, 2, 6, 3, 5, 0, 4]
CHUNKS = {1: (0, 2), 2: (2, 2), 3: (4, 2), 0: (6, 1), FAR: (7, 1)}
LAST = -1
WIDE_CHUNKS = {1: (0, 2), 2: (2, 2), 3: (4, 2), LAST: (6, 2)}


BRIEF = pl.CostEstimate(flops=0, bytes_accessed=0, transcendentals=0)


def swap(array, axis):
    return lax.ppermute(array, axis, [(0, 1), (1, 0)])


def shift(array, by):
    pairs = [(RING[i], RING[(i + by) % CHIPS]) for i in range(CHIPS)]
    return lax.ppermute(array, "chip", pairs)


def fence(*groups):
    flat = lax.optimization_barrier(tuple(array for group in groups for array in group))
    out, at = [], 0
    for group in groups:
        out.append(list(flat[at : at + len(group)]))
        at += len(group)
    return out


def open_jobs(carried, jobs):
    opened = fence(carried, *[list(inputs) for inputs, _ in jobs])
    return opened[0], [(ins, function) for ins, (_, function) in zip(opened[1:], jobs)]


def run_jobs(jobs):
    return [list(function(*inputs)) for inputs, function in jobs]


class Gather:
    def __init__(self, block, far_by=0):
        self.moving = {1: block, -1: block}
        self.cut = block.shape[0] // 2 // 8 * 8
        self.far_by = far_by
        self.fresh = [block]
        self.step = 0
        self.chunks = {}

    def job(self):
        moving, ways = self.moving, [1, -1]
        if self.step + 1 == FAR and self.far_by:
            ways = [self.far_by]
        elif self.step + 1 == FAR:
            moving = {1: moving[1][: self.cut], -1: moving[-1][self.cut :]}

        def function(*arrays):
            moved = [shift(array, by) for array, by in zip(arrays, ways)]
            self.now = [x for block in arrays[len(ways) :] for x in (block, swap(block, "core"))]
            return [*moved, *self.now]

        return [moving[by] for by in ways] + self.fresh, function

    def take(self, results):
        self.step += 1
        if self.step == FAR:
            count = 1 if self.far_by else 2
            last, self.chunks[FAR - 1] = results[:count], list(results[count:])
            last = jnp.concatenate(last, axis=0) if count == 2 else last[0]
            self.chunks[FAR] = [last, swap(last, "core")]
            self.chunks[LAST] = self.chunks[0] + self.chunks[FAR]
            return
        self.moving[1], self.moving[-1], *self.chunks[self.step - 1] = results
        self.fresh = [self.moving[-1], self.moving[1]]


class Scatter:
    def __init__(self, make, inputs=(), ready=False, far_by=0):
        self.make, self.inputs, self.ready, self.far_by = make, list(inputs), ready, far_by
        self.step = 0
        mine, other = make(FAR, *self.inputs)
        first = mine
        if other is not None:
            first = mine.astype(jnp.float32) + swap(other, "core").astype(jnp.float32)
            first = first.astype(jnp.bfloat16)
        self.rows = first.shape[0]
        self.cut = self.rows // 2 // 8 * 8
        self.carried = [first] if far_by else [first[: self.cut], first[self.cut :]]

    def job(self):
        near = FAR - self.step - 1
        count = len(self.carried)
        ways = [self.far_by] if count == 1 else [1, -1]

        def function(*arrays):
            moved = [shift(array, by) for array, by in zip(arrays, ways)]
            mine, other = self.make(near, *arrays[count:])
            self.mine = mine
            terms = [] if self.ready else [mine]
            return moved + terms + ([] if other is None else [swap(other, "core")])

        return self.carried + self.inputs, function

    def take(self, results):
        self.step += 1
        count = len(self.carried)
        moved, terms = list(results[:count]), list(results[count:])
        if self.ready:
            terms = [self.mine] + terms

        def term(i):
            span = slice(i * self.rows, (i + 1) * self.rows)
            return sum(part[span].astype(jnp.float32) for part in terms)

        moved = [array.astype(jnp.float32) for array in moved]
        if self.step == FAR:
            self.last = [*results[:count], *terms]
            self.total = term(0) + moved[0] + moved[1]
            return
        if count == 1:
            moved = [moved[0], 0.0] if self.far_by == 1 else [0.0, moved[0]]
        elif self.step == 1:
            ahead, behind = moved
            ahead = jnp.concatenate([ahead, jnp.zeros_like(behind)], axis=0)
            behind = jnp.concatenate([jnp.zeros_like(ahead[: self.cut]), behind], axis=0)
            moved = [ahead, behind]
        self.carried = [
            (term(0) + moved[0]).astype(jnp.bfloat16),
            (term(1) + moved[1]).astype(jnp.bfloat16),
        ]


def window(items, jobs=(), loose=()):
    every = [item.job() for item in items] + list(jobs) + list(loose)
    _, opened = open_jobs([], every)
    results = run_jobs(opened)
    count = len(items) + len(jobs)
    results = fence(*results[:count]) + results[count:]
    for item, result in zip(items, results):
        item.take(result)
    return results[len(items) :]


def sum_all(values, jobs):
    (values,), jobs = open_jobs([values], jobs)
    core = lax.axis_index("core")
    both = values + swap(values[:, :, ::-1], "core")

    def heard(by):
        pairs = [
            (2 * RING[i] + c, 2 * RING[(i + (by if c == 0 else -by)) % CHIPS] + c)
            for i in range(CHIPS)
            for c in range(2)
        ]
        return lax.ppermute(both, ("chip", "core"), pairs)

    moved = [heard(by) for by in range(1, FAR + 1)]
    done = run_jobs(jobs)
    moved, *done = fence(moved, *done)
    total = jnp.where(core == 0, both, jnp.roll(moved[-1], -FAR, axis=1))
    for by in range(1, FAR):
        total = total + jnp.where(
            core == 0, jnp.roll(moved[by - 1], -by, axis=1), jnp.roll(moved[by - 1], by, axis=1)
        )
    return total + swap(total[:, :, ::-1], "core"), done


def by_place(values, axis):
    return jnp.stack(
        [lax.index_in_dim(values, PLACES.index(at), axis, False) for at in range(CHIPS)], axis
    )


def by_chunk(values, axis):
    return jnp.stack([lax.index_in_dim(values, at, axis, False) for at in PLACES], axis)


def in_hbm(arrays, specs=None):
    return [
        array
        if specs and specs[i].memory_space == pltpu.SMEM
        else pltpu.with_memory_space_constraint(array, pltpu.HBM)
        for i, array in enumerate(arrays)
    ]


def call(
    kernel, name, inputs, ins, outs, shapes, earlier=(), grid=(1,), scratch=(), mib=56, cost=None,
    free=0,
):
    return pl.pallas_call(
        kernel,
        grid=grid,
        in_specs=ins + [pl.BlockSpec(memory_space=pl.ANY)] * len(earlier),
        out_specs=outs,
        out_shape=shapes,
        scratch_shapes=list(scratch),
        input_output_aliases={len(ins) + i: i for i in range(len(earlier))},
        compiler_params=pltpu.CompilerParams(vmem_limit_bytes=mib << 20),
        cost_estimate=BRIEF if cost is None else cost,
        name=name,
    )(*inputs[:free], *in_hbm(inputs[free:], ins[free:]), *in_hbm(earlier))


def whole(array):
    return pl.BlockSpec(array.shape, lambda i: (0,) * len(array.shape))


def once(array):
    return pl.BlockSpec(
        array.shape, lambda i: (0,) * len(array.shape), pipeline_mode=pl.Buffered(1)
    )


def rows_of(step, tok_rows, cols):
    first, count = WIDE_CHUNKS[step] if step == LAST else CHUNKS[step]
    index = first // count
    return pl.BlockSpec((2 * count * tok_rows, cols), lambda i: (index, 0))


def lin_chunk(step, blocks, weight, gain, place, tok_rows, earlier):
    count, width, cols = len(blocks), weight.shape[0], weight.shape[1]
    length = 2 * CHIPS * tok_rows
    rows, head = count * tok_rows, weight.shape[1] // 3

    def kernel(*refs):
        block_refs, weight_ref, gain_ref, place_ref = refs[:count], *refs[count : count + 3]
        lin_ref, all_ref, sum_ref, tag_ref = refs[-4:]
        lanes = pl.ds(pl.multiple_of(place_ref[0] * tok_rows, tok_rows), tok_rows)
        for i in range(count):
            normed, _ = rms_forward(block_refs[i][:tok_rows].astype(jnp.float32), gain_ref[...])
            all_ref[i * tok_rows : (i + 1) * tok_rows] = normed.astype(jnp.bfloat16)
            levels = block_refs[i][tok_rows:, lanes].astype(jnp.float32)
            others = block_refs[i][tok_rows:, : 3 * tok_rows].astype(jnp.float32)
            tag_ref[i * EXTRA : (i + 1) * EXTRA] = jnp.concatenate(
                [levels[:1]]
                + [others[1:2, k * tok_rows : (k + 1) * tok_rows] for k in range(3)]
                + [jnp.zeros((EXTRA - 4, tok_rows), jnp.float32)],
                axis=0,
            )
        lin = product(all_ref[...], weight_ref[...])
        lin_ref[...] = lin
        line = lax.broadcasted_iota(jnp.int32, (8, head), 0)
        total = jnp.zeros((8, rows), jnp.float32)
        for k in range(2):
            part = lin[:, k * head : (k + 1) * head]
            total = total + lax.dot_general(
                (line == k).astype(jnp.float32),
                part * part,
                (((1,), (1,)), ((), ())),
                precision=lax.Precision.HIGHEST,
                preferred_element_type=jnp.float32,
            )
        sum_ref[...] = total

    tags = jax.ShapeDtypeStruct((count * EXTRA, tok_rows), jnp.float32)
    sums = jax.ShapeDtypeStruct((8, rows), jnp.float32)
    return call(
        kernel,
        "lin",
        [*blocks, weight, gain, place],
        [whole(b) for b in blocks]
        + [whole(weight), whole(gain), pl.BlockSpec(memory_space=pltpu.SMEM)],
        [rows_of(step, tok_rows, cols), rows_of(step, tok_rows, width), whole(sums), whole(tags)],
        [
            jax.ShapeDtypeStruct((length, cols), jnp.float32),
            jax.ShapeDtypeStruct((length, width), jnp.bfloat16),
            sums,
            tags,
        ],
        earlier,
        free=count,
        mib=36,
    )


def both_halves(cosine, sine_part):
    return (
        jnp.concatenate([cosine, cosine], axis=-1),
        jnp.concatenate([-sine_part, sine_part], axis=-1),
    )


def rotate_rows(lin, inverse, gains, cosine, sine_part):
    length, cols = lin.shape
    head = cols // 3
    rows = length // 4

    def kernel(lin_ref, inv_ref, gain_ref, cos_ref, sin_ref, q_ref, k_ref, v_ref):
        cos, sin = both_halves(cos_ref[...], sin_ref[...])
        for k, out_ref in enumerate((q_ref, k_ref)):
            part = lin_ref[:, k * head : (k + 1) * head] * inv_ref[:, k : k + 1]
            part = part * gain_ref[k : k + 1]
            turned = pltpu.roll(part, head // 2, 1)
            out_ref[...] = (part * cos + turned * sin).astype(jnp.bfloat16)
        v_ref[...] = lin_ref[:, 2 * head :].astype(jnp.bfloat16)

    row = lambda width: pl.BlockSpec((rows, width), lambda i: (i, 0))
    return call(
        kernel,
        "rotate",
        [lin, inverse, gains, cosine, sine_part],
        [row(cols), row(2), whole(gains), row(head // 2), row(head // 2)],
        [row(head)] * 3,
        [pltpu.HBM((length, head), jnp.bfloat16)] * 3,
        grid=(4,),
        mib=16,
    )


def attend_chunk(step, queries, keys, values, tok_rows, score_scale):
    count = 2 * CHUNKS[step][1]
    head = keys.shape[1]

    def kernel(q_ref, k_ref, v_ref, out_ref, lse_ref, mine_ref, other_ref):
        for i in range(0, count, 2):
            span = pl.ds(i * tok_rows, 2 * tok_rows)
            scores = contract_cols(q_ref[span], k_ref[...]) * score_scale
            row_max = jnp.max(scores, axis=-1, keepdims=True)
            raw = jnp.exp(scores - row_max)
            total = jnp.sum(raw, axis=-1, keepdims=True)
            probs = (raw / total).astype(jnp.bfloat16)
            mixed = product(probs, v_ref[...]).astype(jnp.bfloat16)
            out_ref[span] = mixed
            lse_ref[span] = row_max + jnp.log(total)
            half = pl.ds(i // 2 * tok_rows, tok_rows)
            mine_ref[half] = mixed[:tok_rows]
            other_ref[half] = mixed[tok_rows:]

    rows = count * tok_rows
    shapes = [
        jax.ShapeDtypeStruct((rows, head), jnp.bfloat16),
        jax.ShapeDtypeStruct((rows, 1), jnp.float32),
    ] + [jax.ShapeDtypeStruct((rows // 2, head), jnp.bfloat16)] * 2
    return call(
        kernel,
        "attend",
        [queries, keys, values],
        [rows_of(step, tok_rows, head), whole(keys), whole(values)],
        [whole(shape) for shape in shapes],
        shapes,
        mib=28,
    )


def pair_product(left, right, left_weight, right_weight, transposed, name, step=None):
    multiply = contract_cols if transposed else product
    width = left_weight.shape[0] if transposed else left_weight.shape[1]
    rows, block = left.shape[0], whole(left)
    if step is not None:
        first, count = CHUNKS[step]
        rows, index = rows * count // CHIPS, first // count
        block = pl.BlockSpec((rows, left.shape[1]), lambda i: (index, 0))

    def kernel(left_ref, right_ref, left_weight_ref, right_weight_ref, out_ref):
        total = multiply(left_ref[...], left_weight_ref[...])
        total = total + multiply(right_ref[...], right_weight_ref[...])
        out_ref[...] = total.astype(jnp.bfloat16)

    shape = jax.ShapeDtypeStruct((rows, width), jnp.bfloat16)
    arrays = [left, right, left_weight, right_weight]
    return call(
        kernel,
        name,
        arrays,
        [block, block, whole(left_weight), whole(right_weight)],
        [whole(shape)],
        [shape],
        mib=16,
    )[0]


def attend_back_chunk(
    step, blocks, queries, lse, keys, values, weight, lin, gains, cosine, sine_part, tok_rows,
    score_scale, earlier, final
):
    count = len(blocks)
    length, head = keys.shape
    width = weight.shape[1]
    rows = count * tok_rows

    def unspun(grad, cosine, sine_part, gain):
        cos, sin = both_halves(cosine, sine_part)
        return (grad * cos - pltpu.roll(grad, head // 2, 1) * sin) * gain

    def line_sums(values):
        ones = jnp.ones((8, head), jnp.float32)
        return lax.dot_general(
            ones,
            values,
            (((1,), (1,)), ((), ())),
            precision=lax.Precision.HIGHEST,
            preferred_element_type=jnp.float32,
        )

    def kernel(*refs):
        block_refs = refs[:count]
        q_ref, lse_ref, lin_ref, cos_ref, sin_ref = refs[count : count + 5]
        k_ref, v_ref, w_ref, gain_ref = refs[count + 5 : count + 9]
        rest = refs[count + 9 :]
        if final:
            k_lin_ref, cos_all, sin_all = rest[:3]
            rest = rest[3:]
        if earlier:
            dk, dv = rest[0][...], rest[1][...]
        else:
            dk, dv = 0.0, 0.0
        dq_ref, all_ref, dk_ref, dv_ref, q_sums = rest[-6:-1] if final else rest[-5:]
        for i in range(count):
            all_ref[i * tok_rows : (i + 1) * tok_rows] = block_refs[i][...]
        for i in range(0, count, 2):
            span = pl.ds(i * tok_rows, 2 * tok_rows)
            queries = q_ref[span]
            douts = contract_cols(all_ref[span], w_ref[...]).astype(jnp.bfloat16)
            probs = jnp.exp(contract_cols(queries, k_ref[...]) * score_scale - lse_ref[span])
            dprobs = contract_cols(douts, v_ref[...])
            delta = jnp.sum(probs * dprobs, axis=-1, keepdims=True)
            dscores = (probs * (dprobs - delta)).astype(jnp.bfloat16)
            dq = product(dscores, k_ref[...]) * score_scale
            dq = unspun(dq, cos_ref[span], sin_ref[span], gain_ref[:1])
            dq_ref[span] = dq
            q_sums[:, i * tok_rows : (i + 2) * tok_rows] = line_sums(dq * lin_ref[span])
            dk = dk + contract_rows(dscores, queries) * score_scale
            dv = dv + contract_rows(probs.astype(jnp.bfloat16), douts)
        if final:
            dk = unspun(dk, cos_all[...], sin_all[...], gain_ref[1:])
            rest[-1][...] = line_sums(dk * k_lin_ref[...])
        dk_ref[...] = dk
        dv_ref[...] = dv

    total = jax.ShapeDtypeStruct((length, head), jnp.float32)
    inputs = [*blocks, queries, lse, lin, cosine, sine_part, keys, values, weight, gains]
    ins = [whole(b) for b in blocks] + [
        rows_of(step, tok_rows, head),
        whole(lse),
        rows_of(step, tok_rows, head),
        rows_of(step, tok_rows, head // 2),
        rows_of(step, tok_rows, head // 2),
        whole(keys),
        whole(values),
        whole(weight),
        whole(gains),
    ]
    sums = [jax.ShapeDtypeStruct((8, rows), jnp.float32)]
    if final:
        inputs += [lin, cosine, sine_part]
        ins += [pl.BlockSpec((length, head), lambda i: (0, 1)), whole(cosine), whole(sine_part)]
        sums += [jax.ShapeDtypeStruct((8, length), jnp.float32)]
    so_far = list(earlier[2:4])
    return pl.pallas_call(
        kernel,
        grid=(1,),
        in_specs=ins
        + [whole(part) for part in so_far]
        + [pl.BlockSpec(memory_space=pl.ANY)] * len(earlier[:2]),
        out_specs=[
            rows_of(step, tok_rows, head),
            rows_of(step, tok_rows, width),
            whole(total),
            whole(total),
        ]
        + [whole(part) for part in sums],
        out_shape=[total, jax.ShapeDtypeStruct((length, width), jnp.bfloat16), total, total] + sums,
        input_output_aliases={
            len(ins): 2,
            len(ins) + 1: 3,
            len(ins) + 2: 0,
            len(ins) + 3: 1,
        }
        if earlier
        else {},
        compiler_params=pltpu.CompilerParams(vmem_limit_bytes=42 << 20),
        cost_estimate=BRIEF,
        name="attend_back",
    )(*blocks, *in_hbm(inputs[count:], ins[count:]), *so_far, *in_hbm(earlier[:2]))


def lin_back_rows(dq, dk, dv, lin, inverse, along, tok_rows):
    length, cols = lin.shape
    head = cols // 3
    places = 2
    rows = 2 * places * tok_rows

    def kernel(dq_ref, dk_ref, dv_ref, lin_ref, inv_ref, along_ref, out_ref, mine_ref, other_ref):
        for k, grad_ref in enumerate((dq_ref, dk_ref)):
            span = slice(k * head, (k + 1) * head)
            inv = inv_ref[:, k : k + 1]
            slope = inv * inv * inv * along_ref[:, k : k + 1]
            out_ref[:, span] = (inv * grad_ref[...] - lin_ref[:, span] * slope).astype(jnp.bfloat16)
        out_ref[:, 2 * head :] = dv_ref[...].astype(jnp.bfloat16)
        for i in range(places):
            to, at = slice(i * tok_rows, (i + 1) * tok_rows), 2 * i * tok_rows
            mine_ref[to] = out_ref[at : at + tok_rows]
            other_ref[to] = out_ref[at + tok_rows : at + 2 * tok_rows]

    row = lambda width: pl.BlockSpec((rows, width), lambda i: (i, 0))
    half = jax.ShapeDtypeStruct((length // 2, cols), jnp.bfloat16)
    return call(
        kernel,
        "lin_back",
        [dq, dk, dv, lin, inverse, along],
        [row(head)] * 3 + [row(cols), row(2), row(2)],
        [row(cols)] + [pl.BlockSpec((places * tok_rows, cols), lambda i: (i, 0))] * 2,
        [pltpu.HBM((length, cols), jnp.bfloat16), pltpu.HBM(half.shape, half.dtype), half],
        grid=(CHIPS // places,),
        mib=16,
    )


EXPERT_COLS = 512


def expert_chunk(step, h_blocks, g_blocks, place, kept, router, gate, up, down, tok_rows, earlier):
    count = len(h_blocks)
    width, hidden = gate.shape
    cols = EXPERT_COLS
    rows = count * tok_rows
    length = 2 * CHIPS * tok_rows
    low = jnp.bfloat16
    first, places = WIDE_CHUNKS[step]
    index = first // places
    inner, outer = hidden // cols, width // cols
    long_rows = tok_rows + EXTRA
    per_tile = cols // tok_rows
    apart = places if step == LAST else 1
    together = places // apart

    def kernel(*refs):
        h_refs, g_refs = refs[:count], refs[count : 2 * count]
        place_ref, kept_ref, router_ref = refs[2 * count : 2 * count + 3]
        gate_ref, up_ref, down_ref, gate_rows, up_rows, down_cols = refs[
            2 * count + 3 : 2 * count + 9
        ]
        outs = refs[2 * count + 9 + len(earlier) : -8]
        row_outs, (act_ref, dgate_ref, dup_ref) = outs[:2], outs[2:5]
        mix_refs, dx_refs = outs[5 : 5 + 2 * apart], outs[5 + 2 * apart :]
        h_all, g_all, act_all, dgate_all, dup_all, share_ref, dshare_ref, sems = refs[-8:]
        turn = pl.program_id(0)

        def copies():
            span = pl.ds(index * rows, rows)
            return [
                pltpu.make_async_copy(source, out.at[span], sems.at[i])
                for i, (source, out) in enumerate(zip((h_all, g_all), row_outs))
            ]

        @pl.when(turn == 0)
        def _():
            for i in range(count):
                h_all[i * tok_rows : (i + 1) * tok_rows] = h_refs[i][...]
                g_all[i * tok_rows : (i + 1) * tok_rows] = g_refs[i][...]
            logits = contract_cols(h_all[...], router_ref[...])
            raw = jnp.exp(logits - jnp.max(logits, axis=-1, keepdims=True))
            probs = raw / jnp.sum(raw, axis=-1, keepdims=True)
            lanes = lax.broadcasted_iota(jnp.int32, probs.shape, 1)
            chosen = jnp.sum(
                jnp.where(lanes == place_ref[0], probs, 0.0), axis=-1, keepdims=True
            )
            share_ref[...] = chosen * kept_ref[...]
            dshare_ref[...] = jnp.zeros_like(dshare_ref)

        @pl.when(turn == 1)
        def _():
            for copy in copies():
                copy.start()

        @pl.when(turn < inner)
        def _():
            share = share_ref[...]
            gate_lin = product(h_all[...], gate_ref[...])
            up_lin = product(h_all[...], up_ref[...])
            back = contract_cols(g_all[...], down_ref[...])
            sig = jax.nn.sigmoid(gate_lin)
            silu = gate_lin * sig
            act = silu * up_lin
            dshare_ref[...] += jnp.sum(act * back, axis=-1, keepdims=True)
            act_low = (act * share).astype(low)
            back = back * share
            dgate = (back * up_lin * (sig * (1.0 + gate_lin * (1.0 - sig)))).astype(low)
            dup = (back * silu).astype(low)
            span = pl.ds(pl.multiple_of(turn * cols, cols), cols)
            for ref, everything, value in (
                (act_ref, act_all, act_low),
                (dgate_ref, dgate_all, dgate),
                (dup_ref, dup_all, dup),
            ):
                ref[...] = value
                everything[:, span] = value

        @pl.when(turn >= inner)
        def _():
            mix = product(act_all[...], down_cols[...]).astype(low)
            dx = contract_cols(dgate_all[...], gate_rows[...])
            dx = (dx + contract_cols(dup_all[...], up_rows[...])).astype(low)
            for i in range(count):
                span = slice(i * tok_rows, (i + 1) * tok_rows)
                to, at = i % 2 + i // 2 // together * 2, i // 2 % together
                mix_refs[to][at * tok_rows : (at + 1) * tok_rows] = mix[span]
                dx_refs[to][at * long_rows : at * long_rows + tok_rows] = dx[span]

            total = dshare_ref[...] * kept_ref[...]
            same = lax.broadcasted_iota(jnp.int32, (tok_rows, tok_rows), 0) == (
                lax.broadcasted_iota(jnp.int32, (tok_rows, tok_rows), 1)
            )
            tile_lanes = lax.broadcasted_iota(jnp.int32, (EXTRA, cols), 1) // tok_rows
            here = tile_lanes + (turn - inner) * per_tile == place_ref[0]
            for i in range(count):
                rest = jnp.sum(
                    jnp.where(same, total[i * tok_rows : (i + 1) * tok_rows], 0.0),
                    axis=0,
                    keepdims=True,
                )
                pieces = []
                for _ in range(3):
                    piece = rest.astype(low).astype(jnp.float32)
                    rest = rest - piece
                    pieces.append(piece)
                pieces.append(jnp.zeros((EXTRA - 3, tok_rows), jnp.float32))
                line = jnp.concatenate(pieces, axis=0)
                line = jnp.concatenate([line] * per_tile, axis=1)
                to, at = i % 2 + i // 2 // together * 2, i // 2 % together
                at = at * long_rows + tok_rows
                dx_refs[to][at : at + EXTRA] = jnp.where(here, line, 0.0).astype(low)

        @pl.when(turn == inner + outer - 1)
        def _():
            for copy in copies():
                copy.wait()

    def inner_at(t):
        return jnp.minimum(t, inner - 1)

    def outer_at(t):
        return jnp.maximum(t - inner, 0)

    tile = pl.BlockSpec((rows, cols), lambda t: (index, inner_at(t)))
    wide = jax.ShapeDtypeStruct((length, hidden), low)
    full = jax.ShapeDtypeStruct((length, width), low)
    half = jax.ShapeDtypeStruct((together * tok_rows, width), low)
    longer = jax.ShapeDtypeStruct((together * long_rows, width), low)
    anywhere = pl.BlockSpec(memory_space=pl.ANY)
    out_tile = lambda shape: pl.BlockSpec((shape.shape[0], cols), lambda t: (0, outer_at(t)))
    return call(
        kernel,
        "expert",
        [*h_blocks, *g_blocks, place, kept, router, gate, up, down, gate, up, down],
        [once(b) for b in [*h_blocks, *g_blocks]]
        + [
            pl.BlockSpec(memory_space=pltpu.SMEM),
            pl.BlockSpec((rows, 1), lambda t: (index, 0)),
            whole(router),
            pl.BlockSpec((width, cols), lambda t: (0, inner_at(t))),
            pl.BlockSpec((width, cols), lambda t: (0, inner_at(t))),
            pl.BlockSpec((cols, width), lambda t: (inner_at(t), 0)),
            pl.BlockSpec((cols, hidden), lambda t: (outer_at(t), 0)),
            pl.BlockSpec((cols, hidden), lambda t: (outer_at(t), 0)),
            pl.BlockSpec((hidden, cols), lambda t: (0, outer_at(t))),
        ],
        [anywhere] * 2
        + [tile] * 3
        + [out_tile(half)] * (2 * apart)
        + [out_tile(longer)] * (2 * apart),
        [full] * 2 + [wide] * 3 + [half] * (2 * apart) + [longer] * (2 * apart),
        earlier,
        grid=(inner + outer,),
        scratch=[pltpu.VMEM((rows, width), low)] * 2
        + [pltpu.VMEM((rows, hidden), low)] * 3
        + [pltpu.VMEM((rows, 1), jnp.float32)] * 2
        + [pltpu.SemaphoreType.DMA((2,))],
        mib=46,
        free=2 * count,
    )


def input_grad_rows(parts, tokens, inverse, gain, grads):
    def kernel(ahead_ref, behind_ref, mine_ref, tokens_ref, inv_ref, gain_ref, grads_ref, out_ref):
        upstream = mine_ref[...].astype(jnp.float32) + ahead_ref[...].astype(jnp.float32)
        upstream = upstream + behind_ref[...].astype(jnp.float32)
        rows = tokens_ref[...].astype(jnp.float32)
        inv = inv_ref[...]
        scaled = upstream * gain_ref[...]
        along = jnp.mean(scaled * rows, axis=-1, keepdims=True)
        norm = inv * scaled - rows * inv * inv * inv * along
        out_ref[...] = (grads_ref[...] + norm).astype(jnp.bfloat16)

    arrays = [*parts, tokens, inverse, gain, grads]
    shape = jax.ShapeDtypeStruct(tokens.shape, jnp.bfloat16)
    return call(
        kernel,
        "input_grad",
        arrays,
        [whole(a) for a in arrays],
        [whole(shape)],
        [shape],
        mib=24,
        free=len(arrays),
    )[0]


THIN = 128
HALF_THIN = THIN // 2


def split_parts(values):
    high = values.astype(jnp.bfloat16).astype(jnp.float32)
    return high, values - high


def dense_chunk(rows_h, grads, weight, columns, narrow, part, own_rows):
    length, width = rows_h.shape
    cols = grads.shape[1]
    block = 256
    runs = block // (2 * own_rows)
    wide = narrow is not None
    first_col, count_col = columns

    def kernel(part_ref, h_ref, grads_ref, weight_ref, *refs):
        kept_ref, sent_ref = refs[-2:] if wide else refs[-3:-1]
        grads = contract_rows(h_ref[...], grads_ref[...].astype(jnp.bfloat16))
        weight = weight_ref[...].astype(jnp.float32)[:, first_col : first_col + count_col]
        term = jnp.sum(grads * weight, axis=-1, keepdims=True)
        both = plain = grads
        if wide:
            narrow = refs[0][...]
            lanes = lax.broadcasted_iota(jnp.int32, narrow.shape, 1)
            narrow = jnp.where(lanes == 17, refs[1][...] + term, narrow)
            high, rest = split_parts(narrow)
            both = jnp.concatenate([both, high, rest], axis=-1)
            plain = jnp.concatenate([plain, narrow, jnp.zeros_like(narrow)], axis=-1)
        else:
            refs[-1][...] = term
        second = part_ref[0] == 1
        for i in range(runs):
            at = 2 * i * own_rows
            first = slice(at, at + own_rows)
            other = slice(at + own_rows, at + 2 * own_rows)
            to = slice(i * own_rows, (i + 1) * own_rows)
            kept_ref[to] = jnp.where(second, plain[other], plain[first])
            sent_ref[to] = jnp.where(second, both[first], both[other]).astype(jnp.bfloat16)

    full = cols + (THIN if wide else 0)
    out = lambda kind: jax.ShapeDtypeStruct((width // 2, full), kind)
    row = lambda size: pl.BlockSpec((block // 2, size), lambda i: (i, 0))
    here = lambda size: pl.BlockSpec((block, size), lambda i: (i, 0))
    return call(
        kernel,
        "dense",
        [part, rows_h, grads, weight] + (list(narrow) if wide else []),
        [
            pl.BlockSpec(memory_space=pltpu.SMEM),
            pl.BlockSpec((length, block), lambda i: (0, i)),
            whole(grads),
            here(weight.shape[1]),
        ]
        + ([here(HALF_THIN), here(1)] if wide else []),
        [row(full), row(full)] + ([] if wide else [here(1)]),
        [out(jnp.float32), out(jnp.bfloat16)]
        + ([] if wide else [jax.ShapeDtypeStruct((width, 1), jnp.float32)]),
        grid=(width // block,),
        mib=24,
        cost=pl.CostEstimate(
            flops=2 * length * width * cols,
            bytes_accessed=2 * length * width + 6 * width * full,
            transcendentals=0,
        ),
    )


def dense_sum(kept, got):
    rows, full = kept.shape
    cols = full - THIN
    block = rows // 4

    def kernel(kept_ref, got_ref, out_ref):
        got = got_ref[...].astype(jnp.float32)
        out_ref[:, :cols] = (kept_ref[:, :cols] + got[:, :cols]).astype(jnp.bfloat16)
        narrow = kept_ref[:, cols : cols + HALF_THIN]
        narrow = narrow + got[:, cols : cols + HALF_THIN] + got[:, cols + HALF_THIN :]
        out_ref[:, cols:] = jnp.concatenate(split_parts(narrow), axis=-1).astype(jnp.bfloat16)

    row = pl.BlockSpec((block, full), lambda i: (i, 0))
    return call(
        kernel,
        "dense_sum",
        [kept, got],
        [row, row],
        [row],
        [jax.ShapeDtypeStruct((rows, full), jnp.bfloat16)],
        grid=(4,),
        mib=16,
    )[0]


def body(
    tokens,
    cotangent,
    attn_gain,
    w_query,
    w_key,
    w_value,
    w_out,
    query_gain,
    key_gain,
    ffn_gain,
    router,
    w_gate,
    w_up,
    w_down,
    routes,
    priority,
    positions,
):
    low = jnp.bfloat16
    ctx_count = 2 * CHIPS
    place = lax.axis_index("chip") * 2 + lax.axis_index("core")
    part = lax.axis_index("fsdp")
    tok_rows, model_width = tokens.shape[1:]
    half_width = model_width // 2
    head_dim = HEAD_DIM
    length = tok_rows * ctx_count
    capacity = 9 * tok_rows
    score_scale = head_dim ** (-0.5)
    per_half = ctx_count // 2
    expert_count = router.shape[1]

    def joined(mine, other, axis):
        return jnp.where(
            part == 0,
            jnp.concatenate([mine, other], axis=axis),
            jnp.concatenate([other, mine], axis=axis),
        )

    def head_rows(matrix, width):
        return lax.dynamic_slice_in_dim(matrix, (place % per_half) * width, width, 0)

    small = jnp.concatenate(
        [
            router.T,
            attn_gain[None],
            ffn_gain[None],
            jnp.concatenate(
                [
                    head_rows(query_gain, head_dim),
                    head_rows(key_gain, head_dim),
                    jnp.zeros((half_width - 2 * head_dim,), low),
                ]
            )[None],
        ],
        axis=0,
    )
    qkv_mine = jnp.concatenate(
        [
            lax.dynamic_slice_in_dim(w, place * head_dim, head_dim, 1)
            for w in (w_query, w_key, w_value)
        ],
        axis=1,
    )
    out_mine = head_rows(w_out, head_dim)

    hot = routes[0][:, :, None] == jnp.arange(expert_count, dtype=jnp.int32)[None, None, :]
    levels = jnp.sum(jnp.where(hot, priority[0][:, :, None] - LEVELS, 0), axis=1) + LEVELS
    spot = positions[0]
    line = jnp.concatenate(
        [spot // 128, spot % 128, jnp.full((model_width - 2 * tok_rows,), place, jnp.int32)]
    )
    tags = jnp.concatenate(
        [
            levels.T.reshape(1, model_width),
            line[None],
            jnp.zeros((EXTRA - 2, model_width), jnp.int32),
        ],
        axis=0,
    ).astype(low)

    inputs = tokens[0].astype(jnp.float32)
    inv_one = lax.rsqrt(jnp.mean(inputs * inputs, axis=-1, keepdims=True) + epsilon)
    first_rows = jnp.concatenate([tokens[0], tags], axis=0)
    place_one = place.astype(jnp.int32).reshape(1)
    ready = ()
    sum_parts, tag_parts = {}, {}

    def lin_job(step, blocks):
        def function():
            made = lin_chunk(
                step, blocks(), qkv_weight, g_attn[None], place_one, tok_rows, ready
            )
            return made

        return [], function

    def lin_keep(step, made):
        nonlocal ready
        ready = tuple(made[:2])
        sum_parts[step], tag_parts[step] = made[2][:2], made[3]

    def other_core(array):
        return (swap(array, "core"),)

    rows_one = Gather(first_rows)

    def to_other(*arrays):
        return [swap(array, "fsdp") for array in arrays]

    (small_other,), (qkv_other,) = window(
        [rows_one], [([small], to_other)], loose=[([qkv_mine], to_other)]
    )
    small_full = joined(small, small_other, 1)
    r_weight = small_full[:expert_count]
    g_attn = small_full[expert_count].astype(jnp.float32)
    g_ffn = small_full[expert_count + 1].astype(jnp.float32)
    here = part == place // per_half
    g_heads = jnp.where(here, small[expert_count + 2], small_other[expert_count + 2]).astype(
        jnp.float32
    )
    g_query, g_key = g_heads[:head_dim], g_heads[head_dim : 2 * head_dim]
    qkv_weight = joined(qkv_mine, qkv_other, 0)

    def expert_weights(_, *own):
        return [lax.all_gather(w, "fsdp", axis=k, tiled=True) for w, k in zip(own, (0, 0, 1))]

    made, expert_own = window(
        [rows_one],
        [lin_job(1, lambda: rows_one.now)],
        loose=[([qkv_other, w_gate[0], w_up[0], w_down[0]], expert_weights)],
    )
    gate_weight, up_weight, down_weight = expert_own
    lin_keep(1, made)
    made, (qkv_pair,) = window(
        [rows_one],
        [lin_job(2, lambda: rows_one.now), ([qkv_weight], other_core)],
    )
    lin_keep(2, made)
    made, (out_other,) = window(
        [rows_one], [lin_job(3, lambda: rows_one.now)], loose=[([out_mine], to_other)]
    )
    out_weight = jnp.where(here, out_mine, out_other)
    lin_keep(3, made)
    lin_keep(LAST, lin_job(LAST, lambda: rows_one.chunks[LAST])[1]())
    lin, all_h_one = ready
    all_tags = jnp.concatenate([tag_parts[step] for step in WIDE_CHUNKS], axis=0).reshape(
        ctx_count, EXTRA, tok_rows
    )

    def token_sums(lines, jobs):
        total, done = sum_all(by_place(lines.reshape(-1, CHIPS, 2, tok_rows), 1), jobs)
        return by_chunk(total, 1).reshape(-1, length).T / model_width, done

    def rank_job(all_tags):
        mine, owner = all_tags[:, 0], all_tags[:, 3, :1]
        order = owner * tok_rows + jnp.arange(tok_rows, dtype=jnp.float32)[None]
        mine = mine.reshape(length)
        code = mine * length + order.reshape(length)
        ranks = jnp.sum((code[None, :] < code[:, None]).astype(jnp.float32), axis=1)
        kept = (mine < LEVELS) & (ranks < capacity)
        return (kept.astype(jnp.float32)[:, None],)

    def rope_job(all_tags):
        spots = (all_tags[:, 1] * 128.0 + all_tags[:, 2]).reshape(-1)
        return [table[:, 0] for table in rope_tables(spots, head_dim)]

    square, ((cosine, sine_part),) = token_sums(
        jnp.concatenate([sum_parts[step] for step in WIDE_CHUNKS], axis=1),
        [([all_tags], rope_job)],
    )
    grads_rows = Gather(cotangent[0], -1)
    grads_inputs, grads_step = grads_rows.job()
    (square,), grads_inputs = fence([square], grads_inputs)
    grads_moved = grads_step(*grads_inputs)
    inverse = lax.rsqrt(square + epsilon)
    gains = jnp.stack([g_query, g_key], axis=0)
    q_rot, k_rot, v_low = rotate_rows(lin, inverse, gains, cosine, sine_part)

    heads = {}

    def attend_job(step):
        return [q_rot, k_rot, v_low], lambda queries, keys, values: attend_chunk(
            step, queries, keys, values, tok_rows, score_scale
        )

    def projected(step, made):
        return pair_product(
            made[2], swap(made[3], "core"), out_weight, out_pair, False, "project"
        )

    def first_job(queries, keys, values):
        made = attend_job(FAR)[1](queries, keys, values)
        return [*made, projected(FAR, made)]

    (out_pair,) = other_core(out_weight)
    (*heads[FAR], far_terms), heads[FAR - 1], grads_moved = window(
        [],
        [
            ([q_rot, k_rot, v_low], first_job),
            attend_job(FAR - 1),
            ([], lambda: grads_moved),
        ],
    )
    grads_rows.take(grads_moved)

    def out_terms(step, *parts):
        return (far_terms if step == FAR else projected(step, parts)), None

    out_sum = Scatter(out_terms)
    for near in range(FAR - 1, -1, -1):
        out_sum.inputs = heads[near]
        jobs = [attend_job(near - 1)] if near else []
        held = [([gate_weight], lambda weight: (weight,)), ([all_tags], rank_job)]
        made = window([out_sum], jobs + (held if near == 2 else []))
        if near == 2:
            (gate_weight,), (kept,) = made[-2:]
        if near:
            heads[near - 1] = made[0]
    mixed_low = jnp.concatenate([heads[step][0] for step in CHUNKS], axis=0)
    middle = inputs + out_sum.total

    h_two_f, inv_two = rms_forward(middle, g_ffn)
    h_two = h_two_f.astype(low)
    grad_out = cotangent[0].astype(jnp.float32)
    filled = ()
    mix_terms, dx_terms = {}, {}

    rows_two = Gather(h_two, 1)
    window([rows_two])

    def expert_job(step, h_blocks, g_blocks):
        return [], lambda: expert_chunk(
            step,
            h_blocks(),
            g_blocks(),
            place_one,
            kept,
            r_weight,
            gate_weight,
            up_weight,
            down_weight,
            tok_rows,
            filled,
        )

    for step in list(range(1, FAR)) + [LAST]:
        if step == LAST:
            run = expert_job(step, lambda: rows_two.chunks[LAST], lambda: grads_rows.chunks[LAST])
            made = run[1]()
        else:
            run = expert_job(step, lambda: rows_two.now, lambda: grads_rows.now)
            (made,) = window([rows_two, grads_rows], [run])
        filled, terms = tuple(made[:5]), made[5:]
        if step == LAST:
            mix_terms[0], mix_terms[FAR] = terms[:2], terms[2:4]
            dx_terms[0], dx_terms[FAR] = terms[4:6], terms[6:]
        else:
            mix_terms[step], dx_terms[step] = terms[:2], terms[2:]
    all_h_two, all_grads, act_low, gate_grad, up_grad = filled

    def wgrad(left, right):
        return (contract_rows(left, right).astype(low),)

    def over_sequences(matrix, axis):
        return lax.psum_scatter(matrix, "fsdp", scatter_dimension=axis, tiled=True)

    logits = contract_cols(h_two, r_weight)
    row_max = jnp.max(logits, axis=-1, keepdims=True)
    exps_raw = jnp.exp(logits - row_max)
    router_probs = exps_raw / jnp.sum(exps_raw, axis=-1, keepdims=True)
    dx_sum = Scatter(lambda step: dx_terms[step], ready=True, far_by=1)
    mix_sum = Scatter(lambda step: mix_terms[step], ready=True, far_by=-1)
    ((gate_wgrad,),) = window([dx_sum, mix_sum], [([all_h_two, gate_grad], wgrad)])
    s_gate = over_sequences(gate_wgrad, 0)
    ((up_wgrad,),) = window([dx_sum], [([all_h_two, up_grad], wgrad)])
    s_up = over_sequences(up_wgrad, 0)
    ((down_wgrad,),) = window([dx_sum], [([act_low, all_grads], wgrad)])
    s_down = over_sequences(down_wgrad, 1)
    window([dx_sum])
    hidden_sum = dx_sum.total

    prob_grad = jnp.sum(hidden_sum[tok_rows : tok_rows + 3], axis=0)
    prob_grad = prob_grad.reshape(expert_count, tok_rows).T
    logit_grad = router_probs * (
        prob_grad - jnp.sum(router_probs * prob_grad, axis=-1, keepdims=True)
    )
    hidden_grad = hidden_sum[:tok_rows] + precise(logit_grad, r_weight.astype(jnp.float32))
    norm_grad, ffn_gain_grad = rms_backward(middle, inv_two, g_ffn, hidden_grad)
    middle_grad = grad_out + norm_grad

    sofar = ()

    q_sums = {}
    rows_da = Gather(middle_grad.astype(low))

    def back_job(step, blocks):
        return [], lambda: attend_back_chunk(
            step,
            blocks(),
            q_rot,
            heads[step][1],
            k_rot,
            v_low,
            out_weight,
            lin,
            gains,
            cosine,
            sine_part,
            tok_rows,
            score_scale,
            sofar,
            step == FAR,
        )

    def widen(array):
        return (array.astype(jnp.float32),)

    def narrow_job(h_two, logit_grad, ffn_gain_grad):
        return (
            jnp.concatenate(
                [
                    precise(h_two.astype(jnp.float32).T, logit_grad),
                    ffn_gain_grad[:, None],
                    jnp.zeros((model_width, HALF_THIN - expert_count - 1), jnp.float32),
                ],
                axis=1,
            ),
        )

    besides = {0: [], 1: [mix_sum], 2: [], 3: [mix_sum]}
    also = {0: [([s_gate], widen)], 1: [([h_two, logit_grad, ffn_gain_grad], narrow_job)]}
    for step in range(FAR + 1):
        if step == FAR:
            *made, k_sums = back_job(step, lambda: rows_da.chunks[FAR])[1]()
        else:
            made, *wide = window(
                [rows_da] + besides[step], [back_job(step, lambda: rows_da.now)] + also.get(step, [])
            )
            if step == 0:
                ((s_gate,),) = wide
            if step == 1:
                ((narrow,),) = wide
        sofar, q_sums[step] = tuple(made[:4]), made[4]
    dq, all_branch, dk, dv = sofar

    def out_job(mixed_low, all_branch):
        return (contract_rows(mixed_low, all_branch),)

    own_rows = model_width // (2 * ctx_count)
    part_one = part.astype(jnp.int32).reshape(1)

    def value_job(all_h_one, dv):
        return dense_chunk(
            all_h_one, dv, qkv_weight, (2 * head_dim, head_dim), None,
            part_one, own_rows,
        )

    along, ((v_kept, v_sent, v_term),) = token_sums(
        jnp.stack(
            [jnp.concatenate([q_sums[step][0] for step in CHUNKS], axis=0), k_sums[0]], axis=0
        ),
        [
            ([all_h_one, dv], value_job),
        ],
    )
    mix_inputs, mix_step = mix_sum.job()
    (along,), mix_inputs = fence([along], mix_inputs)
    mix_moved = mix_step(*mix_inputs)
    lin_grad, lin_mine, lin_theirs = lin_back_rows(dq, dk, dv, lin, inverse, along, tok_rows)
    lin_theirs = swap(lin_theirs, "core")


    def pick(blocks, index):
        return lax.dynamic_index_in_dim(blocks, index, 1, False)

    def dense_job(all_h_one, lin_grad, *narrow):
        return dense_chunk(
            all_h_one, lin_grad[:, : 2 * head_dim], qkv_weight, (0, 2 * head_dim), narrow,
            part_one, own_rows,
        )

    def out_swap_job(out_sent, dq, dk, lin):
        gain_rows = jnp.stack(
            [
                jnp.sum(
                    grad * lin[:, k * head_dim : (k + 1) * head_dim] * inverse[:, k : k + 1], axis=0
                )
                for k, grad in enumerate((dq, dk))
            ],
            axis=0,
        )
        gain_rows = (gain_rows / gains).reshape(2, 2, own_rows)
        return swap(out_sent, "fsdp"), swap(pick(gain_rows, 1 - part), "fsdp"), pick(gain_rows, part)

    def h_terms(step, lin_mine, lin_theirs):
        return (
            pair_product(lin_mine, lin_theirs, qkv_weight, qkv_pair, True, "h_terms", step),
            None,
        )

    h_sum = Scatter(h_terms, [lin_mine, lin_theirs])
    def swap_job(sent):
        return (swap(sent, "fsdp"),)

    def owners_job(payload):
        blocks = payload.reshape(ctx_count, own_rows, -1)
        return (lax.all_to_all(blocks, ("chip", "core"), 0, 0, tiled=True),)

    (kept, sent), mix_moved, (s_up,), (v_got,) = window(
        [h_sum],
        [
            ([all_h_one, lin_grad, narrow, v_term], dense_job),
            ([], lambda: mix_moved),
            ([s_up], widen),
        ],
        loose=[([v_sent], swap_job)],
    )
    mix_sum.take(mix_moved)
    layer_out = (middle + mix_sum.total).astype(low)
    (got,), (out_wgrad,), (v_received,) = window(
        [h_sum],
        [([sent], swap_job), ([mixed_low, all_branch], out_job)],
        loose=[([(v_kept + v_got.astype(jnp.float32)).astype(low)], owners_job)],
    )
    out_rows = out_wgrad.reshape(1, 2, own_rows, model_width)
    (received,), (out_got, gain_got, gain_kept) = window(
        [h_sum],
        loose=[
            ([kept, got], lambda kept, got: owners_job(dense_sum(kept, got))),
            ([pick(out_rows, 1 - part)[0].astype(low), dq, dk, lin], out_swap_job),
        ],
    )

    (v_received,), (received,), (out_got, gain_got), (s_down,) = window(
        [h_sum],
        [
            ([], lambda: (v_received,)),
            ([], lambda: (received,)),
            ([], lambda: (out_got, gain_got)),
            ([s_down], widen),
        ],
    )
    d_out = pick(out_rows, part)[0] + out_got.astype(jnp.float32)
    gain_sum = gain_kept + gain_got
    d_qgain, d_kgain = gain_sum[0], gain_sum[1]
    s_gate, s_up, s_down = s_gate[None], s_up[None], s_down[None]
    input_grad = input_grad_rows(h_sum.last, tokens[0], inv_one, g_attn[None], middle_grad)
    d_query, d_key, d_value = (
        columns.transpose(1, 0, 2).reshape(own_rows, model_width).astype(jnp.float32)
        for columns in (received[:, :, :head_dim], received[:, :, head_dim : 2 * head_dim], v_received)
    )
    thin_sum = jnp.sum(received[:, :, 2 * head_dim :].astype(jnp.float32), axis=0)
    thin_sum = thin_sum[:, :HALF_THIN] + thin_sum[:, HALF_THIN:]
    d_router = thin_sum[:, :expert_count]
    own_gain = lax.dynamic_slice_in_dim(g_attn, (2 * place + part) * own_rows, own_rows, 0)
    d_ffn, d_attn = thin_sum[:, expert_count], thin_sum[:, expert_count + 1] / own_gain
    return (
        layer_out[None],
        input_grad[None],
        d_attn,
        d_query,
        d_key,
        d_value,
        d_out,
        d_qgain,
        d_kgain,
        d_ffn,
        d_router,
        s_gate,
        s_up,
        s_down,
    )


def specs_of(ctx):
    rows, both = P("fsdp", ctx, None), ctx + ("fsdp",)
    dense = P("fsdp", None)
    ins = (
        rows,
        rows,
        P("fsdp"),
        dense,
        dense,
        dense,
        dense,
        P("fsdp"),
        P("fsdp"),
        P("fsdp"),
        dense,
        P(ctx, "fsdp", None),
        P(ctx, "fsdp", None),
        P(ctx, None, "fsdp"),
        rows,
        rows,
        P("fsdp", ctx),
    )
    line, matrix = P(both), P(both, None)
    outs = (
        rows,
        rows,
        line,
        matrix,
        matrix,
        matrix,
        matrix,
        line,
        line,
        line,
        matrix,
        P(ctx, "fsdp", None),
        P(ctx, "fsdp", None),
        P(ctx, None, "fsdp"),
    )
    return ins, outs


def solution(mesh):
    ctx_count, fsdp_count = mesh.shape["ctx"], mesh.shape["fsdp"]

    def whole(*arrays):
        heads = arrays[0].shape[2] // HEAD_DIM
        experts = arrays[10].shape[1]
        if ctx_count == 2 * CHIPS == heads == experts and fsdp_count == 2:
            chips = Mesh(mesh.devices.reshape(-1, 2, 2), ("chip", "core", "fsdp"))
            run, grid, ctx = body, chips, ("chip", "core")
        else:
            run, grid, ctx = general_body, mesh, ("ctx",)
        ins, outs = specs_of(ctx)
        return jax.shard_map(run, mesh=grid, in_specs=ins, out_specs=outs, check_vma=False)(*arrays)

    return whole
```
